512 devices in a mesh: seq: 64 (over x, z_lo, core), head: 4 (over y), rep: 2 (over z_hi).
Axes of the slice: x: 4, y: 4, z: 16 (z_hi: 2, z_lo: 8; z = z_hi * 8 + z_lo), core: 2. Of those that a mesh axis runs over, the one named last changes fastest.
Arguments:
- token_ids: int32 [32768], P(('rep', 'seq')), parts along dimension 0, may hold values from 0 to 15
- embedding: float32 [16, 256], replicated, may hold values from -6 to 6
- complement: int32 [256], replicated, may hold values from 0 to 255, each once
- prenorm_first: float32 [256], replicated, may hold values from 0.1 to 1.9
- inproj_first: float32 [256, 2, 512], P(None, None, 'head'), may hold values from -0.375 to 0.375
- statemap_first: float32 [256, 2, 128], replicated, may hold values from -0.375 to 0.375
- stepmap_first: float32 [256, 8], P(None, 'head'), may hold values from -0.375 to 0.375
- stepbias_first: float32 [8], P('head'), may hold values from -1 to 1
- rates_first: float32 [8], P('head'), may hold values from 1.15966797e-05 to 0.11, as said below
- skipgain_first: float32 [8], P('head'), may hold values from 0.5 to 1.5
- outnorm_first: float32 [512], P('head'), may hold values from 0.1 to 1.9
- outproj_first: float32 [512, 256], P('head'), may hold values from -0.25 to 0.25
- prenorm_second: float32 [256], replicated, may hold values from 0.1 to 1.9
- inproj_second: float32 [256, 2, 512], P(None, None, 'head'), may hold values from -0.375 to 0.375
- statemap_second: float32 [256, 2, 128], replicated, may hold values from -0.375 to 0.375
- stepmap_second: float32 [256, 8], P(None, 'head'), may hold values from -0.375 to 0.375
- stepbias_second: float32 [8], P('head'), may hold values from -1 to 1
- rates_second: float32 [8], P('head'), may hold values from 1.15966797e-05 to 0.11, as said below
- skipgain_second: float32 [8], P('head'), may hold values from 0.5 to 1.5
- outnorm_second: float32 [512], P('head'), may hold values from 0.1 to 1.9
- outproj_second: float32 [512, 256], P('head'), may hold values from -0.25 to 0.25
Outputs:
- strand_out: float32 [32768, 256], P(('rep', 'seq', 'head')), parts along dimension 0
The draws below stay inside these ranges and needn't reach their ends.
There are 2 independent parts, one for each index of `rep`. The reference program is written for one: setup_inputs(seed, part) draws one part's arguments, and reference() takes and returns one part's arrays. A program takes and returns all parts, laid end to end along the dimension named above; an argument that names none is the same for every part. Nothing has to cross between parts.
Inputs may be any that keep to these rules, and one draw needn't show every extreme that they name: `complement`: each channel index appears once. `rates_first`: positive rates. `rates_second`: positive rates.
All inputs are finite; a program needn't handle non-finite values.
Results may differ from the reference program's by a relative error of at most 0.00018.
Values sent between devices are 32-bit elements; how exact they have to be, the bound alone decides.
A program may use at most 64 MiB of HBM per device.

```python
import jax
import jax.numpy as jnp
from jax import lax

D = 256
HEADS = 8
STATE = 128
VOCAB = 16
BLOCK = 256
INNER = 512
SEQ_LEN = 16384


def rate_values(key, salt_value):
    mixed_key = jax.random.fold_in(key, salt_value)
    first_key, second_key, third_key = jax.random.split(mixed_key, 3)
    slow_log = jax.random.uniform(first_key, (HEADS,), jnp.float32, jnp.log(0.2 / SEQ_LEN), jnp.log(1.0 / SEQ_LEN))
    fast_log = jax.random.uniform(second_key, (HEADS,), jnp.float32, jnp.log(0.03), jnp.log(0.1))
    slow_count = HEADS // 2
    ranking = jax.random.permutation(third_key, HEADS)
    return jnp.exp(jnp.where(ranking < slow_count, slow_log, fast_log)).astype(jnp.float32)


def draw_rates_first(key, part):
    return rate_values(key, 11)


def draw_rates_second(key, part):
    return rate_values(key, 23)


def plant(result, stream_key, least, high):
    longest = result.shape.index(max(result.shape))
    spots = []
    for shift in (0, 1):
        where = [jax.random.randint(jax.random.fold_in(stream_key, axis), (), 0, length) for axis, length in enumerate(result.shape)]
        where[longest] = (where[longest] + shift) % result.shape[longest]
        spots.append(tuple(where))
    return result.at[spots[0]].set(least).at[spots[1]].set(high)


def block_levels(key, shape, cuts, low, top_value):
    def one(axis_at, parts):
        heights = jax.random.uniform(jax.random.fold_in(jax.random.fold_in(key, 6), axis_at), (parts,), jnp.float32, low / len(cuts), top_value / len(cuts))
        return jnp.repeat(jnp.exp(heights), shape[axis_at] // parts).reshape((-1,) + (1,) * (len(shape) - axis_at - 1))

    loudness = one(*cuts[0])
    for cut in cuts[1:]:
        loudness = loudness * one(*cut)
    return loudness


def bell_draw(stream_key, shape, deviation, bound, pieces=(), dtype=jnp.bfloat16):
    gain = block_levels(stream_key, shape, pieces, -0.22, 0.18) if pieces else 1.0
    array = jax.random.normal(stream_key, shape, jnp.float32) * deviation * gain
    return jnp.minimum(jnp.maximum(array, -bound), bound).astype(dtype)


def setup_inputs(seed: int = 0, part: int = 0) -> dict:
    key_of = jax.random.split(jax.random.key(seed), 22)
    part_splits = jax.random.split(jax.random.fold_in(key_of[21], part), 22)
    token_ids = plant(jax.random.randint(part_splits[0], (SEQ_LEN,), 0, VOCAB), jax.random.fold_in(part_splits[0], 1), 0, VOCAB - 1).astype(jnp.int32)
    embedding = bell_draw(key_of[1], (VOCAB, D), 1.0, 6.0, (), jnp.float32)
    complement = jax.random.permutation(key_of[2], D).astype(jnp.int32)
    prenorm_first = jnp.clip(1.0 + 0.18 * jax.random.normal(key_of[3], (D,), jnp.float32), 0.1, 1.9)
    inproj_first = bell_draw(key_of[4], (D, 2, INNER), D ** -0.5, 0.375, ((2, 4),), jnp.float32)
    statemap_first = bell_draw(key_of[5], (D, 2, STATE), D ** -0.5, 0.375, (), jnp.float32)
    stepmap_first = bell_draw(key_of[6], (D, HEADS), D ** -0.5, 0.375, ((1, 4),), jnp.float32)
    stepbias_first = jnp.clip(jax.random.uniform(key_of[7], (HEADS,), jnp.float32, -1.0, 1.0) * block_levels(key_of[7], (HEADS,), ((0, 4),), -0.4, 0.0), -1.0, 1.0)
    rates_first = draw_rates_first(jax.random.fold_in(key_of[21], 71), part)
    skipgain_first = jnp.clip(0.5 + 1.0 * jax.random.uniform(key_of[9], (HEADS,), jnp.float32) ** block_levels(key_of[9], (HEADS,), ((0, 4),), -0.2, 0.2), 0.5, 1.5)
    outnorm_first = jnp.clip(1.0 + 0.18 * jax.random.normal(key_of[10], (INNER,), jnp.float32), 0.1, 1.9)
    outproj_first = bell_draw(key_of[11], (INNER, D), INNER ** -0.5, 0.25, ((0, 4),), jnp.float32)
    prenorm_second = jnp.clip(1.0 + 0.18 * jax.random.normal(key_of[12], (D,), jnp.float32), 0.1, 1.9)
    inproj_second = bell_draw(key_of[13], (D, 2, INNER), D ** -0.5, 0.375, ((2, 4),), jnp.float32)
    statemap_second = bell_draw(key_of[14], (D, 2, STATE), D ** -0.5, 0.375, (), jnp.float32)
    stepmap_second = bell_draw(key_of[15], (D, HEADS), D ** -0.5, 0.375, ((1, 4),), jnp.float32)
    stepbias_second = jnp.clip(jax.random.uniform(key_of[16], (HEADS,), jnp.float32, -1.0, 1.0) * block_levels(key_of[16], (HEADS,), ((0, 4),), -0.4, 0.0), -1.0, 1.0)
    rates_second = draw_rates_second(jax.random.fold_in(key_of[21], 71), part)
    skipgain_second = jnp.clip(0.5 + 1.0 * jax.random.uniform(key_of[18], (HEADS,), jnp.float32) ** block_levels(key_of[18], (HEADS,), ((0, 4),), -0.2, 0.2), 0.5, 1.5)
    outnorm_second = jnp.clip(1.0 + 0.18 * jax.random.normal(key_of[19], (INNER,), jnp.float32), 0.1, 1.9)
    outproj_second = bell_draw(key_of[20], (INNER, D), INNER ** -0.5, 0.25, ((0, 4),), jnp.float32)
    return dict(token_ids=token_ids, embedding=embedding, complement=complement, prenorm_first=prenorm_first, inproj_first=inproj_first, statemap_first=statemap_first, stepmap_first=stepmap_first, stepbias_first=stepbias_first, rates_first=rates_first, skipgain_first=skipgain_first, outnorm_first=outnorm_first, outproj_first=outproj_first, prenorm_second=prenorm_second, inproj_second=inproj_second, statemap_second=statemap_second, stepmap_second=stepmap_second, stepbias_second=stepbias_second, rates_second=rates_second, skipgain_second=skipgain_second, outnorm_second=outnorm_second, outproj_second=outproj_second)


highest = lax.Precision.HIGHEST
epsilon = 1e-05

def matmul(left, right):
    return jnp.dot(left, right, precision=highest, preferred_element_type=jnp.float32)

def rms_scale(values, gain_vec):
    return values * lax.rsqrt(lax.optimization_barrier(jnp.mean(values * values, axis=-1, keepdims=True)) + epsilon) * gain_vec

def running(values, axis_number, reverse):
    if reverse:
        return jnp.flip(jnp.cumsum(jnp.flip(values, axis_number), axis_number), axis_number)
    return jnp.cumsum(values, axis_number)

def project(layer_in, prenorm, inproj, statemap, stepmap, stepbias, rates):
    normed = rms_scale(layer_in, prenorm)
    length = layer_in.shape[0]
    inner_width = inproj.shape[2]
    head_count = stepmap.shape[1]
    both_parts = matmul(normed, inproj.reshape(inproj.shape[0], 2 * inner_width))
    gate_vals = both_parts[:, :inner_width]
    x_heads = both_parts[:, inner_width:].reshape(length, head_count, inner_width // head_count)
    state_width = statemap.shape[2]
    write_read = matmul(normed, statemap.reshape(statemap.shape[0], 2 * state_width))
    write_vecs = write_read[:, :state_width]
    read_vecs = write_read[:, state_width:]
    step_sizes = jax.nn.softplus(matmul(normed, stepmap) + stepbias)
    log_decay = -rates * step_sizes
    return (gate_vals, x_heads, write_vecs, read_vecs, step_sizes, log_decay)

def gated_norm(outputs, gate_vals, outnorm):
    length, head_count, head_dim = outputs.shape
    gated_vals = outputs * jax.nn.silu(gate_vals).reshape(outputs.shape)
    normed = gated_vals * lax.rsqrt(lax.optimization_barrier(jnp.mean(gated_vals * gated_vals, axis=-1, keepdims=True)) + epsilon)
    return normed.reshape(length, head_count * head_dim) * outnorm

def block_scan(x_heads, step_sizes, log_decay, write_vecs, read_vecs, skipgain, reverse):
    length, head_count, head_dim = x_heads.shape
    blocks = length // BLOCK
    block_items = (x_heads.reshape(blocks, BLOCK, head_count, head_dim), step_sizes.reshape(blocks, BLOCK, head_count), log_decay.reshape(blocks, BLOCK, head_count), write_vecs.reshape(blocks, BLOCK, -1), read_vecs.reshape(blocks, BLOCK, -1))
    positions = jnp.arange(BLOCK)
    if reverse:
        allowed = positions[None, :] >= positions[:, None]
    else:
        allowed = positions[None, :] <= positions[:, None]
    allowed = allowed[:, :, None]

    def block_step(carry_state, item_group):
        x_block, step_block, log_block, write_block, read_block = item_group
        cumulative = running(log_block, 0, reverse)
        pair_products = matmul(read_block, write_block.T)
        differ = cumulative[:, None, :] - cumulative[None, :, :]
        weights = jnp.where(allowed, jnp.exp(jnp.where(allowed, differ, 0.0)), 0.0) * pair_products[:, :, None] * step_block[None, :, :]
        outputs = jnp.einsum('qsh,shp->qhp', weights, x_block, precision=highest)
        outputs = outputs + jnp.exp(cumulative)[:, :, None] * jnp.einsum('qn,hpn->qhp', read_block, carry_state, precision=highest)
        outputs = outputs + skipgain[None, :, None] * x_block
        if reverse:
            end_log = cumulative[0]
        else:
            end_log = cumulative[-1]
        scaled = x_block * (jnp.exp(end_log[None, :] - cumulative) * step_block)[:, :, None]
        new_state = jnp.exp(end_log)[:, None, None] * carry_state + jnp.einsum('shp,sn->hpn', scaled, write_block, precision=highest)
        return (new_state, outputs)
    start_state = jnp.zeros((head_count, head_dim, write_vecs.shape[1]), jnp.float32)
    final_state, outputs = lax.scan(block_step, start_state, block_items, reverse=reverse)
    return outputs.reshape(length, head_count, head_dim)

def reference(token_ids, embedding, complement, prenorm_first, inproj_first, statemap_first, stepmap_first, stepbias_first, rates_first, skipgain_first, outnorm_first, outproj_first, prenorm_second, inproj_second, statemap_second, stepmap_second, stepbias_second, rates_second, skipgain_second, outnorm_second, outproj_second):
    embedded = jnp.take(embedding, token_ids, axis=0)
    gate_vals, x_heads, write_vecs, read_vecs, step_sizes, log_decay = project(embedded, prenorm_first, inproj_first, statemap_first, stepmap_first, stepbias_first, rates_first)
    forward_out = block_scan(x_heads, step_sizes, log_decay, write_vecs, read_vecs, skipgain_first, False)
    backward_out = block_scan(x_heads, step_sizes, log_decay, write_vecs, read_vecs, skipgain_first, True)
    mixed = gated_norm(forward_out, gate_vals, outnorm_first) + gated_norm(backward_out, gate_vals, outnorm_first)
    hidden = embedded + matmul(mixed, outproj_first)
    mirrored = jnp.take(hidden[::-1], complement, axis=1)
    gate_two, x_two, write_two, read_two, step_two, log_two = project(mirrored, prenorm_second, inproj_second, statemap_second, stepmap_second, stepbias_second, rates_second)
    forward_two = block_scan(x_two, step_two, log_two, write_two, read_two, skipgain_second, False)
    return mirrored + matmul(gated_norm(forward_two, gate_two, outnorm_second), outproj_second)
```

```python
import jax
import jax.numpy as jnp
from jax import lax
from jax.experimental import pallas as pl
from jax.experimental.pallas import tpu as pltpu
from jax.sharding import PartitionSpec as P

F32, BF = jnp.float32, jnp.bfloat16
MESH = pl.DeviceIdType.MESH
EPS = 1e-05
NX, NZ, NC, NY = 4, 8, 2, 4
T = 256
V = 16


def mm(a, b):
    return lax.dot_general(a, b, (((1,), (0,)), ((), ())), preferred_element_type=F32)


def mmt(a, b):
    return lax.dot_general(a, b, (((1,), (1,)), ((), ())), preferred_element_type=F32)


def split2(a):
    hi = a.astype(BF)
    return hi, (a - hi.astype(F32)).astype(BF)


def split3(a):
    hi = a.astype(BF)
    rest = a - hi.astype(F32)
    mid = rest.astype(BF)
    return hi, mid, (rest - mid.astype(F32)).astype(BF)


def dot3(a, b, f=mm):
    ah, al = a if isinstance(a, tuple) else split2(a)
    bh, bl = b if isinstance(b, tuple) else split2(b)
    return f(ah, bh) + (f(ah, bl) + f(al, bh))


def exact_left(a, b):
    h, m, l = split3(b)
    return mm(a, h) + (mm(a, m) + mm(a, l))


def exact_right(a, b):
    h, m, l = split3(a)
    return mm(h, b) + (mm(m, b) + mm(l, b))


def iota(shape, dim):
    return lax.broadcasted_iota(jnp.int32, shape, dim)


def softplus(a):
    return jnp.maximum(a, 0.0) + jnp.log1p(jnp.exp(-jnp.abs(a)))


def silu(a):
    return a / (1.0 + jnp.exp(-a))


def rms(a, gain):
    return a * lax.rsqrt(jnp.mean(a * a, axis=-1, keepdims=True) + EPS) * gain


def xor(a, k, bits):
    out = a
    for i in range(bits):
        if k >> i & 1:
            out = out + (1 << i) * (1 - 2 * (a // (1 << i) % 2))
    return out


def pick(flag, a, b):
    return jnp.where(jnp.full(a.shape, flag, jnp.int32) > 0, a, b)


def as_int(cond):
    return jnp.where(cond, 1, 0)


def halves(pair):
    return jnp.where(iota((1, 128), 1) < 64, pair[:, 0:1], pair[:, 1:2])


def scan_rows(coef, decay, reverse):
    rows = iota(coef.shape, 0)
    k = 1
    while k < T:
        if reverse:
            inside = rows < T - k
            shifted_c, shifted_d = pltpu.roll(coef, T - k, 0), pltpu.roll(decay, T - k, 0)
        else:
            inside = rows >= k
            shifted_c, shifted_d = pltpu.roll(coef, k, 0), pltpu.roll(decay, k, 0)
        coef = coef + jnp.where(inside, decay * shifted_c, 0.0)
        decay = jnp.where(inside, decay * shifted_d, decay)
        k *= 2
    return coef, decay


NAMES = (
    "tok", "emb", "comp",
    "pn1", "ip1", "sm1", "sp1", "sb1", "ra1", "sk1", "on1", "op1",
    "pn2", "ip2", "sm2", "sp2", "sb2", "ra2", "sk2", "on2", "op2",
)
SHAPES = (
    (1, T), (V, 256), (1, 256),
    (1, 256), (512, 128), (512, 128), (2, 256), (1, 2), (1, 2), (1, 2), (1, 128), (128, 256),
    (1, 256), (512, 128), (512, 128), (2, 256), (1, 2), (1, 2), (1, 2), (1, 128), (128, 256),
)
TYPES = (jnp.int32, F32, jnp.int32) + (F32,) * 18
N_IN = len(NAMES)
TAB = 80
MSG = 72

SCRATCH = (
    ("tokbuf", (8, 1, T), jnp.int32),
    ("tokm", (1, T), jnp.int32),
    ("tsend", (TAB, 128), F32),
    ("ytab", (NY, TAB, 128), F32),
    ("wo1", (NY, 128, 256), F32),
    ("wo2", (NY, 128, 256), F32),
    ("ztile", (8, 128), F32),
    ("zbuf", (NZ, 8, 128), F32),
    ("mir", (T, 256), F32),
    ("st", (128, 128), F32),
    ("e1s", (MSG, 128), F32),
    ("e1r", (MSG, 128), F32),
    ("bs", (3, MSG, 128), F32),
    ("br", (3, MSG, 128), F32),
    ("xs", (MSG, 128), F32),
    ("xr", (NX, MSG, 128), F32),
    ("ks", (64, 128), F32),
    ("kr", (64, 128), F32),
    ("gs", (T, 128), F32),
    ("gr", (NY, 64, 128), F32),
)
N_SEND = 64


def kernel(*refs):
    hbm = dict(zip(NAMES, refs[:N_IN]))
    out_ref = refs[N_IN]
    vm = dict(zip(NAMES, refs[N_IN + 1 :]))
    sc = {s[0]: r for s, r in zip(SCRATCH, refs[N_IN + 1 + N_IN :])}
    in_sem, send_sem, recv_sem = refs[-3:]

    seq, y = lax.axis_index("seq"), lax.axis_index("head")
    x, z, c = seq // (NZ * NC), seq // NC % NZ, seq % NC
    xc = x * NC + c
    xm, zm = NX - 1 - x, NZ - 1 - z

    def seq_of(xi, zi, ci):
        return (xi * NZ + zi) * NC + ci

    y_peers = [xor(y, k, 2) for k in range(1, NY)]
    xc_peers = [xor(xc, k, 3) for k in range(1, 8)]
    z_peers = [xor(z, k, 3) for k in range(1, NZ)]
    mirror = seq_of(xm, zm, 1 - c)

    barrier = pltpu.get_barrier_semaphore()

    def greet(where):
        pl.semaphore_signal(barrier, inc=1, device_id=where, device_id_type=MESH)

    for p in z_peers:
        greet({"seq": seq_of(x, p, c)})
    greet({"seq": mirror})
    for p in xc_peers:
        greet({"seq": seq_of(p // NC, z, p % NC)})
    for p in y_peers:
        greet({"head": p})

    loads = {n: pltpu.make_async_copy(hbm[n], vm[n], in_sem.at[i]) for i, n in enumerate(NAMES)}
    for n in NAMES:
        loads[n].start()
    own_tok = pltpu.make_async_copy(hbm["tok"], sc["tokbuf"].at[xc], in_sem.at[N_IN])
    own_tok.start()

    used = [0]

    def remote(src, dst, where):
        i = used[0]
        used[0] += 1
        return pltpu.make_async_remote_copy(
            src_ref=src, dst_ref=dst, send_sem=send_sem.at[i], recv_sem=recv_sem.at[i],
            device_id=where, device_id_type=MESH,
        )

    for n in NAMES:
        loads[n].wait()
    own_tok.wait()

    lane = iota((1, 128), 1)
    w1 = vm["ip1"]
    gate_w, inner_w = w1[pl.ds(0, 256, stride=2), :], w1[pl.ds(1, 256, stride=2), :]
    s1 = vm["sm1"]
    write_w, read_w = s1[pl.ds(0, 256, stride=2), :], s1[pl.ds(1, 256, stride=2), :]
    emb = vm["emb"][...]
    normed = rms(emb, vm["pn1"][...])
    normed2 = split2(normed)
    table = dot3(normed2, jnp.concatenate([gate_w, inner_w, write_w, read_w], axis=1))
    gate_t, inner_t, write_t, read_t = (table[:, 128 * i : 128 * (i + 1)] for i in range(4))
    sp = vm["sp1"][...]
    sb, ra, sk = vm["sb1"][...], vm["ra1"][...], vm["sk1"][...]
    r128 = iota((128, 256), 0)
    sp_p = jnp.where(r128 < 64, sp[0:1], sp[1:2])
    sp_alt = jnp.where(r128 // 16 % 2 == 0, sp[0:1], sp[1:2])
    logits = dot3(normed2, jnp.concatenate([sp_p, sp_alt], axis=0), mmt)
    step_p = softplus(logits[:, :128] + halves(sb))
    alt = lane // 16 % 2 == 0
    log_alt = -jnp.where(alt, ra[:, 0:1], ra[:, 1:2]) * softplus(
        logits[:, 128:] + jnp.where(alt, sb[:, 0:1], sb[:, 1:2])
    )
    even = iota((8, 128), 0) % 2 == 0
    sp_r = jnp.where(iota((8, 256), 0) % 2 == 0, sp[0:1], sp[1:2])
    log_r = -jnp.where(even, ra[:, 0:1], ra[:, 1:2]) * softplus(
        dot3(sp_r, jnp.concatenate([normed] * 8, axis=0), mmt)
        + jnp.where(even, sb[:, 0:1], sb[:, 1:2])
    )
    tsend = sc["tsend"]
    tsend[0:16] = step_p * inner_t
    tsend[16:32] = halves(sk) * inner_t
    tsend[32:48] = silu(gate_t)
    tsend[48:64] = log_alt
    tsend[64:72] = log_r
    tsend[72:80] = jnp.broadcast_to(vm["on1"][...], (8, 128))
    g_tab = dot3(read_t, jnp.concatenate([write_t] * 8, axis=0), mmt)

    pl.semaphore_wait(barrier, 18)

    ytab, tokbuf = sc["ytab"], sc["tokbuf"]
    tab_copies = [remote(tsend, ytab.at[y], {"head": p}) for p in y_peers]
    tok_copies = [
        remote(hbm["tok"], tokbuf.at[xc], {"seq": seq_of(p // NC, z, p % NC)}) for p in xc_peers
    ]
    tokm_copy = remote(hbm["tok"], sc["tokm"], {"seq": mirror})
    wo1_copies = [remote(vm["op1"], sc["wo1"].at[y], {"head": p}) for p in y_peers]
    wo2_copies = [remote(vm["op2"], sc["wo2"].at[y], {"head": p}) for p in y_peers]
    for cp in tab_copies + tok_copies + [tokm_copy] + wo1_copies + wo2_copies:
        cp.start()
    ytab[pl.ds(y, 1)] = tsend[...][None]
    sc["wo1"][pl.ds(y, 1)] = vm["op1"][...][None]
    sc["wo2"][pl.ds(y, 1)] = vm["op2"][...][None]

    tri_r, tri_c = iota((256, 256), 0), iota((256, 256), 1)
    one = jnp.ones((), F32)

    def mask_bf(cond):
        return jnp.where(cond, one, 0.0 * one).astype(BF)

    perm = mask_bf(vm["comp"][...] == tri_r)
    w2 = vm["ip2"]
    s2 = vm["sm2"]
    w2_all = split2(
        jnp.concatenate(
            [
                w2[pl.ds(0, 256, stride=2), :],
                w2[pl.ds(1, 256, stride=2), :],
                s2[pl.ds(0, 256, stride=2), :],
                s2[pl.ds(1, 256, stride=2), :],
            ],
            axis=1,
        )
    )
    sp2 = vm["sp2"][...]
    sp2_p = split2(jnp.where(r128 < 64, sp2[0:1], sp2[1:2]))
    emb_p = mm(jnp.concatenate(split3(emb), axis=0), perm).astype(BF)

    for cp in tok_copies:
        cp.wait_recv()
    for cp in tab_copies:
        cp.wait_recv()
    r16 = iota((V, T), 0)
    onehot = jnp.concatenate([as_int(tokbuf[b] == r16) for b in range(8)], axis=0)
    onehot = onehot.astype(F32).astype(BF)
    counts = mm(
        onehot,
        jnp.concatenate(
            [mask_bf(tri_r > tri_c), mask_bf(tri_r < tri_c), jnp.ones((256, 128), BF)], axis=1
        ),
    ).astype(BF)
    row8 = iota((8, 128), 0)
    log_hv = ytab[0, 64:72]
    for i in range(1, NY):
        log_hv = jnp.where(row8 // 2 == i, ytab[i, 64:72], log_hv)
    r64, l64 = iota((64, 128), 0), iota((64, 128), 1)
    log_bd = jnp.where(r64 // 8 == l64 // 16, jnp.concatenate([log_hv] * 8, axis=0), 0.0)
    cums = exact_right(log_bd, counts)
    weight = jnp.exp(cums[:, :512])
    weight = jnp.concatenate([weight[:, :256], weight[:, 256:]], axis=0)
    wh, wl = split2(weight)
    sums = mmt(wh, onehot) + mmt(wl, onehot)
    r2, l2 = iota((128, 128), 0), iota((128, 128), 1)
    sums = jnp.where(r2 // 8 % 8 == l2 // 16, sums, 0.0)
    for shift in (64, 32, 16):
        sums = sums + pltpu.roll(sums, shift, 1)
    sums = jnp.where(r2 % 8 == l2 // 16, sums, 0.0)
    totals = jnp.where(r64 % 8 == l64 // 16, cums[:, 512:], 0.0)

    def fold(a, i):
        return jnp.sum(a[8 * i : 8 * i + 8], axis=0, keepdims=True)

    cf = [fold(sums, b) for b in range(8)]
    cb = [fold(sums, 8 + b) for b in range(8)]
    ld = [fold(totals, b) for b in range(8)]
    cf_pair = [jnp.exp(ld[2 * i + 1]) * cf[2 * i] + cf[2 * i + 1] for i in range(NX)]
    cb_pair = [jnp.exp(ld[2 * i]) * cb[2 * i + 1] + cb[2 * i] for i in range(NX)]
    ld_pair = [ld[2 * i] + ld[2 * i + 1] for i in range(NX)]
    rows = [pick(as_int(xm >= i), cf_pair[i], cb_pair[i]) for i in range(NX)]
    own_b, sib, sib_ld, packed = cb_pair[0], cf[0], ld[0], ld_pair[0]
    for i in range(NX):
        here = as_int(xm == i)
        own_b = pick(here, cb_pair[i], own_b)
        sib = pick(here, pick(c, cb[2 * i + 1], cf[2 * i]), sib)
        sib_ld = pick(here, pick(c, ld[2 * i + 1], ld[2 * i]), sib_ld)
        packed = jnp.where(lane % 16 == i, ld_pair[i], packed)
    tile = jnp.concatenate(rows + [own_b, packed, sib, sib_ld], axis=0)
    ztile, zbuf = sc["ztile"], sc["zbuf"]
    ztile[...] = tile
    z_copies = [remote(ztile, zbuf.at[z], {"seq": seq_of(x, p, c)}) for p in z_peers]
    for cp in z_copies:
        cp.start()
    zbuf[pl.ds(z, 1)] = tile[None]

    def lanes_of(a, b):
        return jnp.concatenate([ytab[i, a:b] for i in range(NY)], axis=1)

    row16 = iota((V, 128), 0)
    l16 = iota((V, 128), 1)
    log_t = ytab[0, 48:64]
    for i in range(1, NY):
        log_t = jnp.where(l16 // 32 == i, ytab[i, 48:64], log_t)
    eye_t = jnp.where(row16 == l16 % 16, 1.0, 0.0)
    tables = jnp.concatenate([lanes_of(32, 48), lanes_of(16, 32), g_tab, jnp.exp(log_t), eye_t], axis=1)
    tables = jnp.concatenate([jnp.concatenate(split3(tables), axis=0), emb_p], axis=1)
    inner_rep = jnp.concatenate([lanes_of(0, 16)] * 8, axis=0)
    bd = iota((128, 512), 0) // 16 == iota((128, 512), 1) // 64
    x_bd = split2(jnp.where(bd, inner_rep, 0.0))
    outnorm_all = lanes_of(72, 73)
    tokm_copy.wait_recv()
    hot_m = as_int(sc["tokm"][...] == r16).astype(F32).astype(BF)
    rev = mask_bf(tri_r + tri_c == T - 1)
    hot_rev = mmt(rev, jnp.concatenate([hot_m] * 3, axis=0)).astype(BF)
    taken = mm(hot_rev, tables)
    silu_g, skip_x = taken[:, :512], taken[:, 512:1024]
    g_row, decay, hot = taken[:, 1024:1152], taken[:, 1152:1280], taken[:, 1280:1408]
    embedded = taken[:, 1408:]
    up_c, up_p = scan_rows(hot, decay, False)
    dn_c, dn_p = scan_rows(hot, decay, True)
    for cp in wo1_copies:
        cp.wait_recv()
    wo1h, wo1l = split2(sc["wo1"][...].reshape(512, 256))
    wo1_p = (mm(wo1h, perm).astype(BF), mm(wo1l, perm).astype(BF))

    for cp in z_copies:
        cp.wait_recv()
    ls, lr = iota((128, 512), 1), iota((128, 512), 0)
    spread = mask_bf((lr // 16 == ls % 128 // 16) & (lr % 16 == ls // 128))
    ld_all = exact_right(zbuf[:, 5, :], spread)
    ld_all = jnp.concatenate([ld_all[:, 128 * i : 128 * i + 128] for i in range(NX)], axis=0)
    qm = xm * NZ + zm
    q, q2 = iota((32, 32), 0), iota((32, 32), 1)
    between = ((q2 > q) & (q2 < qm)) | ((q2 < q) & (q2 > qm))
    share = jnp.exp(exact_left(mask_bf(between), ld_all))
    zrow = iota((8, 128), 0)
    coefs = jnp.concatenate(
        [
            jnp.where((zrow > zm) & (jnp.full((8, 128), xm, jnp.int32) == i), zbuf[:, 4, :], zbuf[:, i, :])
            for i in range(NX)
        ],
        axis=0,
    )
    terms = share * coefs
    qrow = iota((32, 128), 0)
    carry_f = jnp.sum(jnp.where(qrow < qm, terms, 0.0), axis=0, keepdims=True)
    carry_b = jnp.sum(jnp.where(qrow > qm, terms, 0.0), axis=0, keepdims=True)
    at_m = zbuf[pl.ds(zm, 1)].reshape(8, 128)
    sib, sib_d = at_m[6:7], jnp.exp(at_m[7:8])
    carry_f = pick(c, carry_f, sib_d * carry_f + sib)
    carry_b = pick(c, sib_d * carry_b + sib, carry_b)
    coef = jnp.concatenate([up_c + up_p * carry_b, dn_c + dn_p * carry_f], axis=0)
    coef = coef * jnp.concatenate([g_row] * 2, axis=0)
    ssm = dot3(coef, x_bd)

    same_head = mask_bf(r2 // 64 == l2 // 64)

    def head_scale(w):
        parts = []
        for i in range(w.shape[1] // 128):
            h, l = split2(w[:, 128 * i : 128 * i + 128] ** 2)
            parts.append(mm(h, same_head) + mm(l, same_head))
        sq = parts[0] if len(parts) == 1 else jnp.concatenate(parts, axis=1)
        return lax.rsqrt(sq * (1.0 / 64) + EPS)

    w_up = (ssm[:T] + skip_x) * silu_g
    w_dn = (ssm[T:] + skip_x) * silu_g
    mixed = (w_up * head_scale(w_up) + w_dn * head_scale(w_dn)) * outnorm_all
    mirrored = embedded + dot3(mixed, wo1_p)
    mir = sc["mir"]
    mir[...] = mirrored

    n2 = split2(rms(mirrored, vm["pn2"][...]))
    both = dot3(n2, w2_all)
    gate, inner, write, read = (both[:, 128 * i : 128 * (i + 1)] for i in range(4))
    step = softplus(dot3(n2, sp2_p, mmt) + halves(vm["sb2"][...]))
    cum = exact_left(mask_bf(tri_r >= tri_c), -halves(vm["ra2"][...]) * step)
    end = cum[T - 1 : T]
    stepped = inner * step
    write_t2 = split2(write.T)
    state = dot3(write_t2, stepped * jnp.exp(end - cum))
    own_d = jnp.exp(end)
    st, e1s, e1r = sc["st"], sc["e1s"], sc["e1r"]
    st[...] = state
    e1s[0:64] = st[pl.ds(pl.multiple_of(64 * (1 - c), 64), 64), :]
    e1s[64:72] = jnp.broadcast_to(own_d, (8, 128))
    e1 = remote(e1s, e1r, {"seq": seq_of(x, z, 1 - c)})
    e1.start()
    own_half = st[pl.ds(pl.multiple_of(64 * c, 64), 64), :]

    read2 = split2(read)
    pairs = dot3(read2, write_t2)
    cum_t = cum.T
    allowed = tri_r >= tri_c
    local = halves(vm["sk2"][...]) * inner
    first = iota((T, 128), 1) < 64
    for h in range(2):
        diff = cum[:, 64 * h : 64 * h + 1] - cum_t[64 * h : 64 * h + 1, :]
        wts = jnp.where(allowed, jnp.exp(jnp.where(allowed, diff, 0.0)) * pairs, 0.0)
        local = local + dot3(wts, jnp.where(first if h == 0 else ~first, stepped, 0.0))
    gate_s = silu(gate)

    e1.wait_recv()
    got, got_d = e1r[0:64], e1r[64:65]
    s0, s1_ = pick(c, got, own_half), pick(c, own_half, got)
    d0, d1 = pick(c, got_d, own_d), pick(c, own_d, got_d)
    tot, dec = d1 * s0 + s1_, d0 * d1
    pre, pre_d = jnp.zeros((64, 128), F32), jnp.ones((1, 128), F32)
    rounds = []
    for r in range(3):
        bs, br = sc["bs"].at[r], sc["br"].at[r]
        bs[0:64] = tot
        bs[64:72] = jnp.broadcast_to(dec, (8, 128))
        cp = remote(bs, br, {"seq": seq_of(x, xor(z, 1 << r, 3), c)})
        cp.start()
        rounds.append(cp)
        cp.wait_recv()
        got, got_d = br[0:64], br[64:65]
        later = z // (1 << r) % 2
        pre, pre_d = pick(later, pre_d * got + pre, pre), pick(later, got_d * pre_d, pre_d)
        tot = pick(later, dec * got + tot, got_d * tot + got)
        dec = dec * got_d
    xs, xr = sc["xs"], sc["xr"]
    xs[0:64] = tot
    xs[64:72] = jnp.broadcast_to(dec, (8, 128))
    x_copies = [remote(xs, xr.at[x], {"seq": seq_of(xor(x, k, 2), z, c)}) for k in range(1, NX)]
    for cp in x_copies:
        cp.start()
    xr[pl.ds(x, 1)] = xs[...][None]
    for cp in x_copies:
        cp.wait_recv()
    row_in = jnp.zeros((64, 128), F32)
    for i in range(NX - 1):
        row_in = pick(as_int(x > i), xr[i, 64:65] * row_in + xr[i, 0:64], row_in)
    k0 = pre_d * row_in + pre
    k1 = d0 * k0 + s0
    ks, kr = sc["ks"], sc["kr"]
    ks[...] = pick(c, k0, k1)
    k_copy = remote(ks, kr, {"seq": seq_of(x, z, 1 - c)})
    k_copy.start()
    mine = pick(c, k1, k0)
    k_copy.wait_recv()
    got = kr[...]
    carried = jnp.concatenate([pick(c, got, mine), pick(c, mine, got)], axis=0)
    y2 = local + dot3(read2, carried) * jnp.exp(cum)
    w = y2 * gate_s
    gs, gr = sc["gs"], sc["gr"]
    gs[...] = w * head_scale(w) * vm["on2"][...]

    def share_of(ref, p):
        return ref.at[pl.ds(pl.multiple_of(64 * p, 64), 64), :]

    g_copies = [remote(share_of(gs, p), gr.at[y], {"head": p}) for p in y_peers]
    for cp in g_copies:
        cp.start()
    gr[pl.ds(y, 1)] = share_of(gs, y)[...][None]
    for cp in wo2_copies:
        cp.wait_recv()
    out = share_of(mir, y)[...]
    wo2 = [split2(sc["wo2"][i]) for i in range(NY)]
    for cp in g_copies:
        cp.wait_recv()
    for i in range(NY):
        out = out + dot3(gr[i], wo2[i])
    out_ref[...] = out

    for cp in (
        tab_copies + tok_copies + [tokm_copy] + wo1_copies + wo2_copies + z_copies
        + [e1] + rounds + x_copies + [k_copy] + g_copies
    ):
        cp.wait_send()


def per_device(*args):
    a = dict(zip(NAMES, args))
    for n in ("sp1", "sp2"):
        a[n] = a[n].T
    flat = [a[n].reshape(s) for n, s in zip(NAMES, SHAPES)]
    return pl.pallas_call(
        kernel,
        out_shape=jax.ShapeDtypeStruct((64, 256), F32),
        in_specs=[pl.BlockSpec(memory_space=pl.ANY)] * N_IN,
        out_specs=pl.BlockSpec(memory_space=pltpu.VMEM),
        scratch_shapes=[pltpu.VMEM(s, t) for s, t in zip(SHAPES, TYPES)]
        + [pltpu.VMEM(s, t) for _, s, t in SCRATCH]
        + [
            pltpu.SemaphoreType.DMA((N_IN + 1,)),
            pltpu.SemaphoreType.DMA((N_SEND,)),
            pltpu.SemaphoreType.DMA((N_SEND,)),
        ],
        compiler_params=pltpu.CompilerParams(
            collective_id=0, has_side_effects=True, vmem_limit_bytes=48 * 2**20
        ),
    )(*flat)


def solution(mesh):
    tokens = P(("rep", "seq"))
    layer = (P(), P(None, None, "head"), P(), P(None, "head")) + (P("head"),) * 4 + (P("head", None),)
    in_specs = (tokens, P(), P()) + layer + layer
    return jax.shard_map(
        per_device,
        mesh=mesh,
        in_specs=in_specs,
        out_specs=P(("rep", "seq", "head"), None),
        check_vma=False,
    )
```

```python
import jax
import jax.numpy as jnp
from jax import lax
from jax.experimental import pallas as pl
from jax.experimental.pallas import tpu as pltpu
from jax.sharding import PartitionSpec as P

F32, BF = jnp.float32, jnp.bfloat16
MESH = pl.DeviceIdType.MESH
EPS = 1e-05
NX, NZ, NC, NY = 4, 8, 2, 4
T = 256
V = 16


def mm(a, b):
    return lax.dot_general(a, b, (((1,), (0,)), ((), ())), preferred_element_type=F32)


def mmt(a, b):
    return lax.dot_general(a, b, (((1,), (1,)), ((), ())), preferred_element_type=F32)


def split2(a):
    hi = a.astype(BF)
    return hi, (a - hi.astype(F32)).astype(BF)


def split3(a):
    hi = a.astype(BF)
    rest = a - hi.astype(F32)
    mid = rest.astype(BF)
    return hi, mid, (rest - mid.astype(F32)).astype(BF)


def dot3(a, b, f=mm):
    ah, al = a if isinstance(a, tuple) else split2(a)
    bh, bl = b if isinstance(b, tuple) else split2(b)
    return f(ah, bh) + (f(ah, bl) + f(al, bh))


def dot3_short(a, b):
    ah, al = a if isinstance(a, tuple) else split2(a)
    bh, bl = b if isinstance(b, tuple) else split2(b)
    return mm(jnp.concatenate([ah, al], axis=1), jnp.concatenate([bh, bh], axis=0)) + mm(ah, bl)


def exact_left(a, b):
    h, l = split2(b)
    return mm(a, h) + mm(a, l)


def exact_right(a, b):
    h, m, l = split3(a)
    return mm(h, b) + (mm(m, b) + mm(l, b))


def iota(shape, dim):
    return lax.broadcasted_iota(jnp.int32, shape, dim)


def softplus(a):
    return jnp.maximum(a, 0.0) + jnp.log1p(jnp.exp(-jnp.abs(a)))


def silu(a):
    return a / (1.0 + jnp.exp(-a))


def rms(a, gain):
    return a * lax.rsqrt(jnp.mean(a * a, axis=-1, keepdims=True) + EPS) * gain


def xor(a, k, bits):
    out = a
    for i in range(bits):
        if k >> i & 1:
            out = out + (1 << i) * (1 - 2 * (a // (1 << i) % 2))
    return out


def pick(flag, a, b):
    return jnp.where(jnp.full(a.shape, flag, jnp.int32) > 0, a, b)


def as_int(cond):
    return jnp.where(cond, 1, 0)


def halves(pair):
    return jnp.where(iota((1, 128), 1) < 64, pair[:, 0:1], pair[:, 1:2])


def scan_rows(coef, decay, reverse):
    rows = iota(coef.shape, 0)
    k = 1
    while k < T:
        if reverse:
            inside = rows < T - k
            shifted_c, shifted_d = pltpu.roll(coef, T - k, 0), pltpu.roll(decay, T - k, 0)
        else:
            inside = rows >= k
            shifted_c, shifted_d = pltpu.roll(coef, k, 0), pltpu.roll(decay, k, 0)
        coef = coef + jnp.where(inside, decay * shifted_c, 0.0)
        decay = jnp.where(inside, decay * shifted_d, decay)
        k *= 2
    return coef, decay


NAMES = (
    "tok", "emb", "comp",
    "pn1", "ip1", "sm1", "sp1", "sb1", "ra1", "sk1", "on1", "op1",
    "pn2", "ip2", "sm2", "sp2", "sb2", "ra2", "sk2", "on2", "op2",
)
SHAPES = (
    (1, T), (V, 256), (1, 256),
    (1, 256), (512, 128), (512, 128), (2, 256), (1, 2), (1, 2), (1, 2), (1, 128), (128, 256),
    (1, 256), (512, 128), (512, 128), (2, 256), (1, 2), (1, 2), (1, 2), (1, 128), (128, 256),
)
TYPES = (jnp.int32, F32, jnp.int32) + (F32,) * 18
N_IN = len(NAMES)
TAB = 72
HALF = 32
MSG = HALF + 8

SCRATCH = (
    ("tokbuf", (8, 1, T), jnp.int32),
    ("tokm", (1, T), jnp.int32),
    ("lsend", (8, 128), F32),
    ("ltab", (NY, 8, 128), F32),
    ("tsend", (TAB, 128), F32),
    ("ytab", (NY, TAB, 128), F32),
    ("wo1", (NY, 128, 256), F32),
    ("wo1s", (128, 256), F32),
    ("wo2", (NY, 128, 256), F32),
    ("ztile", (8, 128), F32),
    ("zbuf", (NZ, 8, 128), F32),
    ("mir", (T, 256), F32),
    ("st", (128, 128), F32),
    ("e1s", (2, MSG, 128), F32),
    ("e1r", (2, MSG, 128), F32),
    ("bs", (6, MSG, 128), F32),
    ("br", (6, MSG, 128), F32),
    ("xs", (2, MSG, 128), F32),
    ("xr", (2, NX, MSG, 128), F32),
    ("ks", (2, HALF, 128), F32),
    ("kr", (2, HALF, 128), F32),
    ("rd", (T, 256), BF),
    ("loc", (T, 128), F32),
    ("gat", (T, 128), F32),
    ("cue", (T, 128), F32),
    ("gs", (T, 128), F32),
    ("gf", (64, 128), F32),
    ("gr", (NY, 64, 128), F32),
)
N_SEND = 72


def kernel(*refs):
    hbm = dict(zip(NAMES, refs[:N_IN]))
    out_ref = refs[N_IN]
    vm = dict(zip(NAMES, refs[N_IN + 1 :]))
    sc = {s[0]: r for s, r in zip(SCRATCH, refs[N_IN + 1 + N_IN :])}
    in_sem, send_sem, recv_sem = refs[-3:]

    seq, y = lax.axis_index("seq"), lax.axis_index("head")
    x, z, c = seq // (NZ * NC), seq // NC % NZ, seq % NC
    xc = x * NC + c
    xm, zm = NX - 1 - x, NZ - 1 - z

    def seq_of(xi, zi, ci):
        return (xi * NZ + zi) * NC + ci

    y_peers = [xor(y, k, 2) for k in (2, 1, 3)]
    xc_peers = [xor(xc, k, 3) for k in (4, 5, 2, 3, 6, 7, 1)]
    z_peers = [xor(z, k, 3) for k in range(NZ - 1, 0, -1)]
    mirror = seq_of(xm, zm, 1 - c)

    barrier = pltpu.get_barrier_semaphore()

    def greet(where):
        pl.semaphore_signal(barrier, inc=1, device_id=where, device_id_type=MESH)

    for p in z_peers:
        greet({"seq": seq_of(x, p, c)})
    greet({"seq": mirror})
    for p in xc_peers:
        greet({"seq": seq_of(p // NC, z, p % NC)})
    for p in y_peers:
        greet({"head": p})

    loads = {n: pltpu.make_async_copy(hbm[n], vm[n], in_sem.at[i]) for i, n in enumerate(NAMES)}
    for n in NAMES:
        loads[n].start()
    own_tok = pltpu.make_async_copy(hbm["tok"], sc["tokbuf"].at[xc], in_sem.at[N_IN])
    own_tok.start()

    used = [0]

    def remote(src, dst, where):
        i = used[0]
        used[0] += 1
        return pltpu.make_async_remote_copy(
            src_ref=src, dst_ref=dst, send_sem=send_sem.at[i], recv_sem=recv_sem.at[i],
            device_id=where, device_id_type=MESH,
        )

    for n in NAMES:
        loads[n].wait()
    own_tok.wait()

    lane = iota((1, 128), 1)
    w1 = vm["ip1"]
    gate_w, inner_w = w1[pl.ds(0, 256, stride=2), :], w1[pl.ds(1, 256, stride=2), :]
    s1 = vm["sm1"]
    write_w, read_w = s1[pl.ds(0, 256, stride=2), :], s1[pl.ds(1, 256, stride=2), :]
    emb = vm["emb"][...]
    normed = rms(emb, vm["pn1"][...])
    normed2 = split2(normed)
    table = dot3(normed2, jnp.concatenate([gate_w, inner_w, write_w, read_w], axis=1))
    gate_t, inner_t, write_t, read_t = (table[:, 128 * i : 128 * (i + 1)] for i in range(4))
    sp = vm["sp1"][...]
    sb, ra, sk = vm["sb1"][...], vm["ra1"][...], vm["sk1"][...]
    r128 = iota((128, 256), 0)
    sp_p = jnp.where(r128 < 64, sp[0:1], sp[1:2])
    sp_alt = jnp.where(r128 // 16 % 2 == 0, sp[0:1], sp[1:2])
    logits = dot3(normed2, jnp.concatenate([sp_p, sp_alt], axis=0), mmt)
    step_p = softplus(logits[:, :128] + halves(sb))
    alt = lane // 16 % 2 == 0
    log_alt = -jnp.where(alt, ra[:, 0:1], ra[:, 1:2]) * softplus(
        logits[:, 128:] + jnp.where(alt, sb[:, 0:1], sb[:, 1:2])
    )
    even = iota((8, 128), 0) % 2 == 0
    sp_r = jnp.where(iota((8, 256), 0) % 2 == 0, sp[0:1], sp[1:2])
    log_r = -jnp.where(even, ra[:, 0:1], ra[:, 1:2]) * softplus(
        dot3(sp_r, jnp.concatenate([normed] * 8, axis=0), mmt)
        + jnp.where(even, sb[:, 0:1], sb[:, 1:2])
    )
    lsend, tsend = sc["lsend"], sc["tsend"]
    lsend[...] = log_r
    tsend[0:16] = step_p * inner_t
    tsend[16:32] = halves(sk) * inner_t
    tsend[32:48] = silu(gate_t)
    tsend[48:64] = log_alt
    tsend[64:72] = jnp.broadcast_to(vm["on1"][...], (8, 128))
    g_tab = dot3(read_t, jnp.concatenate([write_t] * 8, axis=0), mmt)

    pl.semaphore_wait(barrier, 18)

    ltab, ytab, tokbuf = sc["ltab"], sc["ytab"], sc["tokbuf"]
    log_copies = [remote(lsend, ltab.at[y], {"head": p}) for p in y_peers]
    tok_copies = [
        remote(vm["tok"], tokbuf.at[xc], {"seq": seq_of(p // NC, z, p % NC)}) for p in xc_peers
    ]
    tokm_copy = remote(vm["tok"], sc["tokm"], {"seq": mirror})
    tab_copies = [remote(tsend, ytab.at[y], {"head": p}) for p in y_peers]
    for cp in log_copies + tok_copies + [tokm_copy] + tab_copies:
        cp.start()
    ltab[pl.ds(y, 1)] = log_r[None]
    ytab[pl.ds(y, 1)] = tsend[...][None]
    sc["wo2"][pl.ds(y, 1)] = vm["op2"][...][None]

    tri_r, tri_c = iota((256, 256), 0), iota((256, 256), 1)
    one = jnp.ones((), F32)

    def mask_bf(cond):
        return jnp.where(cond, one, 0.0 * one).astype(BF)

    perm = mask_bf(vm["comp"][...] == tri_r)
    wo1s = sc["wo1s"]
    wo1s[...] = exact_right(vm["op1"][...], perm)
    sc["wo1"][pl.ds(y, 1)] = wo1s[...][None]
    w2, s2 = vm["ip2"], vm["sm2"]
    gain = jnp.broadcast_to(vm["pn2"][...], (128, 256)).T
    w2_early = split2(
        jnp.concatenate([w2[pl.ds(1, 256, stride=2), :] * gain, s2[pl.ds(0, 256, stride=2), :] * gain], axis=1)
    )
    w2_late = split2(
        jnp.concatenate([w2[pl.ds(0, 256, stride=2), :] * gain, s2[pl.ds(1, 256, stride=2), :] * gain], axis=1)
    )
    sp2 = vm["sp2"][...] * vm["pn2"][...]
    sp2_p = split2(jnp.where(r128 < 64, sp2[0:1], sp2[1:2]))
    emb_p = mm(jnp.concatenate(split3(emb), axis=0), perm).astype(BF)

    for cp in tok_copies:
        cp.wait_recv()
    for cp in log_copies:
        cp.wait_recv()
    core_rows = pl.ds(pl.multiple_of(64 * c, 64), 64)
    wo1_copies = [
        remote(wo1s.at[core_rows], sc["wo1"].at[y, core_rows], {"head": p}) for p in y_peers
    ]
    for cp in wo1_copies:
        cp.start()
    r16 = iota((V, T), 0)
    onehot = jnp.concatenate([as_int(tokbuf[b] == r16) for b in range(8)], axis=0)
    onehot = onehot.astype(F32).astype(BF)
    counts = mm(
        onehot,
        jnp.concatenate(
            [mask_bf(tri_r > tri_c), mask_bf(tri_r < tri_c), jnp.ones((256, 128), BF)], axis=1
        ),
    ).astype(BF)
    row8 = iota((8, 128), 0)
    log_hv = ltab[0]
    for i in range(1, NY):
        log_hv = jnp.where(row8 // 2 == i, ltab[i], log_hv)
    r64, l64 = iota((64, 128), 0), iota((64, 128), 1)
    log_bd = jnp.where(r64 // 8 == l64 // 16, jnp.concatenate([log_hv] * 8, axis=0), 0.0)
    cums = mm(
        jnp.concatenate(split2(log_bd), axis=1), jnp.concatenate([counts, counts], axis=0)
    )
    weight = jnp.exp(cums[:, :512])
    weight = jnp.concatenate([weight[:, :256], weight[:, 256:]], axis=0)
    wh, wl = split2(weight)
    sums = mmt(wh, onehot) + mmt(wl, onehot)
    r2, l2 = iota((128, 128), 0), iota((128, 128), 1)
    sums = jnp.where(r2 // 8 % 8 == l2 // 16, sums, 0.0)
    for shift in (64, 32, 16):
        sums = sums + pltpu.roll(sums, shift, 1)
    sums = jnp.where(r2 % 8 == l2 // 16, sums, 0.0)
    totals = jnp.where(r64 % 8 == l64 // 16, cums[:, 512:], 0.0)

    def fold(a, i):
        return jnp.sum(a[8 * i : 8 * i + 8], axis=0, keepdims=True)

    cf = [fold(sums, b) for b in range(8)]
    cb = [fold(sums, 8 + b) for b in range(8)]
    ld = [fold(totals, b) for b in range(8)]
    cf_pair = [jnp.exp(ld[2 * i + 1]) * cf[2 * i] + cf[2 * i + 1] for i in range(NX)]
    cb_pair = [jnp.exp(ld[2 * i]) * cb[2 * i + 1] + cb[2 * i] for i in range(NX)]
    ld_pair = [ld[2 * i] + ld[2 * i + 1] for i in range(NX)]
    rows = [pick(as_int(xm >= i), cf_pair[i], cb_pair[i]) for i in range(NX)]
    own_b, sib, sib_ld, packed = cb_pair[0], cf[0], ld[0], ld_pair[0]
    for i in range(NX):
        here = as_int(xm == i)
        own_b = pick(here, cb_pair[i], own_b)
        sib = pick(here, pick(c, cb[2 * i + 1], cf[2 * i]), sib)
        sib_ld = pick(here, pick(c, ld[2 * i + 1], ld[2 * i]), sib_ld)
        packed = jnp.where(lane % 16 == i, ld_pair[i], packed)
    tile = jnp.concatenate(rows + [own_b, packed, sib, sib_ld], axis=0)
    ztile, zbuf = sc["ztile"], sc["zbuf"]
    ztile[...] = tile
    z_copies = [remote(ztile, zbuf.at[z], {"seq": seq_of(x, p, c)}) for p in z_peers]
    for cp in z_copies:
        cp.start()
    zbuf[pl.ds(z, 1)] = tile[None]

    def lanes_of(a, b):
        return jnp.concatenate([ytab[i, a:b] for i in range(NY)], axis=1)

    for cp in tab_copies:
        cp.wait_recv()
    row16 = iota((V, 128), 0)
    l16 = iota((V, 128), 1)
    log_t = ytab[0, 48:64]
    for i in range(1, NY):
        log_t = jnp.where(l16 // 32 == i, ytab[i, 48:64], log_t)
    eye_t = jnp.where(row16 == l16 % 16, 1.0, 0.0)
    tables = jnp.concatenate([lanes_of(32, 48), lanes_of(16, 32), g_tab, jnp.exp(log_t), eye_t], axis=1)
    tables = jnp.concatenate([jnp.concatenate(split3(tables), axis=0), emb_p], axis=1)
    inner_rep = jnp.concatenate([lanes_of(0, 16)] * 8, axis=0)
    bd = iota((128, 512), 0) // 16 == iota((128, 512), 1) // 64
    x_bd = split2(jnp.where(bd, inner_rep, 0.0))
    outnorm_all = lanes_of(64, 65)
    tokm_copy.wait_recv()
    hot_m = as_int(sc["tokm"][...] == r16).astype(F32).astype(BF)
    rev = mask_bf(tri_r + tri_c == T - 1)
    hot_rev = mmt(rev, jnp.concatenate([hot_m] * 3, axis=0)).astype(BF)
    taken = mm(hot_rev, tables)
    silu_g, skip_x = taken[:, :512], taken[:, 512:1024]
    g_row, decay, hot = taken[:, 1024:1152], taken[:, 1152:1280], taken[:, 1280:1408]
    embedded = taken[:, 1408:]
    up_c, up_p = scan_rows(hot, decay, False)
    dn_c, dn_p = scan_rows(hot, decay, True)
    other_core = {"seq": seq_of(x, z, 1 - c)}
    wo1_passed = []
    for cp, p in zip(wo1_copies, y_peers):
        cp.wait_recv()
        half = sc["wo1"].at[p, core_rows]
        wo1_passed.append(remote(half, half, other_core))
        wo1_passed[-1].start()

    for cp in z_copies:
        cp.wait_recv()
    ls, lr = iota((128, 512), 1), iota((128, 512), 0)
    spread = mask_bf((lr // 16 == ls % 128 // 16) & (lr % 16 == ls // 128))
    ld_all = mm(
        jnp.concatenate(split2(zbuf[:, 5, :]), axis=1), jnp.concatenate([spread, spread], axis=0)
    )
    ld_all = jnp.concatenate([ld_all[:, 128 * i : 128 * i + 128] for i in range(NX)], axis=0)
    qm = xm * NZ + zm
    q, q2 = iota((32, 32), 0), iota((32, 32), 1)
    between = ((q2 > q) & (q2 < qm)) | ((q2 < q) & (q2 > qm))
    share = jnp.exp(exact_left(mask_bf(between), ld_all))
    zrow = iota((8, 128), 0)
    coefs = jnp.concatenate(
        [
            jnp.where((zrow > zm) & (jnp.full((8, 128), xm, jnp.int32) == i), zbuf[:, 4, :], zbuf[:, i, :])
            for i in range(NX)
        ],
        axis=0,
    )
    terms = share * coefs
    qrow = iota((32, 128), 0)
    carry_f = jnp.sum(jnp.where(qrow < qm, terms, 0.0), axis=0, keepdims=True)
    carry_b = jnp.sum(jnp.where(qrow > qm, terms, 0.0), axis=0, keepdims=True)
    at_m = zbuf[pl.ds(zm, 1)].reshape(8, 128)
    sib, sib_d = at_m[6:7], jnp.exp(at_m[7:8])
    carry_f = pick(c, carry_f, sib_d * carry_f + sib)
    carry_b = pick(c, sib_d * carry_b + sib, carry_b)
    coef = jnp.concatenate([up_c + up_p * carry_b, dn_c + dn_p * carry_f], axis=0)
    coef = coef * jnp.concatenate([g_row] * 2, axis=0)
    ssm = dot3_short(coef, x_bd)

    same_head = jnp.where(r2 // 64 == l2 // 64, 1.0 / 64, 0.0).astype(BF)
    same_head = jnp.concatenate([same_head, same_head], axis=0)

    def head_scale(w):
        parts = []
        for i in range(w.shape[1] // 128):
            parts.append(mm(jnp.concatenate(split2(w[:, 128 * i : 128 * i + 128] ** 2), axis=1), same_head))
        sq = parts[0] if len(parts) == 1 else jnp.concatenate(parts, axis=1)
        return lax.rsqrt(sq + EPS)

    for cp in wo1_passed:
        cp.wait_recv()
    wo1_p = split2(sc["wo1"][...].reshape(512, 256))
    w_up = (ssm[:T] + skip_x) * silu_g
    w_dn = (ssm[T:] + skip_x) * silu_g
    mixed = (w_up * head_scale(w_up) + w_dn * head_scale(w_dn)) * outnorm_all
    mirrored = embedded + dot3(mixed, wo1_p)
    mir = sc["mir"]
    mir[...] = mirrored

    n2 = split2(mirrored)
    rms2 = lax.rsqrt(jnp.mean(mirrored * mirrored, axis=-1, keepdims=True) + EPS)
    step = softplus(dot3(n2, sp2_p, mmt) * rms2 + halves(vm["sb2"][...]))
    both = dot3(n2, w2_early) * rms2
    inner, write = both[:, :128], both[:, 128:]
    cum = exact_left(mask_bf(tri_r >= tri_c), -halves(vm["ra2"][...]) * step)
    end = cum[T - 1 : T]
    stepped = inner * step
    write_t2 = split2(write.T)
    state = dot3(write_t2, stepped * jnp.exp(end - cum))
    own_d = jnp.exp(end)
    st, e1s, e1r = sc["st"], sc["e1s"], sc["e1r"]
    st[...] = state
    chunks = range(2)

    def fill(buf, rows, decay):
        buf[0:HALF] = rows
        buf[HALF:MSG] = jnp.broadcast_to(decay, (8, 128))

    def part(core, i):
        return st[pl.ds(pl.multiple_of(64 * core + HALF * i, HALF), HALF), :]

    e1 = []
    for i in chunks:
        fill(e1s.at[i], part(1 - c, i), own_d)
        e1.append(remote(e1s.at[i], e1r.at[i], other_core))
        e1[i].start()

    s0, tot, dec, pre, pre_d = [None] * 2, [None] * 2, [None] * 2, [None] * 2, [None] * 2
    rounds = [[None] * 2 for _ in range(3)]

    def send_round(r, i):
        bs, br = sc["bs"].at[2 * r + i], sc["br"].at[2 * r + i]
        fill(bs, tot[i], dec[i])
        rounds[r][i] = remote(bs, br, {"seq": seq_of(x, xor(z, 1 << r, 3), c)})
        rounds[r][i].start()

    for i in chunks:
        own = part(c, i)
        e1[i].wait_recv()
        got, got_d = e1r[i, 0:HALF], e1r[i, HALF : HALF + 1]
        s0[i], s1_ = pick(c, got, own), pick(c, own, got)
        d0, d1 = pick(c, got_d, own_d), pick(c, own_d, got_d)
        tot[i], dec[i] = d1 * s0[i] + s1_, d0 * d1
        pre[i], pre_d[i] = jnp.zeros((HALF, 128), F32), jnp.ones((1, 128), F32)
        send_round(0, i)

    wo2_copies = [remote(vm["op2"], sc["wo2"].at[y], {"head": p}) for p in y_peers]
    for cp in wo2_copies:
        cp.start()
    both = dot3(n2, w2_late) * rms2
    gate, read = both[:, :128], both[:, 128:]
    read2 = split2(read)
    sc["rd"][...] = jnp.concatenate(read2, axis=1)
    pairs = dot3_short(read2, write_t2)
    cum_t = cum.T
    allowed = tri_r >= tri_c
    local = halves(vm["sk2"][...]) * inner
    first = iota((T, 128), 1) < 64
    xs, xr = sc["xs"], sc["xr"]
    x_copies = [[], []]
    for r in range(3):
        later = z // (1 << r) % 2
        for i in chunks:
            rounds[r][i].wait_recv()
            got, got_d = sc["br"][2 * r + i, 0:HALF], sc["br"][2 * r + i, HALF : HALF + 1]
            tot[i] = pick(later, dec[i] * got + tot[i], got_d * tot[i] + got)
            dec[i] = dec[i] * got_d
            if r < 2:
                send_round(r + 1, i)
            else:
                fill(xs.at[i], tot[i], dec[i])
                x_copies[i] = [
                    remote(xs.at[i], xr.at[i, x], {"seq": seq_of(xor(x, k, 2), z, c)})
                    for k in (2, 1, 3)
                ]
                for cp in x_copies[i]:
                    cp.start()
                xr[i, pl.ds(x, 1)] = xs[i][None]
            pre[i] = pick(later, pre_d[i] * got + pre[i], pre[i])
            pre_d[i] = pick(later, got_d * pre_d[i], pre_d[i])
        if r < 2:
            h = r
            diff = cum[:, 64 * h : 64 * h + 1] - cum_t[64 * h : 64 * h + 1, :]
            wts = jnp.where(allowed, jnp.exp(jnp.where(allowed, diff, 0.0)) * pairs, 0.0)
            local = local + dot3(wts, jnp.where(first if h == 0 else ~first, stepped, 0.0))
    sc["loc"][...] = local
    sc["gat"][...] = silu(gate)
    sc["cue"][...] = jnp.exp(cum)
    for cp in wo2_copies:
        cp.wait_recv()
    ks, kr = sc["ks"], sc["kr"]
    k_copies, mine = [], []
    for i in chunks:
        for cp in x_copies[i]:
            cp.wait_recv()
        row_in = jnp.zeros((HALF, 128), F32)
        for n in range(NX - 1):
            row_in = pick(as_int(x > n), xr[i, n, HALF : HALF + 1] * row_in + xr[i, n, 0:HALF], row_in)
        k0 = pre_d[i] * row_in + pre[i]
        k1 = d0 * k0 + s0[i]
        ks[i] = pick(c, k0, k1)
        k_copies.append(remote(ks.at[i], kr.at[i], other_core))
        k_copies[i].start()
        mine.append(pick(c, k1, k0))
    for cp in k_copies:
        cp.wait_recv()
    got = jnp.concatenate([kr[0], kr[1]], axis=0)
    mine = jnp.concatenate(mine, axis=0)
    carried = jnp.concatenate([pick(c, got, mine), pick(c, mine, got)], axis=0)
    ch, cl = split2(carried)
    chh = jnp.concatenate([ch, ch], axis=0)
    gs, gr = sc["gs"], sc["gr"]

    def finish(rows):
        rd = sc["rd"][rows, :]
        y2 = sc["loc"][rows, :] + (mm(rd, chh) + mm(rd[:, :128], cl)) * sc["cue"][rows, :]
        w = y2 * sc["gat"][rows, :]
        return w * head_scale(w) * vm["on2"][...]

    def rows_of(p):
        return pl.ds(pl.multiple_of(64 * p, 64), 64)

    far = y_peers[0]
    gf = sc["gf"]
    gf[...] = finish(rows_of(far))
    g_copies = [remote(gf, gr.at[y], {"head": far})]
    g_copies[0].start()
    gs[...] = finish(pl.ds(0, T))
    for p in y_peers[1:]:
        g_copies.append(remote(gs.at[rows_of(p)], gr.at[y], {"head": p}))
        g_copies[-1].start()
    wo2 = sc["wo2"]
    out = mir[rows_of(y), :] + dot3_short(gs[rows_of(y), :], wo2[y])
    for cp, p in zip(g_copies[1:] + g_copies[:1], y_peers[1:] + y_peers[:1]):
        cp.wait_recv()
        out = out + dot3_short(gr[p], wo2[p])
    out_ref[...] = out

    for cp in (
        log_copies + tab_copies + tok_copies + [tokm_copy] + wo1_copies + wo1_passed + wo2_copies + z_copies
        + e1 + rounds[0] + rounds[1] + rounds[2] + x_copies[0] + x_copies[1] + k_copies + g_copies
    ):
        cp.wait_send()


def per_device(*args):
    a = dict(zip(NAMES, args))
    for n in ("sp1", "sp2"):
        a[n] = a[n].T
    flat = [a[n].reshape(s) for n, s in zip(NAMES, SHAPES)]
    return pl.pallas_call(
        kernel,
        out_shape=jax.ShapeDtypeStruct((64, 256), F32),
        in_specs=[pl.BlockSpec(memory_space=pltpu.HBM)] * N_IN,
        out_specs=pl.BlockSpec(memory_space=pltpu.VMEM),
        scratch_shapes=[pltpu.VMEM(s, t) for s, t in zip(SHAPES, TYPES)]
        + [pltpu.VMEM(s, t) for _, s, t in SCRATCH]
        + [
            pltpu.SemaphoreType.DMA((N_IN + 1,)),
            pltpu.SemaphoreType.DMA((N_SEND,)),
            pltpu.SemaphoreType.DMA((N_SEND,)),
        ],
        compiler_params=pltpu.CompilerParams(
            collective_id=0, has_side_effects=True, vmem_limit_bytes=60 * 2**20
        ),
    )(*flat)


def solution(mesh):
    tokens = P(("rep", "seq"))
    layer = (P(), P(None, None, "head"), P(), P(None, "head")) + (P("head"),) * 4 + (P("head", None),)
    in_specs = (tokens, P(), P()) + layer + layer
    return jax.shard_map(
        per_device,
        mesh=mesh,
        in_specs=in_specs,
        out_specs=P(("rep", "seq", "head"), None),
        check_vma=False,
    )
```

```python
import jax
import jax.numpy as jnp
from jax import lax
from jax.experimental import pallas as pl
from jax.experimental.pallas import tpu as pltpu
from jax.sharding import PartitionSpec as P

F32, BF = jnp.float32, jnp.bfloat16
MESH = pl.DeviceIdType.MESH
EPS = 1e-05
NX, NZ, NC, NY = 4, 8, 2, 4
T = 256
V = 16


def mm(a, b):
    return lax.dot_general(a, b, (((1,), (0,)), ((), ())), preferred_element_type=F32)


def mmt(a, b):
    return lax.dot_general(a, b, (((1,), (1,)), ((), ())), preferred_element_type=F32)


def split2(a):
    hi = a.astype(BF)
    return hi, (a - hi.astype(F32)).astype(BF)


def split3(a):
    hi = a.astype(BF)
    rest = a - hi.astype(F32)
    mid = rest.astype(BF)
    return hi, mid, (rest - mid.astype(F32)).astype(BF)


def dot3(a, b, f=mm):
    ah, al = a if isinstance(a, tuple) else split2(a)
    bh, bl = b if isinstance(b, tuple) else split2(b)
    return f(ah, bh) + (f(ah, bl) + f(al, bh))


def dot3_short(a, b):
    ah, al = a if isinstance(a, tuple) else split2(a)
    bh, bl = b if isinstance(b, tuple) else split2(b)
    return mm(jnp.concatenate([ah, al], axis=1), jnp.concatenate([bh, bh], axis=0)) + mm(ah, bl)


def exact_left(a, b):
    h, l = split2(b)
    return mm(a, h) + mm(a, l)


def exact_right(a, b):
    h, m, l = split3(a)
    return mm(h, b) + (mm(m, b) + mm(l, b))


def iota(shape, dim):
    return lax.broadcasted_iota(jnp.int32, shape, dim)


def softplus(a):
    return jnp.maximum(a, 0.0) + jnp.log1p(jnp.exp(-jnp.abs(a)))


def silu(a):
    return a / (1.0 + jnp.exp(-a))


def rms(a, gain):
    return a * lax.rsqrt(jnp.mean(a * a, axis=-1, keepdims=True) + EPS) * gain


def xor(a, k, bits):
    out = a
    for i in range(bits):
        if k >> i & 1:
            out = out + (1 << i) * (1 - 2 * (a // (1 << i) % 2))
    return out


def pick(flag, a, b):
    return jnp.where(jnp.full(a.shape, flag, jnp.int32) > 0, a, b)


def as_int(cond):
    return jnp.where(cond, 1, 0)


def halves(pair):
    return jnp.where(iota((1, 128), 1) < 64, pair[:, 0:1], pair[:, 1:2])


def scan_rows(coef, decay, reverse):
    rows = iota(coef.shape, 0)
    k = 1
    while k < T:
        if reverse:
            inside = rows < T - k
            shifted_c, shifted_d = pltpu.roll(coef, T - k, 0), pltpu.roll(decay, T - k, 0)
        else:
            inside = rows >= k
            shifted_c, shifted_d = pltpu.roll(coef, k, 0), pltpu.roll(decay, k, 0)
        coef = coef + jnp.where(inside, decay * shifted_c, 0.0)
        decay = jnp.where(inside, decay * shifted_d, decay)
        k *= 2
    return coef, decay


NAMES = (
    "tok", "emb", "comp",
    "pn1", "ip1", "sm1", "sp1", "sb1", "ra1", "sk1", "on1", "op1",
    "pn2", "ip2", "sm2", "sp2", "sb2", "ra2", "sk2", "on2", "op2",
)
SHAPES = (
    (1, T), (V, 256), (1, 256),
    (1, 256), (512, 128), (512, 128), (2, 256), (1, 2), (1, 2), (1, 2), (1, 128), (128, 256),
    (1, 256), (512, 128), (512, 128), (2, 256), (1, 2), (1, 2), (1, 2), (1, 128), (128, 256),
)
TYPES = (jnp.int32, F32, jnp.int32) + (F32,) * 18
N_IN = len(NAMES)
TAB = 72
HALF = 32
MSG = HALF + 8

SCRATCH = (
    ("tokbuf", (8, 1, T), jnp.int32),
    ("tokr", (1, T), jnp.int32),
    ("tokm", (1, T), jnp.int32),
    ("lsend", (8, 128), F32),
    ("ltab", (NY, 8, 128), F32),
    ("tsend", (TAB, 128), F32),
    ("ytab", (NY, TAB, 128), F32),
    ("wo1", (NY, 128, 256), F32),
    ("wo1s", (128, 256), F32),
    ("wo2", (NY, 128, 256), F32),
    ("ztile", (8, 128), F32),
    ("zbuf", (NZ, 8, 128), F32),
    ("mir", (T, 256), F32),
    ("st", (128, 128), F32),
    ("e1s", (2, MSG, 128), F32),
    ("e1r", (2, MSG, 128), F32),
    ("bs", (6, MSG, 128), F32),
    ("br", (6, MSG, 128), F32),
    ("xs", (2, MSG, 128), F32),
    ("xr", (2, NX, MSG, 128), F32),
    ("ks", (2, HALF, 128), F32),
    ("kr", (2, HALF, 128), F32),
    ("rd", (T, 256), BF),
    ("loc", (T, 128), F32),
    ("gat", (T, 128), F32),
    ("cue", (T, 128), F32),
    ("gs", (T, 128), F32),
    ("gf", (64, 128), F32),
    ("gr", (NY, 64, 128), F32),
)
N_SEND = 72


def kernel(*refs):
    hbm = dict(zip(NAMES, refs[:N_IN]))
    out_ref = refs[N_IN]
    vm = dict(zip(NAMES, refs[N_IN + 1 :]))
    sc = {s[0]: r for s, r in zip(SCRATCH, refs[N_IN + 1 + N_IN :])}
    in_sem, send_sem, recv_sem, present = refs[-4:]

    seq, y = lax.axis_index("seq"), lax.axis_index("head")
    x, z, c = seq // (NZ * NC), seq // NC % NZ, seq % NC
    xc = x * NC + c
    xm, zm = NX - 1 - x, NZ - 1 - z

    def seq_of(xi, zi, ci):
        return (xi * NZ + zi) * NC + ci

    y_peers = [xor(y, k, 2) for k in (2, 1, 3)]
    xc_peers = [xor(xc, k, 3) for k in (4, 5, 2, 3, 6, 7, 1)]
    z_near = [xor(z, k, 3) for k in (4, 3, 2, 1)]
    z_far = [xor(z, k, 3) for k in (7, 6, 5)]

    barrier = pltpu.get_barrier_semaphore()

    def greet(where):
        pl.semaphore_signal(barrier, inc=1, device_id=where, device_id_type=MESH)

    for p in z_near:
        greet({"seq": seq_of(x, p, c)})
    for p in xc_peers:
        greet({"seq": seq_of(p // NC, z, p % NC)})
    for p in y_peers:
        greet({"head": p})

    loads = {n: pltpu.make_async_copy(hbm[n], vm[n], in_sem.at[i]) for i, n in enumerate(NAMES)}
    first_loads = ("tok", "emb", "pn1", "sp1", "sb1", "ra1")
    for n in first_loads:
        loads[n].start()
    own_tok = pltpu.make_async_copy(hbm["tok"], sc["tokbuf"].at[xc], in_sem.at[N_IN])
    own_tok.start()
    other_loads = tuple(n for n in NAMES if n not in first_loads)
    for n in other_loads:
        loads[n].start()

    used = [0]

    def remote(src, dst, where):
        i = used[0]
        used[0] += 1
        return pltpu.make_async_remote_copy(
            src_ref=src, dst_ref=dst, send_sem=send_sem.at[i], recv_sem=recv_sem.at[i],
            device_id=where, device_id_type=MESH,
        )

    for n in first_loads:
        loads[n].wait()

    lane = iota((1, 128), 1)
    emb = vm["emb"][...]
    normed = rms(emb, vm["pn1"][...])
    sp, sb, ra = vm["sp1"][...], vm["sb1"][...], vm["ra1"][...]
    even = iota((8, 128), 0) % 2 == 0
    sp_r = jnp.where(iota((8, 256), 0) % 2 == 0, sp[0:1], sp[1:2])
    log_r = -jnp.where(even, ra[:, 0:1], ra[:, 1:2]) * softplus(
        dot3(sp_r, jnp.concatenate([normed] * 8, axis=0), mmt)
        + jnp.where(even, sb[:, 0:1], sb[:, 1:2])
    )
    lsend, tsend = sc["lsend"], sc["tsend"]
    lsend[...] = log_r

    pl.semaphore_wait(barrier, 14)
    pl.semaphore_signal(
        present, inc=1, device_id={"seq": seq_of(x, z_near[0], c)}, device_id_type=MESH
    )
    ltab, ytab, tokbuf = sc["ltab"], sc["ytab"], sc["tokbuf"]
    log_copies = [remote(lsend, ltab.at[y], {"head": p}) for p in y_peers]
    tok_copies = [
        remote(vm["tok"], tokbuf.at[xc], {"seq": seq_of(p // NC, z, p % NC)}) for p in xc_peers
    ]
    for cp in log_copies + tok_copies:
        cp.start()
    ltab[pl.ds(y, 1)] = log_r[None]

    own_tok.wait()
    for n in other_loads:
        loads[n].wait()
    w1 = vm["ip1"]
    gate_w, inner_w = w1[pl.ds(0, 256, stride=2), :], w1[pl.ds(1, 256, stride=2), :]
    s1 = vm["sm1"]
    write_w, read_w = s1[pl.ds(0, 256, stride=2), :], s1[pl.ds(1, 256, stride=2), :]
    normed2 = split2(normed)
    table = dot3(normed2, jnp.concatenate([gate_w, inner_w, write_w, read_w], axis=1))
    gate_t, inner_t, write_t, read_t = (table[:, 128 * i : 128 * (i + 1)] for i in range(4))
    sk = vm["sk1"][...]
    r128 = iota((128, 256), 0)
    sp_p = jnp.where(r128 < 64, sp[0:1], sp[1:2])
    sp_alt = jnp.where(r128 // 16 % 2 == 0, sp[0:1], sp[1:2])
    logits = dot3(normed2, jnp.concatenate([sp_p, sp_alt], axis=0), mmt)
    step_p = softplus(logits[:, :128] + halves(sb))
    alt = lane // 16 % 2 == 0
    log_alt = -jnp.where(alt, ra[:, 0:1], ra[:, 1:2]) * softplus(
        logits[:, 128:] + jnp.where(alt, sb[:, 0:1], sb[:, 1:2])
    )
    tsend[0:16] = step_p * inner_t
    tsend[16:32] = halves(sk) * inner_t
    tsend[32:48] = silu(gate_t)
    tsend[48:64] = log_alt
    tsend[64:72] = jnp.broadcast_to(vm["on1"][...], (8, 128))
    tab_copies = [remote(tsend, ytab.at[y], {"head": p}) for p in y_peers]
    for cp in tab_copies:
        cp.start()
    g_tab = dot3(read_t, jnp.concatenate([write_t] * 8, axis=0), mmt)
    ytab[pl.ds(y, 1)] = tsend[...][None]
    sc["wo2"][pl.ds(y, 1)] = vm["op2"][...][None]

    tri_r, tri_c = iota((256, 256), 0), iota((256, 256), 1)
    one = jnp.ones((), F32)

    def mask_bf(cond):
        return jnp.where(cond, one, 0.0 * one).astype(BF)

    perm = mask_bf(vm["comp"][...] == tri_r)
    wo1s = sc["wo1s"]
    wo1s[...] = exact_right(vm["op1"][...], perm)
    sc["wo1"][pl.ds(y, 1)] = wo1s[...][None]
    w2, s2 = vm["ip2"], vm["sm2"]
    gain = jnp.broadcast_to(vm["pn2"][...], (128, 256)).T
    w2_early = split2(
        jnp.concatenate([w2[pl.ds(1, 256, stride=2), :] * gain, s2[pl.ds(0, 256, stride=2), :] * gain], axis=1)
    )
    w2_late = split2(
        jnp.concatenate([w2[pl.ds(0, 256, stride=2), :] * gain, s2[pl.ds(1, 256, stride=2), :] * gain], axis=1)
    )
    sp2 = vm["sp2"][...] * vm["pn2"][...]
    sp2_p = split2(jnp.where(r128 < 64, sp2[0:1], sp2[1:2]))
    emb_p = mm(jnp.concatenate(split3(emb), axis=0), perm).astype(BF)

    for cp in tok_copies:
        cp.wait_recv()
    mirror_relay = remote(tokbuf.at[xm * NC + 1 - c], sc["tokr"], {"seq": seq_of(x, z_near[0], c)})
    mirror_relay.start()
    for cp in log_copies:
        cp.wait_recv()
    core_rows = pl.ds(pl.multiple_of(64 * c, 64), 64)
    wo1_copies = [
        remote(wo1s.at[core_rows], sc["wo1"].at[y, core_rows], {"head": p}) for p in y_peers
    ]
    for cp in wo1_copies:
        cp.start()
    r16 = iota((V, T), 0)
    onehot = jnp.concatenate([as_int(tokbuf[b] == r16) for b in range(8)], axis=0)
    onehot = onehot.astype(F32).astype(BF)
    counts = mm(
        onehot,
        jnp.concatenate(
            [mask_bf(tri_r > tri_c), mask_bf(tri_r < tri_c), jnp.ones((256, 128), BF)], axis=1
        ),
    ).astype(BF)
    row8 = iota((8, 128), 0)
    log_hv = ltab[0]
    for i in range(1, NY):
        log_hv = jnp.where(row8 // 2 == i, ltab[i], log_hv)
    r64, l64 = iota((64, 128), 0), iota((64, 128), 1)
    log_bd = jnp.where(r64 // 8 == l64 // 16, jnp.concatenate([log_hv] * 8, axis=0), 0.0)
    cums = mm(
        jnp.concatenate(split2(log_bd), axis=1), jnp.concatenate([counts, counts], axis=0)
    )
    weight = jnp.exp(cums[:, :512])
    weight = jnp.concatenate([weight[:, :256], weight[:, 256:]], axis=0)
    wh, wl = split2(weight)
    sums = mmt(wh, onehot) + mmt(wl, onehot)
    r2, l2 = iota((128, 128), 0), iota((128, 128), 1)
    sums = jnp.where(r2 // 8 % 8 == l2 // 16, sums, 0.0)
    for shift in (64, 32, 16):
        sums = sums + pltpu.roll(sums, shift, 1)
    sums = jnp.where(r2 % 8 == l2 // 16, sums, 0.0)
    totals = jnp.where(r64 % 8 == l64 // 16, cums[:, 512:], 0.0)

    def fold(a, i):
        return jnp.sum(a[8 * i : 8 * i + 8], axis=0, keepdims=True)

    cf = [fold(sums, b) for b in range(8)]
    cb = [fold(sums, 8 + b) for b in range(8)]
    ld = [fold(totals, b) for b in range(8)]
    cf_pair = [jnp.exp(ld[2 * i + 1]) * cf[2 * i] + cf[2 * i + 1] for i in range(NX)]
    cb_pair = [jnp.exp(ld[2 * i]) * cb[2 * i + 1] + cb[2 * i] for i in range(NX)]
    ld_pair = [ld[2 * i] + ld[2 * i + 1] for i in range(NX)]
    rows = [pick(as_int(xm >= i), cf_pair[i], cb_pair[i]) for i in range(NX)]
    own_b, sib, sib_ld, packed = cb_pair[0], cf[0], ld[0], ld_pair[0]
    for i in range(NX):
        here = as_int(xm == i)
        own_b = pick(here, cb_pair[i], own_b)
        sib = pick(here, pick(c, cb[2 * i + 1], cf[2 * i]), sib)
        sib_ld = pick(here, pick(c, ld[2 * i + 1], ld[2 * i]), sib_ld)
        packed = jnp.where(lane % 16 == i, ld_pair[i], packed)
    tile = jnp.concatenate(rows + [own_b, packed, sib, sib_ld], axis=0)
    ztile, zbuf = sc["ztile"], sc["zbuf"]
    ztile[...] = tile
    z_copies = [remote(ztile, zbuf.at[z], {"seq": seq_of(x, p, c)}) for p in z_near]
    for cp in z_copies:
        cp.start()
    zbuf[pl.ds(z, 1)] = tile[None]

    def lanes_of(a, b):
        return jnp.concatenate([ytab[i, a:b] for i in range(NY)], axis=1)

    for cp in tab_copies:
        cp.wait_recv()
    row16 = iota((V, 128), 0)
    l16 = iota((V, 128), 1)
    log_t = ytab[0, 48:64]
    for i in range(1, NY):
        log_t = jnp.where(l16 // 32 == i, ytab[i, 48:64], log_t)
    eye_t = jnp.where(row16 == l16 % 16, 1.0, 0.0)
    tables = jnp.concatenate([lanes_of(32, 48), lanes_of(16, 32), g_tab, jnp.exp(log_t), eye_t], axis=1)
    tables = jnp.concatenate([jnp.concatenate(split3(tables), axis=0), emb_p], axis=1)
    inner_rep = jnp.concatenate([lanes_of(0, 16)] * 8, axis=0)
    bd = iota((128, 512), 0) // 16 == iota((128, 512), 1) // 64
    x_bd = split2(jnp.where(bd, inner_rep, 0.0))
    outnorm_all = lanes_of(64, 65)
    pl.semaphore_wait(present, 1)
    far_copies = [remote(ztile, zbuf.at[z], {"seq": seq_of(x, p, c)}) for p in z_far]
    for cp in far_copies:
        cp.start()
    z_copies += far_copies
    mirror_relay.wait_recv()
    tokm_copy = remote(sc["tokr"], sc["tokm"], {"seq": seq_of(x, z_near[1], c)})
    tokm_copy.start()
    other_core = {"seq": seq_of(x, z, 1 - c)}
    wo1_passed = []
    for cp, p in zip(wo1_copies, y_peers):
        cp.wait_recv()
        half = sc["wo1"].at[p, core_rows]
        wo1_passed.append(remote(half, half, other_core))
        wo1_passed[-1].start()
    tokm_copy.wait_recv()
    hot_m = as_int(sc["tokm"][...] == r16).astype(F32).astype(BF)
    rev = mask_bf(tri_r + tri_c == T - 1)
    hot_rev = mmt(rev, jnp.concatenate([hot_m] * 3, axis=0)).astype(BF)
    taken = mm(hot_rev, tables)
    silu_g, skip_x = taken[:, :512], taken[:, 512:1024]
    g_row, decay, hot = taken[:, 1024:1152], taken[:, 1152:1280], taken[:, 1280:1408]
    embedded = taken[:, 1408:]
    up_c, up_p = scan_rows(hot, decay, False)
    dn_c, dn_p = scan_rows(hot, decay, True)

    for cp in z_copies:
        cp.wait_recv()
    ls, lr = iota((128, 512), 1), iota((128, 512), 0)
    spread = mask_bf((lr // 16 == ls % 128 // 16) & (lr % 16 == ls // 128))
    ld_all = mm(
        jnp.concatenate(split2(zbuf[:, 5, :]), axis=1), jnp.concatenate([spread, spread], axis=0)
    )
    ld_all = jnp.concatenate([ld_all[:, 128 * i : 128 * i + 128] for i in range(NX)], axis=0)
    qm = xm * NZ + zm
    q, q2 = iota((32, 32), 0), iota((32, 32), 1)
    between = ((q2 > q) & (q2 < qm)) | ((q2 < q) & (q2 > qm))
    share = jnp.exp(exact_left(mask_bf(between), ld_all))
    zrow = iota((8, 128), 0)
    coefs = jnp.concatenate(
        [
            jnp.where((zrow > zm) & (jnp.full((8, 128), xm, jnp.int32) == i), zbuf[:, 4, :], zbuf[:, i, :])
            for i in range(NX)
        ],
        axis=0,
    )
    terms = share * coefs
    qrow = iota((32, 128), 0)
    carry_f = jnp.sum(jnp.where(qrow < qm, terms, 0.0), axis=0, keepdims=True)
    carry_b = jnp.sum(jnp.where(qrow > qm, terms, 0.0), axis=0, keepdims=True)
    at_m = zbuf[pl.ds(zm, 1)].reshape(8, 128)
    sib, sib_d = at_m[6:7], jnp.exp(at_m[7:8])
    carry_f = pick(c, carry_f, sib_d * carry_f + sib)
    carry_b = pick(c, sib_d * carry_b + sib, carry_b)
    coef = jnp.concatenate([up_c + up_p * carry_b, dn_c + dn_p * carry_f], axis=0)
    coef = coef * jnp.concatenate([g_row] * 2, axis=0)
    ssm = dot3_short(coef, x_bd)

    same_head = jnp.where(r2 // 64 == l2 // 64, 1.0 / 64, 0.0).astype(BF)
    same_head = jnp.concatenate([same_head, same_head], axis=0)

    def head_scale(w):
        parts = []
        for i in range(w.shape[1] // 128):
            parts.append(mm(jnp.concatenate(split2(w[:, 128 * i : 128 * i + 128] ** 2), axis=1), same_head))
        sq = parts[0] if len(parts) == 1 else jnp.concatenate(parts, axis=1)
        return lax.rsqrt(sq + EPS)

    for cp in wo1_passed:
        cp.wait_recv()
    wo1_p = split2(sc["wo1"][...].reshape(512, 256))
    w_up = (ssm[:T] + skip_x) * silu_g
    w_dn = (ssm[T:] + skip_x) * silu_g
    mixed = (w_up * head_scale(w_up) + w_dn * head_scale(w_dn)) * outnorm_all
    mirrored = embedded + dot3(mixed, wo1_p)
    mir = sc["mir"]
    mir[...] = mirrored

    n2 = split2(mirrored)
    rms2 = lax.rsqrt(jnp.mean(mirrored * mirrored, axis=-1, keepdims=True) + EPS)
    step = softplus(dot3(n2, sp2_p, mmt) * rms2 + halves(vm["sb2"][...]))
    both = dot3(n2, w2_early) * rms2
    inner, write = both[:, :128], both[:, 128:]
    cum = exact_left(mask_bf(tri_r >= tri_c), -halves(vm["ra2"][...]) * step)
    end = cum[T - 1 : T]
    stepped = inner * step
    write_t2 = split2(write.T)
    state = dot3(write_t2, stepped * jnp.exp(end - cum))
    own_d = jnp.exp(end)
    st, e1s, e1r = sc["st"], sc["e1s"], sc["e1r"]
    st[...] = state
    chunks = range(2)

    def fill(buf, rows, decay):
        buf[0:HALF] = rows
        buf[HALF:MSG] = jnp.broadcast_to(decay, (8, 128))

    def part(core, i):
        return st[pl.ds(pl.multiple_of(64 * core + HALF * i, HALF), HALF), :]

    e1 = []
    for i in chunks:
        fill(e1s.at[i], part(1 - c, i), own_d)
        e1.append(remote(e1s.at[i], e1r.at[i], other_core))
        e1[i].start()

    s0, tot, dec, pre, pre_d = [None] * 2, [None] * 2, [None] * 2, [None] * 2, [None] * 2
    rounds = [[None] * 2 for _ in range(3)]

    def send_round(r, i):
        bs, br = sc["bs"].at[2 * r + i], sc["br"].at[2 * r + i]
        fill(bs, tot[i], dec[i])
        rounds[r][i] = remote(bs, br, {"seq": seq_of(x, xor(z, 1 << r, 3), c)})
        rounds[r][i].start()

    for i in chunks:
        own = part(c, i)
        e1[i].wait_recv()
        got, got_d = e1r[i, 0:HALF], e1r[i, HALF : HALF + 1]
        s0[i], s1_ = pick(c, got, own), pick(c, own, got)
        d0, d1 = pick(c, got_d, own_d), pick(c, own_d, got_d)
        tot[i], dec[i] = d1 * s0[i] + s1_, d0 * d1
        pre[i], pre_d[i] = jnp.zeros((HALF, 128), F32), jnp.ones((1, 128), F32)
        send_round(0, i)

    wo2_copies = [remote(vm["op2"], sc["wo2"].at[y], {"head": p}) for p in y_peers]
    for cp in wo2_copies:
        cp.start()
    both = dot3(n2, w2_late) * rms2
    gate, read = both[:, :128], both[:, 128:]
    read2 = split2(read)
    sc["rd"][...] = jnp.concatenate(read2, axis=1)
    pairs = dot3_short(read2, write_t2)
    cum_t = cum.T
    allowed = tri_r >= tri_c
    local = halves(vm["sk2"][...]) * inner
    first = iota((T, 128), 1) < 64
    xs, xr = sc["xs"], sc["xr"]
    x_copies = [[], []]
    for r in range(3):
        later = z // (1 << r) % 2
        for i in chunks:
            rounds[r][i].wait_recv()
            got, got_d = sc["br"][2 * r + i, 0:HALF], sc["br"][2 * r + i, HALF : HALF + 1]
            tot[i] = pick(later, dec[i] * got + tot[i], got_d * tot[i] + got)
            dec[i] = dec[i] * got_d
            if r < 2:
                send_round(r + 1, i)
            else:
                fill(xs.at[i], tot[i], dec[i])
                x_copies[i] = [
                    remote(xs.at[i], xr.at[i, x], {"seq": seq_of(xor(x, k, 2), z, c)})
                    for k in (2, 1, 3)
                ]
                for cp in x_copies[i]:
                    cp.start()
                xr[i, pl.ds(x, 1)] = xs[i][None]
            pre[i] = pick(later, pre_d[i] * got + pre[i], pre[i])
            pre_d[i] = pick(later, got_d * pre_d[i], pre_d[i])
        if r < 2:
            h = r
            diff = cum[:, 64 * h : 64 * h + 1] - cum_t[64 * h : 64 * h + 1, :]
            wts = jnp.where(allowed, jnp.exp(jnp.where(allowed, diff, 0.0)) * pairs, 0.0)
            local = local + dot3(wts, jnp.where(first if h == 0 else ~first, stepped, 0.0))
    sc["loc"][...] = local
    sc["gat"][...] = silu(gate)
    sc["cue"][...] = jnp.exp(cum)
    for cp in wo2_copies:
        cp.wait_recv()
    ks, kr = sc["ks"], sc["kr"]
    k_copies, mine = [], []
    for i in chunks:
        for cp in x_copies[i]:
            cp.wait_recv()
        row_in = jnp.zeros((HALF, 128), F32)
        for n in range(NX - 1):
            row_in = pick(as_int(x > n), xr[i, n, HALF : HALF + 1] * row_in + xr[i, n, 0:HALF], row_in)
        k0 = pre_d[i] * row_in + pre[i]
        k1 = d0 * k0 + s0[i]
        ks[i] = pick(c, k0, k1)
        k_copies.append(remote(ks.at[i], kr.at[i], other_core))
        k_copies[i].start()
        mine.append(pick(c, k1, k0))
    for cp in k_copies:
        cp.wait_recv()
    got = jnp.concatenate([kr[0], kr[1]], axis=0)
    mine = jnp.concatenate(mine, axis=0)
    carried = jnp.concatenate([pick(c, got, mine), pick(c, mine, got)], axis=0)
    ch, cl = split2(carried)
    chh = jnp.concatenate([ch, ch], axis=0)
    gs, gr = sc["gs"], sc["gr"]

    def finish(rows):
        rd = sc["rd"][rows, :]
        y2 = sc["loc"][rows, :] + (mm(rd, chh) + mm(rd[:, :128], cl)) * sc["cue"][rows, :]
        w = y2 * sc["gat"][rows, :]
        return w * head_scale(w) * vm["on2"][...]

    def rows_of(p):
        return pl.ds(pl.multiple_of(64 * p, 64), 64)

    far = y_peers[0]
    gf = sc["gf"]
    gf[...] = finish(rows_of(far))
    g_copies = [remote(gf, gr.at[y], {"head": far})]
    g_copies[0].start()
    gs[...] = finish(pl.ds(0, T))
    for p in y_peers[1:]:
        g_copies.append(remote(gs.at[rows_of(p)], gr.at[y], {"head": p}))
        g_copies[-1].start()
    wo2 = sc["wo2"]
    out = mir[rows_of(y), :] + dot3_short(gs[rows_of(y), :], wo2[y])
    for cp, p in zip(g_copies[1:] + g_copies[:1], y_peers[1:] + y_peers[:1]):
        cp.wait_recv()
        out = out + dot3_short(gr[p], wo2[p])
    out_ref[...] = out

    for cp in (
        log_copies + tab_copies + tok_copies + [mirror_relay, tokm_copy] + wo1_copies + wo1_passed + wo2_copies + z_copies
        + e1 + rounds[0] + rounds[1] + rounds[2] + x_copies[0] + x_copies[1] + k_copies + g_copies
    ):
        cp.wait_send()


def per_device(*args):
    a = dict(zip(NAMES, args))
    for n in ("sp1", "sp2"):
        a[n] = a[n].T
    flat = [a[n].reshape(s) for n, s in zip(NAMES, SHAPES)]
    return pl.pallas_call(
        kernel,
        out_shape=jax.ShapeDtypeStruct((64, 256), F32),
        in_specs=[pl.BlockSpec(memory_space=pltpu.HBM)] * N_IN,
        out_specs=pl.BlockSpec(memory_space=pltpu.VMEM),
        scratch_shapes=[pltpu.VMEM(s, t) for s, t in zip(SHAPES, TYPES)]
        + [pltpu.VMEM(s, t) for _, s, t in SCRATCH]
        + [
            pltpu.SemaphoreType.DMA((N_IN + 1,)),
            pltpu.SemaphoreType.DMA((N_SEND,)),
            pltpu.SemaphoreType.DMA((N_SEND,)),
            pltpu.SemaphoreType.REGULAR,
        ],
        compiler_params=pltpu.CompilerParams(
            collective_id=0, has_side_effects=True, vmem_limit_bytes=60 * 2**20
        ),
    )(*flat)


def solution(mesh):
    tokens = P(("rep", "seq"))
    layer = (P(), P(None, None, "head"), P(), P(None, "head")) + (P("head"),) * 4 + (P("head", None),)
    in_specs = (tokens, P(), P()) + layer + layer
    return jax.shard_map(
        per_device,
        mesh=mesh,
        in_specs=in_specs,
        out_specs=P(("rep", "seq", "head"), None),
        check_vma=False,
    )
```

```python
import jax
import jax.numpy as jnp
from jax import lax
from jax.experimental import pallas as pl
from jax.experimental.pallas import tpu as pltpu
from jax.sharding import PartitionSpec as P

F32, BF = jnp.float32, jnp.bfloat16
MESH = pl.DeviceIdType.MESH
EPS = 1e-05
NX, NZ, NC, NY = 4, 8, 2, 4
T = 256
V = 16


def mm(a, b):
    return lax.dot_general(a, b, (((1,), (0,)), ((), ())), preferred_element_type=F32)


def mmt(a, b):
    return lax.dot_general(a, b, (((1,), (1,)), ((), ())), preferred_element_type=F32)


def split2(a):
    hi = a.astype(BF)
    return hi, (a - hi.astype(F32)).astype(BF)


def split3(a):
    hi = a.astype(BF)
    rest = a - hi.astype(F32)
    mid = rest.astype(BF)
    return hi, mid, (rest - mid.astype(F32)).astype(BF)


def dot3(a, b, f=mm):
    ah, al = a if isinstance(a, tuple) else split2(a)
    bh, bl = b if isinstance(b, tuple) else split2(b)
    return f(ah, bh) + (f(ah, bl) + f(al, bh))


def dot3_short(a, b):
    ah, al = a if isinstance(a, tuple) else split2(a)
    bh, bl = b if isinstance(b, tuple) else split2(b)
    return mm(jnp.concatenate([ah, al], axis=1), jnp.concatenate([bh, bh], axis=0)) + mm(ah, bl)


def exact_left(a, b):
    h, l = split2(b)
    return mm(a, h) + mm(a, l)


def exact_right(a, b):
    h, m, l = split3(a)
    return mm(h, b) + (mm(m, b) + mm(l, b))


def iota(shape, dim):
    return lax.broadcasted_iota(jnp.int32, shape, dim)


def softplus(a):
    return jnp.maximum(a, 0.0) + jnp.log1p(jnp.exp(-jnp.abs(a)))


def silu(a):
    return a / (1.0 + jnp.exp(-a))


def rms(a, gain):
    return a * lax.rsqrt(jnp.mean(a * a, axis=-1, keepdims=True) + EPS) * gain


def xor(a, k, bits):
    out = a
    for i in range(bits):
        if k >> i & 1:
            out = out + (1 << i) * (1 - 2 * (a // (1 << i) % 2))
    return out


def pick(flag, a, b):
    return jnp.where(jnp.full(a.shape, flag, jnp.int32) > 0, a, b)


def as_int(cond):
    return jnp.where(cond, 1, 0)


def halves(pair):
    return jnp.where(iota((1, 128), 1) < 64, pair[:, 0:1], pair[:, 1:2])


def scan_rows(coef, decay, reverse):
    rows = iota(coef.shape, 0)
    k = 1
    while k < T:
        if reverse:
            inside = rows < T - k
            shifted_c, shifted_d = pltpu.roll(coef, T - k, 0), pltpu.roll(decay, T - k, 0)
        else:
            inside = rows >= k
            shifted_c, shifted_d = pltpu.roll(coef, k, 0), pltpu.roll(decay, k, 0)
        coef = coef + jnp.where(inside, decay * shifted_c, 0.0)
        decay = jnp.where(inside, decay * shifted_d, decay)
        k *= 2
    return coef, decay


NAMES = (
    "tok", "emb", "comp",
    "pn1", "ip1", "sm1", "sp1", "sb1", "ra1", "sk1", "on1", "op1",
    "pn2", "ip2", "sm2", "sp2", "sb2", "ra2", "sk2", "on2", "op2",
)
SHAPES = (
    (1, T), (V, 256), (1, 256),
    (1, 256), (512, 128), (512, 128), (2, 256), (1, 2), (1, 2), (1, 2), (1, 128), (128, 256),
    (1, 256), (512, 128), (512, 128), (2, 256), (1, 2), (1, 2), (1, 2), (1, 128), (128, 256),
)
TYPES = (jnp.int32, F32, jnp.int32) + (F32,) * 18
N_IN = len(NAMES)
TAB = 72
HALF = 32
MSG = HALF + 8

SCRATCH = (
    ("tokbuf", (8, 1, T), jnp.int32),
    ("tokm", (1, T), jnp.int32),
    ("lsend", (8, 128), F32),
    ("ltab", (NY, 8, 128), F32),
    ("tsend", (TAB, 128), F32),
    ("ytab", (NY, TAB, 128), F32),
    ("wo1", (NY, 128, 256), F32),
    ("wo1s", (128, 256), F32),
    ("wo2", (NY, 128, 256), F32),
    ("ztile", (8, 128), F32),
    ("zbuf", (NZ, 8, 128), F32),
    ("mir", (T, 256), F32),
    ("st", (128, 128), F32),
    ("e1s", (2, MSG, 128), F32),
    ("e1o", (2, MSG, 128), F32),
    ("e1r", (2, MSG, 128), F32),
    ("n1r", (NC, 2, MSG, 128), F32),
    ("bs", (6, MSG, 128), F32),
    ("br", (6, MSG, 128), F32),
    ("xs", (2, MSG, 128), F32),
    ("xr", (2, NX, MSG, 128), F32),
    ("ks", (2, HALF, 128), F32),
    ("kr", (2, HALF, 128), F32),
    ("rd", (T, 256), BF),
    ("loc", (T, 128), F32),
    ("gat", (T, 128), F32),
    ("cue", (T, 128), F32),
    ("gs", (T, 128), F32),
    ("gf", (64, 128), F32),
    ("gr", (NY, 64, 128), F32),
)
N_SEND = 72


def kernel(*refs):
    hbm = dict(zip(NAMES, refs[:N_IN]))
    out_ref = refs[N_IN]
    vm = dict(zip(NAMES, refs[N_IN + 1 :]))
    sc = {s[0]: r for s, r in zip(SCRATCH, refs[N_IN + 1 + N_IN :])}
    in_sem, send_sem, recv_sem, present = refs[-4:]

    seq, y = lax.axis_index("seq"), lax.axis_index("head")
    x, z, c = seq // (NZ * NC), seq // NC % NZ, seq % NC
    xc = x * NC + c
    xm, zm = NX - 1 - x, NZ - 1 - z

    def seq_of(xi, zi, ci):
        return (xi * NZ + zi) * NC + ci

    y_peers = [xor(y, k, 2) for k in (2, 1, 3)]
    xc_peers = [xor(xc, k, 3) for k in (4, 5, 2, 3, 6, 7, 1)]
    z_near = [xor(z, k, 3) for k in (4, 3, 2, 1)]
    z_far = [xor(z, k, 3) for k in (7, 6, 5)]

    barrier = pltpu.get_barrier_semaphore()

    def greet(where):
        pl.semaphore_signal(barrier, inc=1, device_id=where, device_id_type=MESH)

    for p in z_near:
        greet({"seq": seq_of(x, p, c)})
    for p in xc_peers:
        greet({"seq": seq_of(p // NC, z, p % NC)})
    for p in y_peers:
        greet({"head": p})

    loads = {n: pltpu.make_async_copy(hbm[n], vm[n], in_sem.at[i]) for i, n in enumerate(NAMES)}
    first_loads = ("tok", "emb", "pn1", "sp1", "sb1", "ra1")
    for n in first_loads:
        loads[n].start()
    own_tok = pltpu.make_async_copy(hbm["tok"], sc["tokbuf"].at[xc], in_sem.at[N_IN])
    own_tok.start()
    other_loads = tuple(n for n in NAMES if n not in first_loads)
    for n in other_loads:
        loads[n].start()

    used = [0]

    def remote(src, dst, where):
        i = used[0]
        used[0] += 1
        return pltpu.make_async_remote_copy(
            src_ref=src, dst_ref=dst, send_sem=send_sem.at[i], recv_sem=recv_sem.at[i],
            device_id=where, device_id_type=MESH,
        )

    for n in first_loads:
        loads[n].wait()

    lane = iota((1, 128), 1)
    emb = vm["emb"][...]
    normed = rms(emb, vm["pn1"][...])
    sp, sb, ra = vm["sp1"][...], vm["sb1"][...], vm["ra1"][...]
    even = iota((8, 128), 0) % 2 == 0
    sp_r = jnp.where(iota((8, 256), 0) % 2 == 0, sp[0:1], sp[1:2])
    log_r = -jnp.where(even, ra[:, 0:1], ra[:, 1:2]) * softplus(
        dot3(sp_r, jnp.concatenate([normed] * 8, axis=0), mmt)
        + jnp.where(even, sb[:, 0:1], sb[:, 1:2])
    )
    lsend, tsend = sc["lsend"], sc["tsend"]
    lsend[...] = log_r

    pl.semaphore_wait(barrier, 14)
    pl.semaphore_signal(
        present, inc=1, device_id={"seq": seq_of(x, z_near[0], c)}, device_id_type=MESH
    )
    ltab, ytab, tokbuf = sc["ltab"], sc["ytab"], sc["tokbuf"]
    log_copies = [remote(lsend, ltab.at[y], {"head": p}) for p in y_peers]
    tok_copies = [
        remote(vm["tok"], tokbuf.at[xc], {"seq": seq_of(p // NC, z, p % NC)}) for p in xc_peers
    ]
    for cp in log_copies + tok_copies:
        cp.start()
    ltab[pl.ds(y, 1)] = log_r[None]

    own_tok.wait()
    for n in other_loads:
        loads[n].wait()
    w1 = vm["ip1"]
    gate_w, inner_w = w1[pl.ds(0, 256, stride=2), :], w1[pl.ds(1, 256, stride=2), :]
    s1 = vm["sm1"]
    write_w, read_w = s1[pl.ds(0, 256, stride=2), :], s1[pl.ds(1, 256, stride=2), :]
    normed2 = split2(normed)
    table = dot3(normed2, jnp.concatenate([gate_w, inner_w, write_w, read_w], axis=1))
    gate_t, inner_t, write_t, read_t = (table[:, 128 * i : 128 * (i + 1)] for i in range(4))
    sk = vm["sk1"][...]
    r128 = iota((128, 256), 0)
    sp_p = jnp.where(r128 < 64, sp[0:1], sp[1:2])
    sp_alt = jnp.where(r128 // 16 % 2 == 0, sp[0:1], sp[1:2])
    logits = dot3(normed2, jnp.concatenate([sp_p, sp_alt], axis=0), mmt)
    step_p = softplus(logits[:, :128] + halves(sb))
    alt = lane // 16 % 2 == 0
    log_alt = -jnp.where(alt, ra[:, 0:1], ra[:, 1:2]) * softplus(
        logits[:, 128:] + jnp.where(alt, sb[:, 0:1], sb[:, 1:2])
    )
    tsend[0:16] = step_p * inner_t
    tsend[16:32] = halves(sk) * inner_t
    tsend[32:48] = silu(gate_t)
    tsend[48:64] = log_alt
    tsend[64:72] = jnp.broadcast_to(vm["on1"][...], (8, 128))
    tab_copies = [remote(tsend, ytab.at[y], {"head": p}) for p in y_peers]
    for cp in tab_copies:
        cp.start()
    g_tab = dot3(read_t, jnp.concatenate([write_t] * 8, axis=0), mmt)
    ytab[pl.ds(y, 1)] = tsend[...][None]
    sc["wo2"][pl.ds(y, 1)] = vm["op2"][...][None]

    tri_r, tri_c = iota((256, 256), 0), iota((256, 256), 1)
    one = jnp.ones((), F32)

    def mask_bf(cond):
        return jnp.where(cond, one, 0.0 * one).astype(BF)

    perm = mask_bf(vm["comp"][...] == tri_r)
    wo1s = sc["wo1s"]
    wo1s[...] = exact_right(vm["op1"][...], perm)
    sc["wo1"][pl.ds(y, 1)] = wo1s[...][None]
    w2, s2 = vm["ip2"], vm["sm2"]
    gain = jnp.broadcast_to(vm["pn2"][...], (128, 256)).T
    w2_early = split2(
        jnp.concatenate([w2[pl.ds(1, 256, stride=2), :] * gain, s2[pl.ds(0, 256, stride=2), :] * gain], axis=1)
    )
    w2_late = split2(
        jnp.concatenate([w2[pl.ds(0, 256, stride=2), :] * gain, s2[pl.ds(1, 256, stride=2), :] * gain], axis=1)
    )
    sp2 = vm["sp2"][...] * vm["pn2"][...]
    sp2_p = split2(jnp.where(r128 < 64, sp2[0:1], sp2[1:2]))
    emb_p = mm(jnp.concatenate(split3(emb), axis=0), perm).astype(BF)

    core_rows = pl.ds(pl.multiple_of(64 * c, 64), 64)
    wo1_copies = [
        remote(wo1s.at[core_rows], sc["wo1"].at[y, core_rows], {"head": p}) for p in y_peers
    ]
    for cp in wo1_copies:
        cp.start()
    for cp in tok_copies:
        cp.wait_recv()
    for cp in log_copies:
        cp.wait_recv()
    tokm_copy = remote(tokbuf.at[xm * NC + 1 - c], sc["tokm"], {"seq": seq_of(x, zm, c)})

    def meet_far():
        pl.semaphore_wait(present, 1)
        tokm_copy.start()

    pl.when(z >= 4)(meet_far)
    r16 = iota((V, T), 0)
    onehot = jnp.concatenate([as_int(tokbuf[b] == r16) for b in range(8)], axis=0)
    onehot = onehot.astype(F32).astype(BF)
    counts = mm(
        onehot,
        jnp.concatenate(
            [mask_bf(tri_r > tri_c), mask_bf(tri_r < tri_c), jnp.ones((256, 128), BF)], axis=1
        ),
    ).astype(BF)
    row8 = iota((8, 128), 0)
    log_hv = ltab[0]
    for i in range(1, NY):
        log_hv = jnp.where(row8 // 2 == i, ltab[i], log_hv)
    r64, l64 = iota((64, 128), 0), iota((64, 128), 1)
    log_bd = jnp.where(r64 // 8 == l64 // 16, jnp.concatenate([log_hv] * 8, axis=0), 0.0)
    cums = mm(
        jnp.concatenate(split2(log_bd), axis=1), jnp.concatenate([counts, counts], axis=0)
    )
    weight = jnp.exp(cums[:, :512])
    weight = jnp.concatenate([weight[:, :256], weight[:, 256:]], axis=0)
    wh, wl = split2(weight)
    sums = mmt(wh, onehot) + mmt(wl, onehot)
    r2, l2 = iota((128, 128), 0), iota((128, 128), 1)
    sums = jnp.where(r2 // 8 % 8 == l2 // 16, sums, 0.0)
    for shift in (64, 32, 16):
        sums = sums + pltpu.roll(sums, shift, 1)
    sums = jnp.where(r2 % 8 == l2 // 16, sums, 0.0)
    totals = jnp.where(r64 % 8 == l64 // 16, cums[:, 512:], 0.0)

    def fold(a, i):
        return jnp.sum(a[8 * i : 8 * i + 8], axis=0, keepdims=True)

    cf = [fold(sums, b) for b in range(8)]
    cb = [fold(sums, 8 + b) for b in range(8)]
    ld = [fold(totals, b) for b in range(8)]
    cf_pair = [jnp.exp(ld[2 * i + 1]) * cf[2 * i] + cf[2 * i + 1] for i in range(NX)]
    cb_pair = [jnp.exp(ld[2 * i]) * cb[2 * i + 1] + cb[2 * i] for i in range(NX)]
    ld_pair = [ld[2 * i] + ld[2 * i + 1] for i in range(NX)]
    rows = [pick(as_int(xm >= i), cf_pair[i], cb_pair[i]) for i in range(NX)]
    own_b, sib, sib_ld, packed = cb_pair[0], cf[0], ld[0], ld_pair[0]
    for i in range(NX):
        here = as_int(xm == i)
        own_b = pick(here, cb_pair[i], own_b)
        sib = pick(here, pick(c, cb[2 * i + 1], cf[2 * i]), sib)
        sib_ld = pick(here, pick(c, ld[2 * i + 1], ld[2 * i]), sib_ld)
        packed = jnp.where(lane % 16 == i, ld_pair[i], packed)
    tile = jnp.concatenate(rows + [own_b, packed, sib, sib_ld], axis=0)
    ztile, zbuf = sc["ztile"], sc["zbuf"]
    ztile[...] = tile
    z_copies = [remote(ztile, zbuf.at[z], {"seq": seq_of(x, p, c)}) for p in z_near]
    for cp in z_copies:
        cp.start()
    pl.when(z < 4)(meet_far)
    far_copies = [remote(ztile, zbuf.at[z], {"seq": seq_of(x, p, c)}) for p in z_far]
    for cp in far_copies:
        cp.start()
    z_copies += far_copies
    zbuf[pl.ds(z, 1)] = tile[None]

    def lanes_of(a, b):
        return jnp.concatenate([ytab[i, a:b] for i in range(NY)], axis=1)

    for cp in tab_copies:
        cp.wait_recv()
    row16 = iota((V, 128), 0)
    l16 = iota((V, 128), 1)
    log_t = ytab[0, 48:64]
    for i in range(1, NY):
        log_t = jnp.where(l16 // 32 == i, ytab[i, 48:64], log_t)
    eye_t = jnp.where(row16 == l16 % 16, 1.0, 0.0)
    tables = jnp.concatenate([lanes_of(32, 48), lanes_of(16, 32), g_tab, jnp.exp(log_t), eye_t], axis=1)
    tables = jnp.concatenate([jnp.concatenate(split3(tables), axis=0), emb_p], axis=1)
    inner_rep = jnp.concatenate([lanes_of(0, 16)] * 8, axis=0)
    bd = iota((128, 512), 0) // 16 == iota((128, 512), 1) // 64
    x_bd = split2(jnp.where(bd, inner_rep, 0.0))
    outnorm_all = lanes_of(64, 65)
    other_core = {"seq": seq_of(x, z, 1 - c)}
    wo1_passed = []
    for cp, p in zip(wo1_copies, y_peers):
        cp.wait_recv()
        half = sc["wo1"].at[p, core_rows]
        wo1_passed.append(remote(half, half, other_core))
        wo1_passed[-1].start()
    tokm_copy.wait_recv()
    hot_m = as_int(sc["tokm"][...] == r16).astype(F32).astype(BF)
    rev = mask_bf(tri_r + tri_c == T - 1)
    hot_rev = mmt(rev, jnp.concatenate([hot_m] * 3, axis=0)).astype(BF)
    taken = mm(hot_rev, tables)
    silu_g, skip_x = taken[:, :512], taken[:, 512:1024]
    g_row, decay, hot = taken[:, 1024:1152], taken[:, 1152:1280], taken[:, 1280:1408]
    embedded = taken[:, 1408:]
    up_c, up_p = scan_rows(hot, decay, False)
    dn_c, dn_p = scan_rows(hot, decay, True)

    for cp in z_copies:
        cp.wait_recv()
    ls, lr = iota((128, 512), 1), iota((128, 512), 0)
    spread = mask_bf((lr // 16 == ls % 128 // 16) & (lr % 16 == ls // 128))
    ld_all = mm(
        jnp.concatenate(split2(zbuf[:, 5, :]), axis=1), jnp.concatenate([spread, spread], axis=0)
    )
    ld_all = jnp.concatenate([ld_all[:, 128 * i : 128 * i + 128] for i in range(NX)], axis=0)
    qm = xm * NZ + zm
    q, q2 = iota((32, 32), 0), iota((32, 32), 1)
    between = ((q2 > q) & (q2 < qm)) | ((q2 < q) & (q2 > qm))
    share = jnp.exp(exact_left(mask_bf(between), ld_all))
    zrow = iota((8, 128), 0)
    coefs = jnp.concatenate(
        [
            jnp.where((zrow > zm) & (jnp.full((8, 128), xm, jnp.int32) == i), zbuf[:, 4, :], zbuf[:, i, :])
            for i in range(NX)
        ],
        axis=0,
    )
    terms = share * coefs
    qrow = iota((32, 128), 0)
    carry_f = jnp.sum(jnp.where(qrow < qm, terms, 0.0), axis=0, keepdims=True)
    carry_b = jnp.sum(jnp.where(qrow > qm, terms, 0.0), axis=0, keepdims=True)
    at_m = zbuf[pl.ds(zm, 1)].reshape(8, 128)
    sib, sib_d = at_m[6:7], jnp.exp(at_m[7:8])
    carry_f = pick(c, carry_f, sib_d * carry_f + sib)
    carry_b = pick(c, sib_d * carry_b + sib, carry_b)
    coef = jnp.concatenate([up_c + up_p * carry_b, dn_c + dn_p * carry_f], axis=0)
    coef = coef * jnp.concatenate([g_row] * 2, axis=0)
    ssm = dot3_short(coef, x_bd)

    same_head = jnp.where(r2 // 64 == l2 // 64, 1.0 / 64, 0.0).astype(BF)
    same_head = jnp.concatenate([same_head, same_head], axis=0)

    def head_scale(w):
        parts = []
        for i in range(w.shape[1] // 128):
            parts.append(mm(jnp.concatenate(split2(w[:, 128 * i : 128 * i + 128] ** 2), axis=1), same_head))
        sq = parts[0] if len(parts) == 1 else jnp.concatenate(parts, axis=1)
        return lax.rsqrt(sq + EPS)

    for cp in wo1_passed:
        cp.wait_recv()
    wo1_p = split2(sc["wo1"][...].reshape(512, 256))
    w_up = (ssm[:T] + skip_x) * silu_g
    w_dn = (ssm[T:] + skip_x) * silu_g
    mixed = (w_up * head_scale(w_up) + w_dn * head_scale(w_dn)) * outnorm_all
    mirrored = embedded + dot3(mixed, wo1_p)
    mir = sc["mir"]
    mir[...] = mirrored

    n2 = split2(mirrored)
    rms2 = lax.rsqrt(jnp.mean(mirrored * mirrored, axis=-1, keepdims=True) + EPS)
    step = softplus(dot3(n2, sp2_p, mmt) * rms2 + halves(vm["sb2"][...]))
    both = dot3(n2, w2_early) * rms2
    inner, write = both[:, :128], both[:, 128:]
    cum = exact_left(mask_bf(tri_r >= tri_c), -halves(vm["ra2"][...]) * step)
    end = cum[T - 1 : T]
    stepped = inner * step
    write_t2 = split2(write.T)
    state = dot3(write_t2, stepped * jnp.exp(end - cum))
    own_d = jnp.exp(end)
    st, e1s, e1r = sc["st"], sc["e1s"], sc["e1r"]
    st[...] = state
    chunks = range(2)

    def fill(buf, rows, decay):
        buf[0:HALF] = rows
        buf[HALF:MSG] = jnp.broadcast_to(decay, (8, 128))

    def sent(ref, i):
        return ref.at[pl.ds(0, HALF + 1 if i == 0 else HALF)]

    def part(core, i):
        return st[pl.ds(pl.multiple_of(64 * core + HALF * i, HALF), HALF), :]

    e1o, n1r = sc["e1o"], sc["n1r"]
    next_same = {"seq": seq_of(x, xor(z, 1, 3), c)}
    next_other = {"seq": seq_of(x, xor(z, 1, 3), 1 - c)}
    e1 = [[], []]
    for i in chunks:
        fill(e1s.at[i], part(1 - c, i), own_d)
        fill(e1o.at[i], part(c, i), own_d)
        e1[i] = [
            remote(sent(e1s.at[i], i), sent(n1r.at[c, i], i), next_other),
            remote(sent(e1o.at[i], i), sent(n1r.at[c, i], i), next_same),
            remote(sent(e1s.at[i], i), sent(e1r.at[i], i), other_core),
        ]
        for cp in e1[i]:
            cp.start()

    s0, tot, dec, pre, pre_d = [None] * 2, [None] * 2, [None] * 2, [None] * 2, [None] * 2
    rounds = [[None] * 2 for _ in range(3)]

    def send_round(r, i):
        bs, br = sc["bs"].at[2 * r + i], sc["br"].at[2 * r + i]
        fill(bs, tot[i], dec[i])
        rounds[r][i] = remote(
            sent(bs, i), sent(br, i), {"seq": seq_of(x, xor(z, 1 << r, 3), c)}
        )
        rounds[r][i].start()

    wo2_copies = [remote(vm["op2"], sc["wo2"].at[y], {"head": p}) for p in y_peers]
    for cp in wo2_copies:
        cp.start()
    both = dot3(n2, w2_late) * rms2
    gate, read = both[:, :128], both[:, 128:]
    read2 = split2(read)
    sc["rd"][...] = jnp.concatenate(read2, axis=1)
    pairs = dot3_short(read2, write_t2)
    cum_t = cum.T
    allowed = tri_r >= tri_c
    local = halves(vm["sk2"][...]) * inner
    first = iota((T, 128), 1) < 64
    xs, xr = sc["xs"], sc["xr"]
    x_peers = [xor(x, k, 2) for k in (2, 1, 3)]
    x_copies = [[], []]
    for r in range(3):
        later = z // (1 << r) % 2
        for i in chunks:
            if r == 0:
                for cp in e1[i]:
                    cp.wait_recv()
                own, got = part(c, i), e1r[i, 0:HALF]
                s0[i], s1_ = pick(c, got, own), pick(c, own, got)
                if i == 0:
                    got_d = e1r[0, HALF : HALF + 1]
                    d0, d1 = pick(c, got_d, own_d), pick(c, own_d, got_d)
                    n0, n1 = n1r[0, 0, HALF : HALF + 1], n1r[1, 0, HALF : HALF + 1]
                    next_d = n0 * n1
                tot[i], dec[i] = d1 * s0[i] + s1_, d0 * d1
                pre[i], pre_d[i] = jnp.zeros((HALF, 128), F32), jnp.ones((1, 128), F32)
                got, got_d = n1 * n1r[0, i, 0:HALF] + n1r[1, i, 0:HALF], next_d
            else:
                rounds[r][i].wait_recv()
                got, got_d = sc["br"][2 * r + i, 0:HALF], sc["br"][2 * r, HALF : HALF + 1]
            tot[i] = pick(later, dec[i] * got + tot[i], got_d * tot[i] + got)
            dec[i] = dec[i] * got_d
            if r < 2:
                send_round(r + 1, i)
            else:
                fill(xs.at[i], tot[i], dec[i])
                x_copies[i] = [
                    remote(sent(xs.at[i], i), sent(xr.at[i, x], i), {"seq": seq_of(p, z, c)}) for p in x_peers
                ]
                for cp, p in zip(x_copies[i], x_peers):
                    pl.when(p > x)(cp.start)
            pre[i] = pick(later, pre_d[i] * got + pre[i], pre[i])
            pre_d[i] = pick(later, got_d * pre_d[i], pre_d[i])
        if r < 2:
            h = r
            diff = cum[:, 64 * h : 64 * h + 1] - cum_t[64 * h : 64 * h + 1, :]
            wts = jnp.where(allowed, jnp.exp(jnp.where(allowed, diff, 0.0)) * pairs, 0.0)
            local = local + dot3(wts, jnp.where(first if h == 0 else ~first, stepped, 0.0))
    sc["loc"][...] = local
    sc["gat"][...] = silu(gate)
    sc["cue"][...] = jnp.exp(cum)
    for cp in wo2_copies:
        cp.wait_recv()
    ks, kr = sc["ks"], sc["kr"]
    k_copies, mine = [], []
    for i in chunks:
        for cp, p in zip(x_copies[i], x_peers):
            pl.when(p < x)(cp.wait_recv)
        row_in = jnp.zeros((HALF, 128), F32)
        for n in range(NX - 1):
            row_in = pick(as_int(x > n), xr[0, n, HALF : HALF + 1] * row_in + xr[i, n, 0:HALF], row_in)
        k0 = pre_d[i] * row_in + pre[i]
        k1 = d0 * k0 + s0[i]
        ks[i] = pick(c, k0, k1)
        k_copies.append(remote(ks.at[i], kr.at[i], other_core))
        k_copies[i].start()
        mine.append(pick(c, k1, k0))
    for cp in k_copies:
        cp.wait_recv()
    got = jnp.concatenate([kr[0], kr[1]], axis=0)
    mine = jnp.concatenate(mine, axis=0)
    carried = jnp.concatenate([pick(c, got, mine), pick(c, mine, got)], axis=0)
    ch, cl = split2(carried)
    chh = jnp.concatenate([ch, ch], axis=0)
    gs, gr = sc["gs"], sc["gr"]

    def finish(rows):
        rd = sc["rd"][rows, :]
        y2 = sc["loc"][rows, :] + (mm(rd, chh) + mm(rd[:, :128], cl)) * sc["cue"][rows, :]
        w = y2 * sc["gat"][rows, :]
        return w * head_scale(w) * vm["on2"][...]

    def rows_of(p):
        return pl.ds(pl.multiple_of(64 * p, 64), 64)

    far = y_peers[0]
    gf = sc["gf"]
    gf[...] = finish(rows_of(far))
    g_copies = [remote(gf, gr.at[y], {"head": far})]
    g_copies[0].start()
    gs[...] = finish(pl.ds(0, T))
    for p in y_peers[1:]:
        g_copies.append(remote(gs.at[rows_of(p)], gr.at[y], {"head": p}))
        g_copies[-1].start()
    wo2 = sc["wo2"]
    out = mir[rows_of(y), :] + dot3_short(gs[rows_of(y), :], wo2[y])
    for cp, p in zip(g_copies[1:] + g_copies[:1], y_peers[1:] + y_peers[:1]):
        cp.wait_recv()
        out = out + dot3_short(gr[p], wo2[p])
    out_ref[...] = out

    for cp in (
        log_copies + tab_copies + tok_copies + [tokm_copy] + wo1_copies + wo1_passed + wo2_copies + z_copies
        + e1[0] + e1[1] + rounds[1] + rounds[2] + k_copies + g_copies
    ):
        cp.wait_send()
    for i in chunks:
        for cp, p in zip(x_copies[i], x_peers):
            pl.when(p > x)(cp.wait_send)


def per_device(*args):
    a = dict(zip(NAMES, args))
    for n in ("sp1", "sp2"):
        a[n] = a[n].T
    flat = [a[n].reshape(s) for n, s in zip(NAMES, SHAPES)]
    return pl.pallas_call(
        kernel,
        out_shape=jax.ShapeDtypeStruct((64, 256), F32),
        in_specs=[pl.BlockSpec(memory_space=pltpu.HBM)] * N_IN,
        out_specs=pl.BlockSpec(memory_space=pltpu.VMEM),
        scratch_shapes=[pltpu.VMEM(s, t) for s, t in zip(SHAPES, TYPES)]
        + [pltpu.VMEM(s, t) for _, s, t in SCRATCH]
        + [
            pltpu.SemaphoreType.DMA((N_IN + 1,)),
            pltpu.SemaphoreType.DMA((N_SEND,)),
            pltpu.SemaphoreType.DMA((N_SEND,)),
            pltpu.SemaphoreType.REGULAR,
        ],
        compiler_params=pltpu.CompilerParams(
            collective_id=0, has_side_effects=True, vmem_limit_bytes=60 * 2**20
        ),
    )(*flat)


def solution(mesh):
    tokens = P(("rep", "seq"))
    layer = (P(), P(None, None, "head"), P(), P(None, "head")) + (P("head"),) * 4 + (P("head", None),)
    in_specs = (tokens, P(), P()) + layer + layer
    return jax.shard_map(
        per_device,
        mesh=mesh,
        in_specs=in_specs,
        out_specs=P(("rep", "seq", "head"), None),
        check_vma=False,
    )
```

```python
import jax
import jax.numpy as jnp
from jax import lax
from jax.experimental import pallas as pl
from jax.experimental.pallas import tpu as pltpu
from jax.sharding import PartitionSpec as P

F32, BF = jnp.float32, jnp.bfloat16
MESH = pl.DeviceIdType.MESH
EPS = 1e-05
NX, NZ, NC, NY = 4, 8, 2, 4
T = 256
V = 16


def mm(a, b):
    return lax.dot_general(a, b, (((1,), (0,)), ((), ())), preferred_element_type=F32)


def mmt(a, b):
    return lax.dot_general(a, b, (((1,), (1,)), ((), ())), preferred_element_type=F32)


def split2(a):
    hi = a.astype(BF)
    return hi, (a - hi.astype(F32)).astype(BF)


def split3(a):
    hi = a.astype(BF)
    rest = a - hi.astype(F32)
    mid = rest.astype(BF)
    return hi, mid, (rest - mid.astype(F32)).astype(BF)


def dot3(a, b, f=mm):
    ah, al = a if isinstance(a, tuple) else split2(a)
    bh, bl = b if isinstance(b, tuple) else split2(b)
    return f(ah, bh) + (f(ah, bl) + f(al, bh))


def dot3_short(a, b):
    ah, al = a if isinstance(a, tuple) else split2(a)
    bh, bl = b if isinstance(b, tuple) else split2(b)
    return mm(jnp.concatenate([ah, al], axis=1), jnp.concatenate([bh, bh], axis=0)) + mm(ah, bl)


def exact_left(a, b):
    h, l = split2(b)
    return mm(a, h) + mm(a, l)


def exact_right(a, b):
    h, m, l = split3(a)
    return mm(h, b) + (mm(m, b) + mm(l, b))


def iota(shape, dim):
    return lax.broadcasted_iota(jnp.int32, shape, dim)


def softplus(a):
    return jnp.maximum(a, 0.0) + jnp.log1p(jnp.exp(-jnp.abs(a)))


def silu(a):
    return a / (1.0 + jnp.exp(-a))


def rms(a, gain):
    return a * lax.rsqrt(jnp.mean(a * a, axis=-1, keepdims=True) + EPS) * gain


def xor(a, k, bits):
    out = a
    for i in range(bits):
        if k >> i & 1:
            out = out + (1 << i) * (1 - 2 * (a // (1 << i) % 2))
    return out


def pick(flag, a, b):
    return jnp.where(jnp.full(a.shape, flag, jnp.int32) > 0, a, b)


def as_int(cond):
    return jnp.where(cond, 1, 0)


def halves(pair):
    return jnp.where(iota((1, 128), 1) < 64, pair[:, 0:1], pair[:, 1:2])


def scan_rows(coef, decay, reverse):
    rows = iota(coef.shape, 0)
    k = 1
    while k < T:
        if reverse:
            inside = rows < T - k
            shifted_c, shifted_d = pltpu.roll(coef, T - k, 0), pltpu.roll(decay, T - k, 0)
        else:
            inside = rows >= k
            shifted_c, shifted_d = pltpu.roll(coef, k, 0), pltpu.roll(decay, k, 0)
        coef = coef + jnp.where(inside, decay * shifted_c, 0.0)
        decay = jnp.where(inside, decay * shifted_d, decay)
        k *= 2
    return coef, decay


NAMES = (
    "tok", "emb", "comp",
    "pn1", "ip1", "sm1", "sp1", "sb1", "ra1", "sk1", "on1", "op1",
    "pn2", "ip2", "sm2", "sp2", "sb2", "ra2", "sk2", "on2", "op2",
)
SHAPES = (
    (1, T), (V, 256), (1, 256),
    (1, 256), (512, 128), (512, 128), (2, 256), (1, 2), (1, 2), (1, 2), (1, 128), (128, 256),
    (1, 256), (512, 128), (512, 128), (2, 256), (1, 2), (1, 2), (1, 2), (1, 128), (128, 256),
)
TYPES = (jnp.int32, F32, jnp.int32) + (F32,) * 18
N_IN = len(NAMES)
TAB = 72
HALF = 32
MSG = HALF + 8

SCRATCH = (
    ("tokbuf", (8, 1, T), jnp.int32),
    ("tokm", (1, T), jnp.int32),
    ("lsend", (8, 128), F32),
    ("ltab", (NY, 8, 128), F32),
    ("tsend", (TAB, 128), F32),
    ("ytab", (NY, TAB, 128), F32),
    ("wo1", (NY, 128, 256), F32),
    ("wo1s", (128, 256), F32),
    ("wo2", (NY, 128, 256), F32),
    ("ztile", (8, 128), F32),
    ("zbuf", (NZ, 8, 128), F32),
    ("mir", (T, 256), F32),
    ("st", (128, 128), F32),
    ("e1s", (2, MSG, 128), F32),
    ("e1o", (2, MSG, 128), F32),
    ("e1r", (2, MSG, 128), F32),
    ("n1r", (NC, 2, MSG, 128), F32),
    ("bs", (6, MSG, 128), F32),
    ("br", (6, MSG, 128), F32),
    ("xs", (2, MSG, 128), F32),
    ("xr", (2, NX, MSG, 128), F32),
    ("ks", (2, HALF, 128), F32),
    ("kr", (2, HALF, 128), F32),
    ("rd", (T, 256), BF),
    ("loc", (T, 128), F32),
    ("gat", (T, 128), F32),
    ("cue", (T, 128), F32),
    ("gs", (T, 128), F32),
    ("gf", (64, 128), F32),
    ("gr", (NY, 64, 128), F32),
)
N_RECV = 24
N_MORE = 2


def kernel(*refs):
    hbm = dict(zip(NAMES, refs[:N_IN]))
    out_ref = refs[N_IN]
    vm = dict(zip(NAMES, refs[N_IN + 1 :]))
    sc = {s[0]: r for s, r in zip(SCRATCH, refs[N_IN + 1 + N_IN :])}
    in_sem, recv_sem, present = refs[-3:]

    seq, y = lax.axis_index("seq"), lax.axis_index("head")
    x, z, c = seq // (NZ * NC), seq // NC % NZ, seq % NC
    xc = x * NC + c
    xm, zm = NX - 1 - x, NZ - 1 - z

    def seq_of(xi, zi, ci):
        return (xi * NZ + zi) * NC + ci

    y_peers = [xor(y, k, 2) for k in (2, 1, 3)]
    xc_peers = [xor(xc, k, 3) for k in (4, 5, 2, 3, 6, 7, 1)]
    z_near = [xor(z, k, 3) for k in (4, 3, 2, 1)]
    z_far = [xor(z, k, 3) for k in (7, 6, 5)]

    barrier = pltpu.get_barrier_semaphore()

    def greet(where):
        pl.semaphore_signal(barrier, inc=1, device_id=where, device_id_type=MESH)

    for p in z_near:
        greet({"seq": seq_of(x, p, c)})
    for p in xc_peers:
        greet({"seq": seq_of(p // NC, z, p % NC)})
    for p in y_peers:
        greet({"head": p})

    loads = {n: pltpu.make_async_copy(hbm[n], vm[n], in_sem.at[i]) for i, n in enumerate(NAMES)}
    first_loads = ("tok", "emb", "pn1", "sp1", "sb1", "ra1")
    for n in first_loads:
        loads[n].start()
    own_tok = pltpu.make_async_copy(hbm["tok"], sc["tokbuf"].at[xc], in_sem.at[N_IN])
    own_tok.start()
    other_loads = tuple(n for n in NAMES if n not in first_loads)
    for n in other_loads:
        loads[n].start()

    used = [0, 0]

    def next_sems():
        used[0] += 1
        used[1] += 1
        return in_sem.at[used[0] - 1], recv_sem.at[used[1] - 1]

    def remote(src, dst, where, sems=None):
        send, recv = sems or next_sems()
        return pltpu.make_async_remote_copy(
            src_ref=src, dst_ref=dst, send_sem=send, recv_sem=recv,
            device_id=where, device_id_type=MESH,
        )

    class Group:
        def __init__(self, like):
            self.send, self.recv = self.sems = next_sems()
            self.like = like

        def start(self, src, dst, where):
            remote(src, dst, where, self.sems).start()

        def wait_recv(self):
            pltpu.make_async_copy(self.like, self.like, self.recv).wait()

        def wait_send(self):
            pltpu.make_async_copy(self.like, self.like, self.send).wait()

    for n in first_loads:
        loads[n].wait()

    lane = iota((1, 128), 1)
    emb = vm["emb"][...]
    normed = rms(emb, vm["pn1"][...])
    sp, sb, ra = vm["sp1"][...], vm["sb1"][...], vm["ra1"][...]
    even = iota((8, 128), 0) % 2 == 0
    sp_r = jnp.where(iota((8, 256), 0) % 2 == 0, sp[0:1], sp[1:2])
    log_r = -jnp.where(even, ra[:, 0:1], ra[:, 1:2]) * softplus(
        dot3(sp_r, jnp.concatenate([normed] * 8, axis=0), mmt)
        + jnp.where(even, sb[:, 0:1], sb[:, 1:2])
    )
    lsend, tsend = sc["lsend"], sc["tsend"]
    lsend[...] = log_r

    pl.semaphore_wait(barrier, 14)
    pl.semaphore_signal(
        present, inc=1, device_id={"seq": seq_of(x, z_near[0], c)}, device_id_type=MESH
    )
    ltab, ytab, tokbuf = sc["ltab"], sc["ytab"], sc["tokbuf"]
    log_copies = Group(ltab.at[pl.ds(0, NY - 1)])
    tok_copies = Group(tokbuf.at[pl.ds(0, 7)])
    for p in y_peers:
        log_copies.start(lsend, ltab.at[y], {"head": p})
    for p in xc_peers:
        tok_copies.start(vm["tok"], tokbuf.at[xc], {"seq": seq_of(p // NC, z, p % NC)})
    ltab[pl.ds(y, 1)] = log_r[None]

    own_tok.wait()
    for n in other_loads:
        loads[n].wait()
    w1 = vm["ip1"]
    gate_w, inner_w = w1[pl.ds(0, 256, stride=2), :], w1[pl.ds(1, 256, stride=2), :]
    s1 = vm["sm1"]
    write_w, read_w = s1[pl.ds(0, 256, stride=2), :], s1[pl.ds(1, 256, stride=2), :]
    normed2 = split2(normed)
    table = dot3(normed2, jnp.concatenate([gate_w, inner_w, write_w, read_w], axis=1))
    gate_t, inner_t, write_t, read_t = (table[:, 128 * i : 128 * (i + 1)] for i in range(4))
    sk = vm["sk1"][...]
    r128 = iota((128, 256), 0)
    sp_p = jnp.where(r128 < 64, sp[0:1], sp[1:2])
    sp_alt = jnp.where(r128 // 16 % 2 == 0, sp[0:1], sp[1:2])
    logits = dot3(normed2, jnp.concatenate([sp_p, sp_alt], axis=0), mmt)
    step_p = softplus(logits[:, :128] + halves(sb))
    alt = lane // 16 % 2 == 0
    log_alt = -jnp.where(alt, ra[:, 0:1], ra[:, 1:2]) * softplus(
        logits[:, 128:] + jnp.where(alt, sb[:, 0:1], sb[:, 1:2])
    )
    tsend[0:16] = step_p * inner_t
    tsend[16:32] = halves(sk) * inner_t
    tsend[32:48] = silu(gate_t)
    tsend[48:64] = log_alt
    tsend[64:72] = jnp.broadcast_to(vm["on1"][...], (8, 128))
    tab_copies = Group(ytab.at[pl.ds(0, NY - 1)])
    for p in y_peers:
        tab_copies.start(tsend, ytab.at[y], {"head": p})
    g_tab = dot3(read_t, jnp.concatenate([write_t] * 8, axis=0), mmt)
    ytab[pl.ds(y, 1)] = tsend[...][None]
    sc["wo2"][pl.ds(y, 1)] = vm["op2"][...][None]

    tri_r, tri_c = iota((256, 256), 0), iota((256, 256), 1)
    one = jnp.ones((), F32)

    def mask_bf(cond):
        return jnp.where(cond, one, 0.0 * one).astype(BF)

    perm = mask_bf(vm["comp"][...] == tri_r)
    wo1s = sc["wo1s"]
    wo1s[...] = exact_right(vm["op1"][...], perm)
    sc["wo1"][pl.ds(y, 1)] = wo1s[...][None]
    w2, s2 = vm["ip2"], vm["sm2"]
    gain = jnp.broadcast_to(vm["pn2"][...], (128, 256)).T
    w2_early = split2(
        jnp.concatenate([w2[pl.ds(1, 256, stride=2), :] * gain, s2[pl.ds(0, 256, stride=2), :] * gain], axis=1)
    )
    w2_late = split2(
        jnp.concatenate([w2[pl.ds(0, 256, stride=2), :] * gain, s2[pl.ds(1, 256, stride=2), :] * gain], axis=1)
    )
    sp2 = vm["sp2"][...] * vm["pn2"][...]
    sp2_p = split2(jnp.where(r128 < 64, sp2[0:1], sp2[1:2]))
    emb_p = mm(jnp.concatenate(split3(emb), axis=0), perm).astype(BF)

    core_rows = pl.ds(pl.multiple_of(64 * c, 64), 64)
    wo1_copies = Group(sc["wo1"].at[pl.ds(0, NY - 1), pl.ds(0, 64)])
    for p in y_peers:
        wo1_copies.start(wo1s.at[core_rows], sc["wo1"].at[y, core_rows], {"head": p})
    tok_copies.wait_recv()
    log_copies.wait_recv()
    tokm_copy = remote(tokbuf.at[xm * NC + 1 - c], sc["tokm"], {"seq": seq_of(x, zm, c)})

    def meet_far():
        pl.semaphore_wait(present, 1)
        tokm_copy.start()

    pl.when(z >= 4)(meet_far)
    r16 = iota((V, T), 0)
    onehot = jnp.concatenate([as_int(tokbuf[b] == r16) for b in range(8)], axis=0)
    onehot = onehot.astype(F32).astype(BF)
    counts = mm(
        onehot,
        jnp.concatenate(
            [mask_bf(tri_r > tri_c), mask_bf(tri_r < tri_c), jnp.ones((256, 128), BF)], axis=1
        ),
    ).astype(BF)
    row8 = iota((8, 128), 0)
    log_hv = ltab[0]
    for i in range(1, NY):
        log_hv = jnp.where(row8 // 2 == i, ltab[i], log_hv)
    r64, l64 = iota((64, 128), 0), iota((64, 128), 1)
    log_bd = jnp.where(r64 // 8 == l64 // 16, jnp.concatenate([log_hv] * 8, axis=0), 0.0)
    cums = mm(
        jnp.concatenate(split2(log_bd), axis=1), jnp.concatenate([counts, counts], axis=0)
    )
    weight = jnp.exp(cums[:, :512])
    weight = jnp.concatenate([weight[:, :256], weight[:, 256:]], axis=0)
    wh, wl = split2(weight)
    sums = mmt(wh, onehot) + mmt(wl, onehot)
    r2, l2 = iota((128, 128), 0), iota((128, 128), 1)
    sums = jnp.where(r2 // 8 % 8 == l2 // 16, sums, 0.0)
    for shift in (64, 32, 16):
        sums = sums + pltpu.roll(sums, shift, 1)
    sums = jnp.where(r2 % 8 == l2 // 16, sums, 0.0)
    totals = jnp.where(r64 % 8 == l64 // 16, cums[:, 512:], 0.0)

    def fold(a, i):
        return jnp.sum(a[8 * i : 8 * i + 8], axis=0, keepdims=True)

    cf = [fold(sums, b) for b in range(8)]
    cb = [fold(sums, 8 + b) for b in range(8)]
    ld = [fold(totals, b) for b in range(8)]
    cf_pair = [jnp.exp(ld[2 * i + 1]) * cf[2 * i] + cf[2 * i + 1] for i in range(NX)]
    cb_pair = [jnp.exp(ld[2 * i]) * cb[2 * i + 1] + cb[2 * i] for i in range(NX)]
    ld_pair = [ld[2 * i] + ld[2 * i + 1] for i in range(NX)]
    rows = [pick(as_int(xm >= i), cf_pair[i], cb_pair[i]) for i in range(NX)]
    own_b, sib, sib_ld, packed = cb_pair[0], cf[0], ld[0], ld_pair[0]
    for i in range(NX):
        here = as_int(xm == i)
        own_b = pick(here, cb_pair[i], own_b)
        sib = pick(here, pick(c, cb[2 * i + 1], cf[2 * i]), sib)
        sib_ld = pick(here, pick(c, ld[2 * i + 1], ld[2 * i]), sib_ld)
        packed = jnp.where(lane % 16 == i, ld_pair[i], packed)
    tile = jnp.concatenate(rows + [own_b, packed, sib, sib_ld], axis=0)
    ztile, zbuf = sc["ztile"], sc["zbuf"]
    ztile[...] = tile
    z_copies = Group(zbuf.at[pl.ds(0, NZ - 1)])
    for p in z_near:
        z_copies.start(ztile, zbuf.at[z], {"seq": seq_of(x, p, c)})
    pl.when(z < 4)(meet_far)
    for p in z_far:
        z_copies.start(ztile, zbuf.at[z], {"seq": seq_of(x, p, c)})
    zbuf[pl.ds(z, 1)] = tile[None]

    def lanes_of(a, b):
        return jnp.concatenate([ytab[i, a:b] for i in range(NY)], axis=1)

    tab_copies.wait_recv()
    row16 = iota((V, 128), 0)
    l16 = iota((V, 128), 1)
    log_t = ytab[0, 48:64]
    for i in range(1, NY):
        log_t = jnp.where(l16 // 32 == i, ytab[i, 48:64], log_t)
    eye_t = jnp.where(row16 == l16 % 16, 1.0, 0.0)
    tables = jnp.concatenate([lanes_of(32, 48), lanes_of(16, 32), g_tab, jnp.exp(log_t), eye_t], axis=1)
    tables = jnp.concatenate([jnp.concatenate(split3(tables), axis=0), emb_p], axis=1)
    inner_rep = jnp.concatenate([lanes_of(0, 16)] * 8, axis=0)
    bd = iota((128, 512), 0) // 16 == iota((128, 512), 1) // 64
    x_bd = split2(jnp.where(bd, inner_rep, 0.0))
    outnorm_all = lanes_of(64, 65)
    other_core = {"seq": seq_of(x, z, 1 - c)}
    wo1_passed = Group(sc["wo1"].at[pl.ds(0, NY - 1), pl.ds(0, 64)])
    wo1_copies.wait_recv()
    for p in y_peers:
        half = sc["wo1"].at[p, core_rows]
        wo1_passed.start(half, half, other_core)
    tokm_copy.wait_recv()
    hot_m = as_int(sc["tokm"][...] == r16).astype(F32).astype(BF)
    rev = mask_bf(tri_r + tri_c == T - 1)
    hot_rev = mmt(rev, jnp.concatenate([hot_m] * 3, axis=0)).astype(BF)
    taken = mm(hot_rev, tables)
    silu_g, skip_x = taken[:, :512], taken[:, 512:1024]
    g_row, decay, hot = taken[:, 1024:1152], taken[:, 1152:1280], taken[:, 1280:1408]
    embedded = taken[:, 1408:]
    up_c, up_p = scan_rows(hot, decay, False)
    dn_c, dn_p = scan_rows(hot, decay, True)

    z_copies.wait_recv()
    ls, lr = iota((128, 512), 1), iota((128, 512), 0)
    spread = mask_bf((lr // 16 == ls % 128 // 16) & (lr % 16 == ls // 128))
    ld_all = mm(
        jnp.concatenate(split2(zbuf[:, 5, :]), axis=1), jnp.concatenate([spread, spread], axis=0)
    )
    ld_all = jnp.concatenate([ld_all[:, 128 * i : 128 * i + 128] for i in range(NX)], axis=0)
    qm = xm * NZ + zm
    q, q2 = iota((32, 32), 0), iota((32, 32), 1)
    between = ((q2 > q) & (q2 < qm)) | ((q2 < q) & (q2 > qm))
    share = jnp.exp(exact_left(mask_bf(between), ld_all))
    zrow = iota((8, 128), 0)
    coefs = jnp.concatenate(
        [
            jnp.where((zrow > zm) & (jnp.full((8, 128), xm, jnp.int32) == i), zbuf[:, 4, :], zbuf[:, i, :])
            for i in range(NX)
        ],
        axis=0,
    )
    terms = share * coefs
    qrow = iota((32, 128), 0)
    carry_f = jnp.sum(jnp.where(qrow < qm, terms, 0.0), axis=0, keepdims=True)
    carry_b = jnp.sum(jnp.where(qrow > qm, terms, 0.0), axis=0, keepdims=True)
    at_m = zbuf[pl.ds(zm, 1)].reshape(8, 128)
    sib, sib_d = at_m[6:7], jnp.exp(at_m[7:8])
    carry_f = pick(c, carry_f, sib_d * carry_f + sib)
    carry_b = pick(c, sib_d * carry_b + sib, carry_b)
    coef = jnp.concatenate([up_c + up_p * carry_b, dn_c + dn_p * carry_f], axis=0)
    coef = coef * jnp.concatenate([g_row] * 2, axis=0)
    ssm = dot3_short(coef, x_bd)

    same_head = jnp.where(r2 // 64 == l2 // 64, 1.0 / 64, 0.0).astype(BF)
    same_head = jnp.concatenate([same_head, same_head], axis=0)

    def head_scale(w):
        parts = []
        for i in range(w.shape[1] // 128):
            parts.append(mm(jnp.concatenate(split2(w[:, 128 * i : 128 * i + 128] ** 2), axis=1), same_head))
        sq = parts[0] if len(parts) == 1 else jnp.concatenate(parts, axis=1)
        return lax.rsqrt(sq + EPS)

    wo1_passed.wait_recv()
    wo1_p = split2(sc["wo1"][...].reshape(512, 256))
    w_up = (ssm[:T] + skip_x) * silu_g
    w_dn = (ssm[T:] + skip_x) * silu_g
    mixed = (w_up * head_scale(w_up) + w_dn * head_scale(w_dn)) * outnorm_all
    mirrored = embedded + dot3(mixed, wo1_p)
    mir = sc["mir"]
    mir[...] = mirrored

    n2 = split2(mirrored)
    rms2 = lax.rsqrt(jnp.mean(mirrored * mirrored, axis=-1, keepdims=True) + EPS)
    step = softplus(dot3(n2, sp2_p, mmt) * rms2 + halves(vm["sb2"][...]))
    both = dot3(n2, w2_early) * rms2
    inner, write = both[:, :128], both[:, 128:]
    cum = exact_left(mask_bf(tri_r >= tri_c), -halves(vm["ra2"][...]) * step)
    end = cum[T - 1 : T]
    stepped = inner * step
    write_t2 = split2(write.T)
    state = dot3(write_t2, stepped * jnp.exp(end - cum))
    own_d = jnp.exp(end)
    st, e1s, e1r = sc["st"], sc["e1s"], sc["e1r"]
    st[...] = state
    chunks = range(2)

    def fill(buf, rows, decay):
        buf[0:HALF] = rows
        buf[HALF:MSG] = jnp.broadcast_to(decay, (8, 128))

    def sent(ref, i):
        return ref.at[pl.ds(0, HALF + 1 if i == 0 else HALF)]

    def part(core, i):
        return st[pl.ds(pl.multiple_of(64 * core + HALF * i, HALF), HALF), :]

    e1o, n1r = sc["e1o"], sc["n1r"]
    next_same = {"seq": seq_of(x, xor(z, 1, 3), c)}
    next_other = {"seq": seq_of(x, xor(z, 1, 3), 1 - c)}
    e1 = [Group(sc["bs"].at[pl.ds(0, 3), pl.ds(0, HALF + 1 - i)]) for i in chunks]
    for i in chunks:
        fill(e1s.at[i], part(1 - c, i), own_d)
        fill(e1o.at[i], part(c, i), own_d)
        e1[i].start(sent(e1s.at[i], i), sent(n1r.at[c, i], i), next_other)
        e1[i].start(sent(e1o.at[i], i), sent(n1r.at[c, i], i), next_same)
        e1[i].start(sent(e1s.at[i], i), sent(e1r.at[i], i), other_core)

    s0, tot, dec, pre, pre_d = [None] * 2, [None] * 2, [None] * 2, [None] * 2, [None] * 2
    rounds = [[None] * 2 for _ in range(3)]

    def send_round(r, i):
        bs, br = sc["bs"].at[2 * r + i], sc["br"].at[2 * r + i]
        fill(bs, tot[i], dec[i])
        rounds[r][i] = remote(
            sent(bs, i), sent(br, i), {"seq": seq_of(x, xor(z, 1 << r, 3), c)}
        )
        rounds[r][i].start()

    wo2_copies = Group(sc["wo2"].at[pl.ds(0, NY - 1)])
    for p in y_peers:
        wo2_copies.start(vm["op2"], sc["wo2"].at[y], {"head": p})
    both = dot3(n2, w2_late) * rms2
    gate, read = both[:, :128], both[:, 128:]
    read2 = split2(read)
    sc["rd"][...] = jnp.concatenate(read2, axis=1)
    pairs = dot3_short(read2, write_t2)
    cum_t = cum.T
    allowed = tri_r >= tri_c
    local = halves(vm["sk2"][...]) * inner
    first = iota((T, 128), 1) < 64
    xs, xr = sc["xs"], sc["xr"]
    x_peers = [xor(x, k, 2) for k in (2, 1, 3)]
    x_copies = [[], []]
    for r in range(3):
        later = z // (1 << r) % 2
        for i in chunks:
            if r == 0:
                e1[i].wait_recv()
                own, got = part(c, i), e1r[i, 0:HALF]
                s0[i], s1_ = pick(c, got, own), pick(c, own, got)
                if i == 0:
                    got_d = e1r[0, HALF : HALF + 1]
                    d0, d1 = pick(c, got_d, own_d), pick(c, own_d, got_d)
                    n0, n1 = n1r[0, 0, HALF : HALF + 1], n1r[1, 0, HALF : HALF + 1]
                    next_d = n0 * n1
                tot[i], dec[i] = d1 * s0[i] + s1_, d0 * d1
                pre[i], pre_d[i] = jnp.zeros((HALF, 128), F32), jnp.ones((1, 128), F32)
                got, got_d = n1 * n1r[0, i, 0:HALF] + n1r[1, i, 0:HALF], next_d
            else:
                rounds[r][i].wait_recv()
                got, got_d = sc["br"][2 * r + i, 0:HALF], sc["br"][2 * r, HALF : HALF + 1]
            tot[i] = pick(later, dec[i] * got + tot[i], got_d * tot[i] + got)
            dec[i] = dec[i] * got_d
            if r < 2:
                send_round(r + 1, i)
            else:
                fill(xs.at[i], tot[i], dec[i])
                x_copies[i] = [
                    remote(sent(xs.at[i], i), sent(xr.at[i, x], i), {"seq": seq_of(p, z, c)}) for p in x_peers
                ]
                for cp, p in zip(x_copies[i], x_peers):
                    pl.when(p > x)(cp.start)
            pre[i] = pick(later, pre_d[i] * got + pre[i], pre[i])
            pre_d[i] = pick(later, got_d * pre_d[i], pre_d[i])
        if r < 2:
            h = r
            diff = cum[:, 64 * h : 64 * h + 1] - cum_t[64 * h : 64 * h + 1, :]
            wts = jnp.where(allowed, jnp.exp(jnp.where(allowed, diff, 0.0)) * pairs, 0.0)
            local = local + dot3(wts, jnp.where(first if h == 0 else ~first, stepped, 0.0))
    sc["loc"][...] = local
    sc["gat"][...] = silu(gate)
    sc["cue"][...] = jnp.exp(cum)
    wo2_copies.wait_recv()
    ks, kr = sc["ks"], sc["kr"]
    k_copies, mine = Group(kr), []
    for i in chunks:
        for cp, p in zip(x_copies[i], x_peers):
            pl.when(p < x)(cp.wait_recv)
        row_in = jnp.zeros((HALF, 128), F32)
        for n in range(NX - 1):
            row_in = pick(as_int(x > n), xr[0, n, HALF : HALF + 1] * row_in + xr[i, n, 0:HALF], row_in)
        k0 = pre_d[i] * row_in + pre[i]
        k1 = d0 * k0 + s0[i]
        ks[i] = pick(c, k0, k1)
        k_copies.start(ks.at[i], kr.at[i], other_core)
        mine.append(pick(c, k1, k0))
    k_copies.wait_recv()
    got = jnp.concatenate([kr[0], kr[1]], axis=0)
    mine = jnp.concatenate(mine, axis=0)
    carried = jnp.concatenate([pick(c, got, mine), pick(c, mine, got)], axis=0)
    ch, cl = split2(carried)
    chh = jnp.concatenate([ch, ch], axis=0)
    gs, gr = sc["gs"], sc["gr"]

    def finish(rows):
        rd = sc["rd"][rows, :]
        y2 = sc["loc"][rows, :] + (mm(rd, chh) + mm(rd[:, :128], cl)) * sc["cue"][rows, :]
        w = y2 * sc["gat"][rows, :]
        return w * head_scale(w) * vm["on2"][...]

    def rows_of(p):
        return pl.ds(pl.multiple_of(64 * p, 64), 64)

    far = y_peers[0]
    gf = sc["gf"]
    gf[...] = finish(rows_of(far))
    g_copies = [remote(gf, gr.at[y], {"head": far})]
    g_copies[0].start()
    gs[...] = finish(pl.ds(0, T))
    for p in y_peers[1:]:
        g_copies.append(remote(gs.at[rows_of(p)], gr.at[y], {"head": p}))
        g_copies[-1].start()
    wo2 = sc["wo2"]
    out = mir[rows_of(y), :] + dot3_short(gs[rows_of(y), :], wo2[y])
    for cp, p in zip(g_copies[1:] + g_copies[:1], y_peers[1:] + y_peers[:1]):
        cp.wait_recv()
        out = out + dot3_short(gr[p], wo2[p])
    out_ref[...] = out

    for cp in (
        [log_copies, tab_copies, tok_copies, tokm_copy, wo1_copies, wo1_passed, wo2_copies, z_copies]
        + e1 + rounds[1] + rounds[2] + [k_copies] + g_copies
    ):
        cp.wait_send()
    for i in chunks:
        for cp, p in zip(x_copies[i], x_peers):
            pl.when(p > x)(cp.wait_send)


def per_device(*args):
    a = dict(zip(NAMES, args))
    for n in ("sp1", "sp2"):
        a[n] = a[n].T
    flat = [a[n].reshape(s) for n, s in zip(NAMES, SHAPES)]
    return pl.pallas_call(
        kernel,
        out_shape=pltpu.VMEM((64, 256), F32),
        in_specs=[pl.BlockSpec(memory_space=pltpu.HBM)] * N_IN,
        out_specs=pl.BlockSpec(memory_space=pltpu.VMEM),
        scratch_shapes=[pltpu.VMEM(s, t) for s, t in zip(SHAPES, TYPES)]
        + [pltpu.VMEM(s, t) for _, s, t in SCRATCH]
        + [
            pltpu.SemaphoreType.DMA((N_IN + 1 + N_MORE,)),
            pltpu.SemaphoreType.DMA((N_RECV,)),
            pltpu.SemaphoreType.REGULAR,
        ],
        compiler_params=pltpu.CompilerParams(
            collective_id=0, has_side_effects=True, vmem_limit_bytes=60 * 2**20
        ),
    )(*flat)


def solution(mesh):
    tokens = P(("rep", "seq"))
    layer = (P(), P(None, None, "head"), P(), P(None, "head")) + (P("head"),) * 4 + (P("head", None),)
    in_specs = (tokens, P(), P()) + layer + layer
    return jax.shard_map(
        per_device,
        mesh=mesh,
        in_specs=in_specs,
        out_specs=P(("rep", "seq", "head"), None),
        check_vma=False,
    )
```

```python
import jax
import jax.numpy as jnp
from jax import lax
from jax.experimental import pallas as pl
from jax.experimental.pallas import tpu as pltpu
from jax.sharding import PartitionSpec as P

F32, BF = jnp.float32, jnp.bfloat16
MESH = pl.DeviceIdType.MESH
EPS = 1e-05
NX, NZ, NC, NY = 4, 8, 2, 4
T = 256
V = 16


def mm(a, b):
    return lax.dot_general(a, b, (((1,), (0,)), ((), ())), preferred_element_type=F32)


def mmt(a, b):
    return lax.dot_general(a, b, (((1,), (1,)), ((), ())), preferred_element_type=F32)


def split2(a):
    hi = a.astype(BF)
    return hi, (a - hi.astype(F32)).astype(BF)


def split3(a):
    hi = a.astype(BF)
    rest = a - hi.astype(F32)
    mid = rest.astype(BF)
    return hi, mid, (rest - mid.astype(F32)).astype(BF)


def dot3(a, b, f=mm):
    ah, al = a if isinstance(a, tuple) else split2(a)
    bh, bl = b if isinstance(b, tuple) else split2(b)
    return f(ah, bh) + (f(ah, bl) + f(al, bh))


def dot3_short(a, b):
    ah, al = a if isinstance(a, tuple) else split2(a)
    bh, bl = b if isinstance(b, tuple) else split2(b)
    return mm(jnp.concatenate([ah, al], axis=1), jnp.concatenate([bh, bh], axis=0)) + mm(ah, bl)


def exact_left(a, b):
    h, l = split2(b)
    return mm(a, h) + mm(a, l)


def exact_right(a, b):
    h, m, l = split3(a)
    return mm(h, b) + (mm(m, b) + mm(l, b))


def iota(shape, dim):
    return lax.broadcasted_iota(jnp.int32, shape, dim)


def softplus(a):
    return jnp.maximum(a, 0.0) + jnp.log1p(jnp.exp(-jnp.abs(a)))


def silu(a):
    return a / (1.0 + jnp.exp(-a))


def rms(a, gain):
    return a * lax.rsqrt(jnp.mean(a * a, axis=-1, keepdims=True) + EPS) * gain


def xor(a, k, bits):
    out = a
    for i in range(bits):
        if k >> i & 1:
            out = out + (1 << i) * (1 - 2 * (a // (1 << i) % 2))
    return out


def pick(flag, a, b):
    return jnp.where(jnp.full(a.shape, flag, jnp.int32) > 0, a, b)


def as_int(cond):
    return jnp.where(cond, 1, 0)


def halves(pair):
    return jnp.where(iota((1, 128), 1) < 64, pair[:, 0:1], pair[:, 1:2])


def scan_rows(coef, decay, reverse):
    rows = iota(coef.shape, 0)
    k = 1
    while k < T:
        if reverse:
            inside = rows < T - k
            shifted_c, shifted_d = pltpu.roll(coef, T - k, 0), pltpu.roll(decay, T - k, 0)
        else:
            inside = rows >= k
            shifted_c, shifted_d = pltpu.roll(coef, k, 0), pltpu.roll(decay, k, 0)
        coef = coef + jnp.where(inside, decay * shifted_c, 0.0)
        decay = jnp.where(inside, decay * shifted_d, decay)
        k *= 2
    return coef, decay


NAMES = (
    "tok", "emb", "comp",
    "pn1", "ip1", "sm1", "sp1", "sb1", "ra1", "sk1", "on1", "op1",
    "pn2", "ip2", "sm2", "sp2", "sb2", "ra2", "sk2", "on2", "op2",
)
SHAPES = (
    (1, T), (V, 256), (1, 256),
    (1, 256), (512, 128), (512, 128), (2, 256), (1, 2), (1, 2), (1, 2), (1, 128), (128, 256),
    (1, 256), (512, 128), (512, 128), (2, 256), (1, 2), (1, 2), (1, 2), (1, 128), (128, 256),
)
TYPES = (jnp.int32, F32, jnp.int32) + (F32,) * 18
N_IN = len(NAMES)
TAB = 72
HALF = 32
MSG = HALF + 8

SCRATCH = (
    ("tokbuf", (8, 1, T), jnp.int32),
    ("tokr", (4, 1, T), jnp.int32),
    ("tokm", (1, T), jnp.int32),
    ("lsend", (8, 128), F32),
    ("ltab", (NY, 8, 128), F32),
    ("tsend", (TAB, 128), F32),
    ("ytab", (NY, TAB, 128), F32),
    ("wo1", (NY, 128, 256), F32),
    ("wo1s", (128, 256), F32),
    ("wo2", (NY, 128, 256), F32),
    ("ztile", (8, 128), F32),
    ("zbuf", (NZ, 8, 128), F32),
    ("mir", (T, 256), F32),
    ("st", (128, 128), F32),
    ("e1s", (2, MSG, 128), F32),
    ("e1o", (2, MSG, 128), F32),
    ("e1r", (2, MSG, 128), F32),
    ("n1r", (NC, 2, MSG, 128), F32),
    ("bs", (6, MSG, 128), F32),
    ("br", (6, MSG, 128), F32),
    ("xs", (2, MSG, 128), F32),
    ("xr", (2, NX, MSG, 128), F32),
    ("ks", (2, HALF, 128), F32),
    ("kr", (2, HALF, 128), F32),
    ("rd", (T, 256), BF),
    ("loc", (T, 128), F32),
    ("gat", (T, 128), F32),
    ("cue", (T, 128), F32),
    ("gs", (T, 128), F32),
    ("gf", (64, 128), F32),
    ("gr", (NY, 64, 128), F32),
)
N_RECV = 29
N_MORE = 7


def kernel(*refs):
    hbm = dict(zip(NAMES, refs[:N_IN]))
    out_ref = refs[N_IN]
    vm = dict(zip(NAMES, refs[N_IN + 1 :]))
    sc = {s[0]: r for s, r in zip(SCRATCH, refs[N_IN + 1 + N_IN :])}
    in_sem, recv_sem, present = refs[-3:]

    seq, y = lax.axis_index("seq"), lax.axis_index("head")
    x, z, c = seq // (NZ * NC), seq // NC % NZ, seq % NC
    xc = x * NC + c
    xm, zm = NX - 1 - x, NZ - 1 - z

    def seq_of(xi, zi, ci):
        return (xi * NZ + zi) * NC + ci

    y_peers = [xor(y, k, 2) for k in (2, 1, 3)]
    xc_peers = [xor(xc, k, 3) for k in (4, 5, 2, 3, 6, 7, 1)]
    z_group = [xor(z, k, 3) for k in (3, 2, 1)]
    low, high, relay, above = z < 4, z >= 4, z == 4, z > 4

    barrier = pltpu.get_barrier_semaphore()

    def greet(where):
        pl.semaphore_signal(barrier, inc=1, device_id=where, device_id_type=MESH)

    for p in z_group:
        greet({"seq": seq_of(x, p, c)})
    pl.when(z == 3)(lambda: greet({"seq": seq_of(x, 4, c)}))
    pl.when(relay)(lambda: greet({"seq": seq_of(x, 3, c)}))
    for p in xc_peers:
        greet({"seq": seq_of(p // NC, z, p % NC)})
    for p in y_peers:
        greet({"head": p})

    loads = {n: pltpu.make_async_copy(hbm[n], vm[n], in_sem.at[i]) for i, n in enumerate(NAMES)}
    first_loads = ("tok", "emb", "pn1", "sp1", "sb1", "ra1")
    for n in first_loads:
        loads[n].start()
    own_tok = pltpu.make_async_copy(hbm["tok"], sc["tokbuf"].at[xc], in_sem.at[N_IN])
    own_tok.start()
    other_loads = tuple(n for n in NAMES if n not in first_loads)
    for n in other_loads:
        loads[n].start()

    used = [0, 0]

    def next_sems():
        used[0] += 1
        used[1] += 1
        assert used[1] <= N_RECV
        assert used[0] <= N_IN + 1 + N_MORE
        return in_sem.at[used[0] - 1], recv_sem.at[used[1] - 1]

    def remote(src, dst, where, sems=None):
        send, recv = sems or next_sems()
        return pltpu.make_async_remote_copy(
            src_ref=src, dst_ref=dst, send_sem=send, recv_sem=recv,
            device_id=where, device_id_type=MESH,
        )

    class Group:
        def __init__(self, like, sent_like=None):
            self.send, self.recv = self.sems = next_sems()
            self.like = like
            self.sent_like = like if sent_like is None else sent_like

        def start(self, src, dst, where):
            remote(src, dst, where, self.sems).start()

        def wait_recv(self):
            pltpu.make_async_copy(self.like, self.like, self.recv).wait()

        def wait_send(self):
            pltpu.make_async_copy(self.sent_like, self.sent_like, self.send).wait()

    for n in first_loads:
        loads[n].wait()

    lane = iota((1, 128), 1)
    emb = vm["emb"][...]
    normed = rms(emb, vm["pn1"][...])
    sp, sb, ra = vm["sp1"][...], vm["sb1"][...], vm["ra1"][...]
    even = iota((8, 128), 0) % 2 == 0
    sp_r = jnp.where(iota((8, 256), 0) % 2 == 0, sp[0:1], sp[1:2])
    log_r = -jnp.where(even, ra[:, 0:1], ra[:, 1:2]) * softplus(
        dot3(sp_r, jnp.concatenate([normed] * 8, axis=0), mmt)
        + jnp.where(even, sb[:, 0:1], sb[:, 1:2])
    )
    lsend, tsend = sc["lsend"], sc["tsend"]
    lsend[...] = log_r

    def tell(p):
        pl.semaphore_signal(
            present, inc=1, device_id={"seq": seq_of(x, p, c)}, device_id_type=MESH
        )

    across = (z == 3) | relay
    pl.when(across)(lambda: pl.semaphore_wait(barrier, 14))
    pl.when(jnp.logical_not(across))(lambda: pl.semaphore_wait(barrier, 13))

    @pl.when(z == 3)
    def _():
        for p in (4, 0, 1, 2):
            tell(p)

    @pl.when(relay)
    def _():
        pl.semaphore_wait(present, 1)
        for p in (7, 6, 5):
            tell(p)

    ltab, ytab, tokbuf = sc["ltab"], sc["ytab"], sc["tokbuf"]
    log_copies = Group(ltab.at[pl.ds(0, NY - 1)])
    tok_copies = Group(tokbuf.at[pl.ds(0, 7)])
    for p in y_peers:
        log_copies.start(lsend, ltab.at[y], {"head": p})
    for p in xc_peers:
        tok_copies.start(vm["tok"], tokbuf.at[xc], {"seq": seq_of(p // NC, z, p % NC)})
    ltab[pl.ds(y, 1)] = log_r[None]

    own_tok.wait()
    for n in other_loads:
        loads[n].wait()
    w1 = vm["ip1"]
    gate_w, inner_w = w1[pl.ds(0, 256, stride=2), :], w1[pl.ds(1, 256, stride=2), :]
    s1 = vm["sm1"]
    write_w, read_w = s1[pl.ds(0, 256, stride=2), :], s1[pl.ds(1, 256, stride=2), :]
    normed2 = split2(normed)
    table = dot3(normed2, jnp.concatenate([gate_w, inner_w, write_w, read_w], axis=1))
    gate_t, inner_t, write_t, read_t = (table[:, 128 * i : 128 * (i + 1)] for i in range(4))
    sk = vm["sk1"][...]
    r128 = iota((128, 256), 0)
    sp_p = jnp.where(r128 < 64, sp[0:1], sp[1:2])
    sp_alt = jnp.where(r128 // 16 % 2 == 0, sp[0:1], sp[1:2])
    logits = dot3(normed2, jnp.concatenate([sp_p, sp_alt], axis=0), mmt)
    step_p = softplus(logits[:, :128] + halves(sb))
    alt = lane // 16 % 2 == 0
    log_alt = -jnp.where(alt, ra[:, 0:1], ra[:, 1:2]) * softplus(
        logits[:, 128:] + jnp.where(alt, sb[:, 0:1], sb[:, 1:2])
    )
    tsend[0:16] = step_p * inner_t
    tsend[16:32] = halves(sk) * inner_t
    tsend[32:48] = silu(gate_t)
    tsend[48:64] = log_alt
    tsend[64:72] = jnp.broadcast_to(vm["on1"][...], (8, 128))
    tab_copies = Group(ytab.at[pl.ds(0, NY - 1)])
    for p in y_peers:
        tab_copies.start(tsend, ytab.at[y], {"head": p})
    g_tab = dot3(read_t, jnp.concatenate([write_t] * 8, axis=0), mmt)
    ytab[pl.ds(y, 1)] = tsend[...][None]
    sc["wo2"][pl.ds(y, 1)] = vm["op2"][...][None]

    tri_r, tri_c = iota((256, 256), 0), iota((256, 256), 1)
    one = jnp.ones((), F32)

    def mask_bf(cond):
        return jnp.where(cond, one, 0.0 * one).astype(BF)

    perm = mask_bf(vm["comp"][...] == tri_r)
    wo1s = sc["wo1s"]
    wo1s[...] = exact_right(vm["op1"][...], perm)
    sc["wo1"][pl.ds(y, 1)] = wo1s[...][None]
    w2, s2 = vm["ip2"], vm["sm2"]
    gain = jnp.broadcast_to(vm["pn2"][...], (128, 256)).T
    w2_early = split2(
        jnp.concatenate([w2[pl.ds(1, 256, stride=2), :] * gain, s2[pl.ds(0, 256, stride=2), :] * gain], axis=1)
    )
    w2_late = split2(
        jnp.concatenate([w2[pl.ds(0, 256, stride=2), :] * gain, s2[pl.ds(1, 256, stride=2), :] * gain], axis=1)
    )
    sp2 = vm["sp2"][...] * vm["pn2"][...]
    sp2_p = split2(jnp.where(r128 < 64, sp2[0:1], sp2[1:2]))
    emb_p = mm(jnp.concatenate(split3(emb), axis=0), perm).astype(BF)

    core_rows = pl.ds(pl.multiple_of(64 * c, 64), 64)
    wo1_copies = Group(sc["wo1"].at[pl.ds(0, NY - 1), pl.ds(0, 64)])
    for p in y_peers:
        wo1_copies.start(wo1s.at[core_rows], sc["wo1"].at[y, core_rows], {"head": p})
    tok_copies.wait_recv()
    log_copies.wait_recv()
    pl.when(jnp.logical_not(across))(lambda: pl.semaphore_wait(present, 1))
    tokr, tokm = sc["tokr"], sc["tokm"]
    to_gate = {"seq": seq_of(x, 4, c)}
    mirror_tok = tokbuf.at[xm * NC + 1 - c]
    tokm_copy = remote(mirror_tok, tokm, {"seq": seq_of(x, zm, c)})
    tok_low = Group(tokr, tokr.at[pl.ds(0, 1)])
    pl.when(high)(tokm_copy.start)
    pl.when(low)(lambda: tok_low.start(mirror_tok, tokr.at[z], to_gate))
    r16 = iota((V, T), 0)
    onehot = jnp.concatenate([as_int(tokbuf[b] == r16) for b in range(8)], axis=0)
    onehot = onehot.astype(F32).astype(BF)
    counts = mm(
        onehot,
        jnp.concatenate(
            [mask_bf(tri_r > tri_c), mask_bf(tri_r < tri_c), jnp.ones((256, 128), BF)], axis=1
        ),
    ).astype(BF)
    row8 = iota((8, 128), 0)
    log_hv = ltab[0]
    for i in range(1, NY):
        log_hv = jnp.where(row8 // 2 == i, ltab[i], log_hv)
    r64, l64 = iota((64, 128), 0), iota((64, 128), 1)
    log_bd = jnp.where(r64 // 8 == l64 // 16, jnp.concatenate([log_hv] * 8, axis=0), 0.0)
    cums = mm(
        jnp.concatenate(split2(log_bd), axis=1), jnp.concatenate([counts, counts], axis=0)
    )
    weight = jnp.exp(cums[:, :512])
    weight = jnp.concatenate([weight[:, :256], weight[:, 256:]], axis=0)
    wh, wl = split2(weight)
    sums = mmt(wh, onehot) + mmt(wl, onehot)
    r2, l2 = iota((128, 128), 0), iota((128, 128), 1)
    sums = jnp.where(r2 // 8 % 8 == l2 // 16, sums, 0.0)
    for shift in (64, 32, 16):
        sums = sums + pltpu.roll(sums, shift, 1)
    sums = jnp.where(r2 % 8 == l2 // 16, sums, 0.0)
    totals = jnp.where(r64 % 8 == l64 // 16, cums[:, 512:], 0.0)

    def fold(a, i):
        return jnp.sum(a[8 * i : 8 * i + 8], axis=0, keepdims=True)

    cf = [fold(sums, b) for b in range(8)]
    cb = [fold(sums, 8 + b) for b in range(8)]
    ld = [fold(totals, b) for b in range(8)]
    cf_pair = [jnp.exp(ld[2 * i + 1]) * cf[2 * i] + cf[2 * i + 1] for i in range(NX)]
    cb_pair = [jnp.exp(ld[2 * i]) * cb[2 * i + 1] + cb[2 * i] for i in range(NX)]
    ld_pair = [ld[2 * i] + ld[2 * i + 1] for i in range(NX)]
    rows = [pick(as_int(xm >= i), cf_pair[i], cb_pair[i]) for i in range(NX)]
    own_b, sib, sib_ld, packed = cb_pair[0], cf[0], ld[0], ld_pair[0]
    for i in range(NX):
        here = as_int(xm == i)
        own_b = pick(here, cb_pair[i], own_b)
        sib = pick(here, pick(c, cb[2 * i + 1], cf[2 * i]), sib)
        sib_ld = pick(here, pick(c, ld[2 * i + 1], ld[2 * i]), sib_ld)
        packed = jnp.where(lane % 16 == i, ld_pair[i], packed)
    tile = jnp.concatenate(rows + [own_b, packed, sib, sib_ld], axis=0)
    ztile, zbuf = sc["ztile"], sc["zbuf"]
    ztile[...] = tile
    tiles = zbuf.at[pl.ds(0, 4)]
    z_own = Group(zbuf.at[pl.ds(0, 3)])
    z_down = Group(tiles)
    z_low = Group(tiles, zbuf.at[pl.ds(0, 1)])
    z_up = Group(tiles, sc["loc"].at[pl.ds(0, 96)])
    tok_up = Group(tokm, tokr.at[pl.ds(0, 3)])
    pl.when(low)(lambda: z_low.start(ztile, zbuf.at[z], to_gate))

    @pl.when(high)
    def _():
        for p in range(4):
            z_down.start(ztile, zbuf.at[z], {"seq": seq_of(x, p, c)})

    for p in z_group:
        z_own.start(ztile, zbuf.at[z], {"seq": seq_of(x, p, c)})

    @pl.when(relay)
    def _():
        tok_low.wait_recv()
        for p in range(3):
            tok_up.start(tokr.at[p], tokm, {"seq": seq_of(x, NZ - 1 - p, c)})
        z_low.wait_recv()
        for p in (7, 6, 5):
            for n in range(4):
                z_up.start(zbuf.at[n], zbuf.at[n], {"seq": seq_of(x, p, c)})
        tokm[...] = tokr[3]

    zbuf[pl.ds(z, 1)] = tile[None]

    def lanes_of(a, b):
        return jnp.concatenate([ytab[i, a:b] for i in range(NY)], axis=1)

    tab_copies.wait_recv()
    row16 = iota((V, 128), 0)
    l16 = iota((V, 128), 1)
    log_t = ytab[0, 48:64]
    for i in range(1, NY):
        log_t = jnp.where(l16 // 32 == i, ytab[i, 48:64], log_t)
    eye_t = jnp.where(row16 == l16 % 16, 1.0, 0.0)
    tables = jnp.concatenate([lanes_of(32, 48), lanes_of(16, 32), g_tab, jnp.exp(log_t), eye_t], axis=1)
    tables = jnp.concatenate([jnp.concatenate(split3(tables), axis=0), emb_p], axis=1)
    inner_rep = jnp.concatenate([lanes_of(0, 16)] * 8, axis=0)
    bd = iota((128, 512), 0) // 16 == iota((128, 512), 1) // 64
    x_bd = split2(jnp.where(bd, inner_rep, 0.0))
    outnorm_all = lanes_of(64, 65)
    other_core = {"seq": seq_of(x, z, 1 - c)}
    wo1_passed = Group(sc["wo1"].at[pl.ds(0, NY - 1), pl.ds(0, 64)])
    wo1_copies.wait_recv()
    for p in y_peers:
        half = sc["wo1"].at[p, core_rows]
        wo1_passed.start(half, half, other_core)
    pl.when(low)(tokm_copy.wait_recv)
    pl.when(above)(tok_up.wait_recv)
    hot_m = as_int(sc["tokm"][...] == r16).astype(F32).astype(BF)
    rev = mask_bf(tri_r + tri_c == T - 1)
    hot_rev = mmt(rev, jnp.concatenate([hot_m] * 3, axis=0)).astype(BF)
    taken = mm(hot_rev, tables)
    silu_g, skip_x = taken[:, :512], taken[:, 512:1024]
    g_row, decay, hot = taken[:, 1024:1152], taken[:, 1152:1280], taken[:, 1280:1408]
    embedded = taken[:, 1408:]
    up_c, up_p = scan_rows(hot, decay, False)
    dn_c, dn_p = scan_rows(hot, decay, True)

    z_own.wait_recv()
    pl.when(low)(z_down.wait_recv)
    pl.when(above)(z_up.wait_recv)
    ls, lr = iota((128, 512), 1), iota((128, 512), 0)
    spread = mask_bf((lr // 16 == ls % 128 // 16) & (lr % 16 == ls // 128))
    ld_all = mm(
        jnp.concatenate(split2(zbuf[:, 5, :]), axis=1), jnp.concatenate([spread, spread], axis=0)
    )
    ld_all = jnp.concatenate([ld_all[:, 128 * i : 128 * i + 128] for i in range(NX)], axis=0)
    qm = xm * NZ + zm
    q, q2 = iota((32, 32), 0), iota((32, 32), 1)
    between = ((q2 > q) & (q2 < qm)) | ((q2 < q) & (q2 > qm))
    share = jnp.exp(exact_left(mask_bf(between), ld_all))
    zrow = iota((8, 128), 0)
    coefs = jnp.concatenate(
        [
            jnp.where((zrow > zm) & (jnp.full((8, 128), xm, jnp.int32) == i), zbuf[:, 4, :], zbuf[:, i, :])
            for i in range(NX)
        ],
        axis=0,
    )
    terms = share * coefs
    qrow = iota((32, 128), 0)
    carry_f = jnp.sum(jnp.where(qrow < qm, terms, 0.0), axis=0, keepdims=True)
    carry_b = jnp.sum(jnp.where(qrow > qm, terms, 0.0), axis=0, keepdims=True)
    at_m = zbuf[pl.ds(zm, 1)].reshape(8, 128)
    sib, sib_d = at_m[6:7], jnp.exp(at_m[7:8])
    carry_f = pick(c, carry_f, sib_d * carry_f + sib)
    carry_b = pick(c, sib_d * carry_b + sib, carry_b)
    coef = jnp.concatenate([up_c + up_p * carry_b, dn_c + dn_p * carry_f], axis=0)
    coef = coef * jnp.concatenate([g_row] * 2, axis=0)
    ssm = dot3_short(coef, x_bd)

    same_head = jnp.where(r2 // 64 == l2 // 64, 1.0 / 64, 0.0).astype(BF)
    same_head = jnp.concatenate([same_head, same_head], axis=0)

    def head_scale(w):
        parts = []
        for i in range(w.shape[1] // 128):
            parts.append(mm(jnp.concatenate(split2(w[:, 128 * i : 128 * i + 128] ** 2), axis=1), same_head))
        sq = parts[0] if len(parts) == 1 else jnp.concatenate(parts, axis=1)
        return lax.rsqrt(sq + EPS)

    wo1_passed.wait_recv()
    wo1_p = split2(sc["wo1"][...].reshape(512, 256))
    w_up = (ssm[:T] + skip_x) * silu_g
    w_dn = (ssm[T:] + skip_x) * silu_g
    mixed = (w_up * head_scale(w_up) + w_dn * head_scale(w_dn)) * outnorm_all
    mirrored = embedded + dot3(mixed, wo1_p)
    mir = sc["mir"]
    mir[...] = mirrored

    n2 = split2(mirrored)
    rms2 = lax.rsqrt(jnp.mean(mirrored * mirrored, axis=-1, keepdims=True) + EPS)
    step = softplus(dot3(n2, sp2_p, mmt) * rms2 + halves(vm["sb2"][...]))
    both = dot3(n2, w2_early) * rms2
    inner, write = both[:, :128], both[:, 128:]
    cum = exact_left(mask_bf(tri_r >= tri_c), -halves(vm["ra2"][...]) * step)
    end = cum[T - 1 : T]
    stepped = inner * step
    write_t2 = split2(write.T)
    state = dot3(write_t2, stepped * jnp.exp(end - cum))
    own_d = jnp.exp(end)
    st, e1s, e1r = sc["st"], sc["e1s"], sc["e1r"]
    st[...] = state
    chunks = range(2)

    def fill(buf, rows, decay):
        buf[0:HALF] = rows
        buf[HALF:MSG] = jnp.broadcast_to(decay, (8, 128))

    def sent(ref, i):
        return ref.at[pl.ds(0, HALF + 1 if i == 0 else HALF)]

    def part(core, i):
        return st[pl.ds(pl.multiple_of(64 * core + HALF * i, HALF), HALF), :]

    e1o, n1r = sc["e1o"], sc["n1r"]
    next_same = {"seq": seq_of(x, xor(z, 1, 3), c)}
    next_other = {"seq": seq_of(x, xor(z, 1, 3), 1 - c)}
    e1 = [Group(sc["bs"].at[pl.ds(0, 3), pl.ds(0, HALF + 1 - i)]) for i in chunks]
    for i in chunks:
        fill(e1s.at[i], part(1 - c, i), own_d)
        fill(e1o.at[i], part(c, i), own_d)
        e1[i].start(sent(e1s.at[i], i), sent(n1r.at[c, i], i), next_other)
        e1[i].start(sent(e1o.at[i], i), sent(n1r.at[c, i], i), next_same)
        e1[i].start(sent(e1s.at[i], i), sent(e1r.at[i], i), other_core)

    s0, tot, dec, pre, pre_d = [None] * 2, [None] * 2, [None] * 2, [None] * 2, [None] * 2
    rounds = [[None] * 2 for _ in range(3)]

    def send_round(r, i):
        bs, br = sc["bs"].at[2 * r + i], sc["br"].at[2 * r + i]
        fill(bs, tot[i], dec[i])
        rounds[r][i] = remote(
            sent(bs, i), sent(br, i), {"seq": seq_of(x, xor(z, 1 << r, 3), c)}
        )
        rounds[r][i].start()

    wo2_copies = Group(sc["wo2"].at[pl.ds(0, NY - 1)])
    for p in y_peers:
        wo2_copies.start(vm["op2"], sc["wo2"].at[y], {"head": p})
    both = dot3(n2, w2_late) * rms2
    gate, read = both[:, :128], both[:, 128:]
    read2 = split2(read)
    sc["rd"][...] = jnp.concatenate(read2, axis=1)
    pairs = dot3_short(read2, write_t2)
    cum_t = cum.T
    allowed = tri_r >= tri_c
    local = halves(vm["sk2"][...]) * inner
    first = iota((T, 128), 1) < 64
    xs, xr = sc["xs"], sc["xr"]
    x_peers = [xor(x, k, 2) for k in (2, 1, 3)]
    x_copies = [[], []]
    for r in range(3):
        later = z // (1 << r) % 2
        for i in chunks:
            if r == 0:
                e1[i].wait_recv()
                own, got = part(c, i), e1r[i, 0:HALF]
                s0[i], s1_ = pick(c, got, own), pick(c, own, got)
                if i == 0:
                    got_d = e1r[0, HALF : HALF + 1]
                    d0, d1 = pick(c, got_d, own_d), pick(c, own_d, got_d)
                    n0, n1 = n1r[0, 0, HALF : HALF + 1], n1r[1, 0, HALF : HALF + 1]
                    next_d = n0 * n1
                tot[i], dec[i] = d1 * s0[i] + s1_, d0 * d1
                pre[i], pre_d[i] = jnp.zeros((HALF, 128), F32), jnp.ones((1, 128), F32)
                got, got_d = n1 * n1r[0, i, 0:HALF] + n1r[1, i, 0:HALF], next_d
            else:
                rounds[r][i].wait_recv()
                got, got_d = sc["br"][2 * r + i, 0:HALF], sc["br"][2 * r, HALF : HALF + 1]
            tot[i] = pick(later, dec[i] * got + tot[i], got_d * tot[i] + got)
            dec[i] = dec[i] * got_d
            if r < 2:
                send_round(r + 1, i)
            else:
                fill(xs.at[i], tot[i], dec[i])
                x_copies[i] = [
                    remote(sent(xs.at[i], i), sent(xr.at[i, x], i), {"seq": seq_of(p, z, c)}) for p in x_peers
                ]
                for cp, p in zip(x_copies[i], x_peers):
                    pl.when(p > x)(cp.start)
            pre[i] = pick(later, pre_d[i] * got + pre[i], pre[i])
            pre_d[i] = pick(later, got_d * pre_d[i], pre_d[i])
        if r < 2:
            h = r
            diff = cum[:, 64 * h : 64 * h + 1] - cum_t[64 * h : 64 * h + 1, :]
            wts = jnp.where(allowed, jnp.exp(jnp.where(allowed, diff, 0.0)) * pairs, 0.0)
            local = local + dot3(wts, jnp.where(first if h == 0 else ~first, stepped, 0.0))
    sc["loc"][...] = local
    sc["gat"][...] = silu(gate)
    sc["cue"][...] = jnp.exp(cum)
    wo2_copies.wait_recv()
    ks, kr = sc["ks"], sc["kr"]
    k_copies, mine = Group(kr), []
    for i in chunks:
        for cp, p in zip(x_copies[i], x_peers):
            pl.when(p < x)(cp.wait_recv)
        row_in = jnp.zeros((HALF, 128), F32)
        for n in range(NX - 1):
            row_in = pick(as_int(x > n), xr[0, n, HALF : HALF + 1] * row_in + xr[i, n, 0:HALF], row_in)
        k0 = pre_d[i] * row_in + pre[i]
        k1 = d0 * k0 + s0[i]
        ks[i] = pick(c, k0, k1)
        k_copies.start(ks.at[i], kr.at[i], other_core)
        mine.append(pick(c, k1, k0))
    k_copies.wait_recv()
    got = jnp.concatenate([kr[0], kr[1]], axis=0)
    mine = jnp.concatenate(mine, axis=0)
    carried = jnp.concatenate([pick(c, got, mine), pick(c, mine, got)], axis=0)
    ch, cl = split2(carried)
    chh = jnp.concatenate([ch, ch], axis=0)
    gs, gr = sc["gs"], sc["gr"]

    def finish(rows):
        rd = sc["rd"][rows, :]
        y2 = sc["loc"][rows, :] + (mm(rd, chh) + mm(rd[:, :128], cl)) * sc["cue"][rows, :]
        w = y2 * sc["gat"][rows, :]
        return w * head_scale(w) * vm["on2"][...]

    def rows_of(p):
        return pl.ds(pl.multiple_of(64 * p, 64), 64)

    far = y_peers[0]
    gf = sc["gf"]
    gf[...] = finish(rows_of(far))
    g_copies = [remote(gf, gr.at[y], {"head": far})]
    g_copies[0].start()
    gs[...] = finish(pl.ds(0, T))
    for p in y_peers[1:]:
        g_copies.append(remote(gs.at[rows_of(p)], gr.at[y], {"head": p}))
        g_copies[-1].start()
    wo2 = sc["wo2"]
    out = mir[rows_of(y), :] + dot3_short(gs[rows_of(y), :], wo2[y])
    for cp, p in zip(g_copies[1:] + g_copies[:1], y_peers[1:] + y_peers[:1]):
        cp.wait_recv()
        out = out + dot3_short(gr[p], wo2[p])
    out_ref[...] = out

    for cp in (
        [log_copies, tab_copies, tok_copies, wo1_copies, wo1_passed, wo2_copies, z_own]
        + e1 + rounds[1] + rounds[2] + [k_copies] + g_copies
    ):
        cp.wait_send()
    for cond, cp in (
        (low, tok_low), (low, z_low), (high, tokm_copy), (high, z_down), (relay, tok_up), (relay, z_up)
    ):
        pl.when(cond)(cp.wait_send)
    for i in chunks:
        for cp, p in zip(x_copies[i], x_peers):
            pl.when(p > x)(cp.wait_send)


def per_device(*args):
    a = dict(zip(NAMES, args))
    for n in ("sp1", "sp2"):
        a[n] = a[n].T
    flat = [a[n].reshape(s) for n, s in zip(NAMES, SHAPES)]
    return pl.pallas_call(
        kernel,
        out_shape=pltpu.VMEM((64, 256), F32),
        in_specs=[pl.BlockSpec(memory_space=pltpu.HBM)] * N_IN,
        out_specs=pl.BlockSpec(memory_space=pltpu.VMEM),
        scratch_shapes=[pltpu.VMEM(s, t) for s, t in zip(SHAPES, TYPES)]
        + [pltpu.VMEM(s, t) for _, s, t in SCRATCH]
        + [
            pltpu.SemaphoreType.DMA((N_IN + 1 + N_MORE,)),
            pltpu.SemaphoreType.DMA((N_RECV,)),
            pltpu.SemaphoreType.REGULAR,
        ],
        compiler_params=pltpu.CompilerParams(
            collective_id=0, has_side_effects=True, vmem_limit_bytes=60 * 2**20
        ),
    )(*flat)


def solution(mesh):
    tokens = P(("rep", "seq"))
    layer = (P(), P(None, None, "head"), P(), P(None, "head")) + (P("head"),) * 4 + (P("head", None),)
    in_specs = (tokens, P(), P()) + layer + layer
    return jax.shard_map(
        per_device,
        mesh=mesh,
        in_specs=in_specs,
        out_specs=P(("rep", "seq", "head"), None),
        check_vma=False,
    )
```

```python
import jax
import jax.numpy as jnp
from jax import lax
from jax.experimental import pallas as pl
from jax.experimental.pallas import tpu as pltpu
from jax.sharding import PartitionSpec as P

F32, BF = jnp.float32, jnp.bfloat16
MESH = pl.DeviceIdType.MESH
EPS = 1e-05
NX, NZ, NC, NY = 4, 8, 2, 4
T = 256
V = 16


def mm(a, b):
    return lax.dot_general(a, b, (((1,), (0,)), ((), ())), preferred_element_type=F32)


def mmt(a, b):
    return lax.dot_general(a, b, (((1,), (1,)), ((), ())), preferred_element_type=F32)


def split2(a):
    hi = a.astype(BF)
    return hi, (a - hi.astype(F32)).astype(BF)


def split3(a):
    hi = a.astype(BF)
    rest = a - hi.astype(F32)
    mid = rest.astype(BF)
    return hi, mid, (rest - mid.astype(F32)).astype(BF)


def dot3(a, b, f=mm):
    ah, al = a if isinstance(a, tuple) else split2(a)
    bh, bl = b if isinstance(b, tuple) else split2(b)
    return f(ah, bh) + (f(ah, bl) + f(al, bh))


def dot3_short(a, b):
    ah, al = a if isinstance(a, tuple) else split2(a)
    bh, bl = b if isinstance(b, tuple) else split2(b)
    return mm(jnp.concatenate([ah, al], axis=1), jnp.concatenate([bh, bh], axis=0)) + mm(ah, bl)


def exact_left(a, b):
    h, l = split2(b)
    return mm(a, h) + mm(a, l)


def exact_right(a, b):
    h, m, l = split3(a)
    return mm(h, b) + (mm(m, b) + mm(l, b))


def iota(shape, dim):
    return lax.broadcasted_iota(jnp.int32, shape, dim)


def softplus(a):
    return jnp.maximum(a, 0.0) + jnp.log1p(jnp.exp(-jnp.abs(a)))


def silu(a):
    return a / (1.0 + jnp.exp(-a))


def rms(a, gain):
    return a * lax.rsqrt(jnp.mean(a * a, axis=-1, keepdims=True) + EPS) * gain


def xor(a, k, bits):
    out = a
    for i in range(bits):
        if k >> i & 1:
            out = out + (1 << i) * (1 - 2 * (a // (1 << i) % 2))
    return out


def pick(flag, a, b):
    return jnp.where(jnp.full(a.shape, flag, jnp.int32) > 0, a, b)


def as_int(cond):
    return jnp.where(cond, 1, 0)


def halves(pair):
    return jnp.where(iota((1, 128), 1) < 64, pair[:, 0:1], pair[:, 1:2])


def scan_rows(coef, decay, reverse):
    rows = iota(coef.shape, 0)
    k = 1
    while k < T:
        if reverse:
            inside = rows < T - k
            shifted_c, shifted_d = pltpu.roll(coef, T - k, 0), pltpu.roll(decay, T - k, 0)
        else:
            inside = rows >= k
            shifted_c, shifted_d = pltpu.roll(coef, k, 0), pltpu.roll(decay, k, 0)
        coef = coef + jnp.where(inside, decay * shifted_c, 0.0)
        decay = jnp.where(inside, decay * shifted_d, decay)
        k *= 2
    return coef, decay


NAMES = (
    "tok", "emb", "comp",
    "pn1", "ip1", "sm1", "sp1", "sb1", "ra1", "sk1", "on1", "op1",
    "pn2", "ip2", "sm2", "sp2", "sb2", "ra2", "sk2", "on2", "op2",
)
SHAPES = (
    (1, T), (V, 256), (1, 256),
    (1, 256), (512, 128), (512, 128), (2, 256), (1, 2), (1, 2), (1, 2), (1, 128), (128, 256),
    (1, 256), (512, 128), (512, 128), (2, 256), (1, 2), (1, 2), (1, 2), (1, 128), (128, 256),
)
TYPES = (jnp.int32, F32, jnp.int32) + (F32,) * 18
N_IN = len(NAMES)
TAB = 72
HALF = 32
MSG = HALF + 8

SCRATCH = (
    ("tokbuf", (8, 1, T), jnp.int32),
    ("tokr", (4, 1, T), jnp.int32),
    ("tokm", (1, T), jnp.int32),
    ("lsend", (8, 128), F32),
    ("ltab", (NY, 8, 128), F32),
    ("tsend", (TAB, 128), F32),
    ("ytab", (NY, TAB, 128), F32),
    ("wo1", (NY, 128, 256), F32),
    ("wo1s", (128, 256), F32),
    ("wo2", (NY, 128, 256), F32),
    ("ztile", (8, 128), F32),
    ("zbuf", (NZ, 8, 128), F32),
    ("mir", (T, 256), F32),
    ("st", (128, 128), F32),
    ("e1s", (2, MSG, 128), F32),
    ("e1o", (2, MSG, 128), F32),
    ("e1r", (2, MSG, 128), F32),
    ("n1r", (NC, 2, MSG, 128), F32),
    ("bs", (6, MSG, 128), F32),
    ("br", (6, MSG, 128), F32),
    ("xs", (2, MSG, 128), F32),
    ("xr", (2, NX, MSG, 128), F32),
    ("ks", (2, HALF, 128), F32),
    ("kr", (2, HALF, 128), F32),
    ("rd", (T, 256), BF),
    ("loc", (T, 128), F32),
    ("gat", (T, 128), F32),
    ("cue", (T, 128), F32),
    ("gs", (T, 128), F32),
    ("gf", (64, 128), F32),
    ("gr", (NY, 64, 128), F32),
)
N_RECV = 30
N_MORE = 8


def kernel(*refs):
    hbm = dict(zip(NAMES, refs[:N_IN]))
    out_ref = refs[N_IN]
    vm = dict(zip(NAMES, refs[N_IN + 1 :]))
    sc = {s[0]: r for s, r in zip(SCRATCH, refs[N_IN + 1 + N_IN :])}
    in_sem, recv_sem, present = refs[-3:]

    seq, y = lax.axis_index("seq"), lax.axis_index("head")
    x, z, c = seq // (NZ * NC), seq // NC % NZ, seq % NC
    xc = x * NC + c
    xm, zm = NX - 1 - x, NZ - 1 - z

    def seq_of(xi, zi, ci):
        return (xi * NZ + zi) * NC + ci

    y_peers = [xor(y, k, 2) for k in (2, 1, 3)]
    xc_peers = [xor(xc, k, 3) for k in (7, 4, 5, 2, 3, 6, 1)]
    z_group = [xor(z, k, 3) for k in (3, 2, 1)]
    low, high, relay, above = z < 4, z >= 4, z == 4, z > 4

    barrier = pltpu.get_barrier_semaphore()

    def greet(where):
        pl.semaphore_signal(barrier, inc=1, device_id=where, device_id_type=MESH)

    for p in z_group:
        greet({"seq": seq_of(x, p, c)})
    pl.when(z == 3)(lambda: greet({"seq": seq_of(x, 4, c)}))
    pl.when(relay)(lambda: greet({"seq": seq_of(x, 3, c)}))
    for p in xc_peers:
        greet({"seq": seq_of(p // NC, z, p % NC)})
    for p in y_peers:
        greet({"head": p})

    first_loads = ("tok", "emb", "pn1", "sp1", "sb1", "ra1")
    other_loads = tuple(n for n in NAMES if n not in first_loads)
    loads = {
        n: pltpu.make_async_copy(hbm[n], vm[n], in_sem.at[i])
        for i, n in enumerate(first_loads + other_loads)
    }
    for n in first_loads:
        loads[n].start()
    own_tok = pltpu.make_async_copy(hbm["tok"], sc["tokbuf"].at[xc], in_sem.at[N_IN])
    own_tok.start()
    for n in other_loads:
        loads[n].start()

    used = [0, 0]

    def next_sems():
        used[0] += 1
        used[1] += 1
        assert used[1] <= N_RECV
        assert used[0] <= N_IN + 1 + N_MORE
        return in_sem.at[used[0] - 1], recv_sem.at[used[1] - 1]

    def remote(src, dst, where, sems=None):
        send, recv = sems or next_sems()
        return pltpu.make_async_remote_copy(
            src_ref=src, dst_ref=dst, send_sem=send, recv_sem=recv,
            device_id=where, device_id_type=MESH,
        )

    class Group:
        def __init__(self, like, sent_like=None):
            self.send, self.recv = self.sems = next_sems()
            self.like = like
            self.sent_like = like if sent_like is None else sent_like

        def start(self, src, dst, where):
            remote(src, dst, where, self.sems).start()

        def wait_recv(self):
            pltpu.make_async_copy(self.like, self.like, self.recv).wait()

        def wait_send(self):
            pltpu.make_async_copy(self.sent_like, self.sent_like, self.send).wait()

    for n in first_loads:
        loads[n].wait()

    lane = iota((1, 128), 1)
    emb = vm["emb"][...]
    normed = rms(emb, vm["pn1"][...])
    sp, sb, ra = vm["sp1"][...], vm["sb1"][...], vm["ra1"][...]
    even = iota((8, 128), 0) % 2 == 0
    sp_r = jnp.where(iota((8, 256), 0) % 2 == 0, sp[0:1], sp[1:2])
    log_r = -jnp.where(even, ra[:, 0:1], ra[:, 1:2]) * softplus(
        dot3(sp_r, jnp.concatenate([normed] * 8, axis=0), mmt)
        + jnp.where(even, sb[:, 0:1], sb[:, 1:2])
    )
    lsend, tsend = sc["lsend"], sc["tsend"]
    lsend[...] = log_r

    def tell(p):
        pl.semaphore_signal(
            present, inc=1, device_id={"seq": seq_of(x, p, c)}, device_id_type=MESH
        )

    across = (z == 3) | relay
    pl.when(across)(lambda: pl.semaphore_wait(barrier, 14))
    pl.when(jnp.logical_not(across))(lambda: pl.semaphore_wait(barrier, 13))

    @pl.when(z == 3)
    def _():
        for p in (4, 0, 1, 2):
            tell(p)

    @pl.when(relay)
    def _():
        pl.semaphore_wait(present, 1)
        for p in (7, 6, 5):
            tell(p)

    ltab, ytab, tokbuf = sc["ltab"], sc["ytab"], sc["tokbuf"]
    log_copies = Group(ltab.at[pl.ds(0, NY - 1)])
    tok_first = Group(tokbuf.at[pl.ds(0, 1)])
    tok_copies = Group(tokbuf.at[pl.ds(0, 6)])
    tok_first.start(vm["tok"], tokbuf.at[xc], {"seq": seq_of(xc_peers[0] // NC, z, xc_peers[0] % NC)})
    for p in y_peers:
        log_copies.start(lsend, ltab.at[y], {"head": p})
    for p in xc_peers[1:]:
        tok_copies.start(vm["tok"], tokbuf.at[xc], {"seq": seq_of(p // NC, z, p % NC)})
    ltab[pl.ds(y, 1)] = log_r[None]

    own_tok.wait()
    for n in other_loads:
        loads[n].wait()
    w1 = vm["ip1"]
    gate_w, inner_w = w1[pl.ds(0, 256, stride=2), :], w1[pl.ds(1, 256, stride=2), :]
    s1 = vm["sm1"]
    write_w, read_w = s1[pl.ds(0, 256, stride=2), :], s1[pl.ds(1, 256, stride=2), :]
    normed2 = split2(normed)
    table = dot3(normed2, jnp.concatenate([gate_w, inner_w, write_w, read_w], axis=1))
    gate_t, inner_t, write_t, read_t = (table[:, 128 * i : 128 * (i + 1)] for i in range(4))
    sk = vm["sk1"][...]
    r128 = iota((128, 256), 0)
    sp_p = jnp.where(r128 < 64, sp[0:1], sp[1:2])
    sp_alt = jnp.where(r128 // 16 % 2 == 0, sp[0:1], sp[1:2])
    logits = dot3(normed2, jnp.concatenate([sp_p, sp_alt], axis=0), mmt)
    step_p = softplus(logits[:, :128] + halves(sb))
    alt = lane // 16 % 2 == 0
    log_alt = -jnp.where(alt, ra[:, 0:1], ra[:, 1:2]) * softplus(
        logits[:, 128:] + jnp.where(alt, sb[:, 0:1], sb[:, 1:2])
    )
    tsend[0:16] = step_p * inner_t
    tsend[16:32] = halves(sk) * inner_t
    tsend[32:48] = silu(gate_t)
    tsend[48:64] = log_alt
    tsend[64:72] = jnp.broadcast_to(vm["on1"][...], (8, 128))
    tab_copies = Group(ytab.at[pl.ds(0, NY - 1)])
    for p in y_peers:
        tab_copies.start(tsend, ytab.at[y], {"head": p})
    g_tab = dot3(read_t, jnp.concatenate([write_t] * 8, axis=0), mmt)
    ytab[pl.ds(y, 1)] = tsend[...][None]
    sc["wo2"][pl.ds(y, 1)] = vm["op2"][...][None]

    tri_r, tri_c = iota((256, 256), 0), iota((256, 256), 1)
    one = jnp.ones((), F32)

    def mask_bf(cond):
        return jnp.where(cond, one, 0.0 * one).astype(BF)

    perm = mask_bf(vm["comp"][...] == tri_r)
    lower_tri = mask_bf(tri_r >= tri_c)
    count_mat = jnp.concatenate(
        [mask_bf(tri_r > tri_c), mask_bf(tri_r < tri_c), jnp.ones((256, 128), BF)], axis=1
    )
    ls, lr = iota((128, 512), 1), iota((128, 512), 0)
    spread = mask_bf((lr // 16 == ls % 128 // 16) & (lr % 16 == ls // 128))
    spread = jnp.concatenate([spread, spread], axis=0)
    qm = xm * NZ + zm
    q, q2 = iota((32, 32), 0), iota((32, 32), 1)
    between = mask_bf(((q2 > q) & (q2 < qm)) | ((q2 < q) & (q2 > qm)))
    r2, l2 = iota((128, 128), 0), iota((128, 128), 1)
    same_head = jnp.where(r2 // 64 == l2 // 64, 1.0 / 64, 0.0).astype(BF)
    same_head = jnp.concatenate([same_head, same_head], axis=0)
    rev = mask_bf(tri_r + tri_c == T - 1)
    wo1s = sc["wo1s"]
    wo1s[...] = exact_right(vm["op1"][...], perm)
    sc["wo1"][pl.ds(y, 1)] = wo1s[...][None]
    w2, s2 = vm["ip2"], vm["sm2"]
    gain = jnp.broadcast_to(vm["pn2"][...], (128, 256)).T
    w2_early = split2(
        jnp.concatenate([w2[pl.ds(1, 256, stride=2), :] * gain, s2[pl.ds(0, 256, stride=2), :] * gain], axis=1)
    )
    w2_late = split2(
        jnp.concatenate([w2[pl.ds(0, 256, stride=2), :] * gain, s2[pl.ds(1, 256, stride=2), :] * gain], axis=1)
    )
    sp2 = vm["sp2"][...] * vm["pn2"][...]
    sp2_p = split2(jnp.where(r128 < 64, sp2[0:1], sp2[1:2]))
    emb_p = mm(jnp.concatenate(split3(emb), axis=0), perm).astype(BF)

    core_rows = pl.ds(pl.multiple_of(64 * c, 64), 64)
    wo1_copies = Group(sc["wo1"].at[pl.ds(0, NY - 1), pl.ds(0, 64)])
    for p in y_peers:
        wo1_copies.start(wo1s.at[core_rows], sc["wo1"].at[y, core_rows], {"head": p})
    tok_first.wait_recv()
    pl.when(jnp.logical_not(across))(lambda: pl.semaphore_wait(present, 1))
    tokr, tokm = sc["tokr"], sc["tokm"]
    to_gate = {"seq": seq_of(x, 4, c)}
    mirror_tok = tokbuf.at[xm * NC + 1 - c]
    tokm_copy = remote(mirror_tok, tokm, {"seq": seq_of(x, zm, c)})
    tok_low = Group(tokr, tokr.at[pl.ds(0, 1)])
    pl.when(high)(tokm_copy.start)
    pl.when(low)(lambda: tok_low.start(mirror_tok, tokr.at[z], to_gate))
    tok_copies.wait_recv()
    log_copies.wait_recv()
    r16 = iota((V, T), 0)
    onehot = jnp.concatenate([as_int(tokbuf[b] == r16) for b in range(8)], axis=0)
    onehot = onehot.astype(F32).astype(BF)
    counts = mm(onehot, count_mat).astype(BF)
    row8 = iota((8, 128), 0)
    log_hv = ltab[0]
    for i in range(1, NY):
        log_hv = jnp.where(row8 // 2 == i, ltab[i], log_hv)
    r64, l64 = iota((64, 128), 0), iota((64, 128), 1)
    log_bd = jnp.where(r64 // 8 == l64 // 16, jnp.concatenate([log_hv] * 8, axis=0), 0.0)
    cums = mm(
        jnp.concatenate(split2(log_bd), axis=1), jnp.concatenate([counts, counts], axis=0)
    )
    weight = jnp.exp(cums[:, :512])
    weight = jnp.concatenate([weight[:, :256], weight[:, 256:]], axis=0)
    wh, wl = split2(weight)
    sums = mmt(wh, onehot) + mmt(wl, onehot)
    sums = jnp.where(r2 // 8 % 8 == l2 // 16, sums, 0.0)
    for shift in (64, 32, 16):
        sums = sums + pltpu.roll(sums, shift, 1)
    sums = jnp.where(r2 % 8 == l2 // 16, sums, 0.0)
    totals = jnp.where(r64 % 8 == l64 // 16, cums[:, 512:], 0.0)

    def fold(a, i):
        return jnp.sum(a[8 * i : 8 * i + 8], axis=0, keepdims=True)

    cf = [fold(sums, b) for b in range(8)]
    cb = [fold(sums, 8 + b) for b in range(8)]
    ld = [fold(totals, b) for b in range(8)]
    cf_pair = [jnp.exp(ld[2 * i + 1]) * cf[2 * i] + cf[2 * i + 1] for i in range(NX)]
    cb_pair = [jnp.exp(ld[2 * i]) * cb[2 * i + 1] + cb[2 * i] for i in range(NX)]
    ld_pair = [ld[2 * i] + ld[2 * i + 1] for i in range(NX)]
    rows = [pick(as_int(xm >= i), cf_pair[i], cb_pair[i]) for i in range(NX)]
    own_b, sib, sib_ld, packed = cb_pair[0], cf[0], ld[0], ld_pair[0]
    for i in range(NX):
        here = as_int(xm == i)
        own_b = pick(here, cb_pair[i], own_b)
        sib = pick(here, pick(c, cb[2 * i + 1], cf[2 * i]), sib)
        sib_ld = pick(here, pick(c, ld[2 * i + 1], ld[2 * i]), sib_ld)
        packed = jnp.where(lane % 16 == i, ld_pair[i], packed)
    tile = jnp.concatenate(rows + [own_b, packed, sib, sib_ld], axis=0)
    ztile, zbuf = sc["ztile"], sc["zbuf"]
    ztile[...] = tile
    tiles = zbuf.at[pl.ds(0, 4)]
    z_own = Group(zbuf.at[pl.ds(0, 3)])
    z_down = Group(tiles)
    z_low = Group(tiles, zbuf.at[pl.ds(0, 1)])
    z_up = Group(tiles, sc["loc"].at[pl.ds(0, 96)])
    tok_up = Group(tokm, tokr.at[pl.ds(0, 3)])
    pl.when(low)(lambda: z_low.start(ztile, zbuf.at[z], to_gate))

    @pl.when(high)
    def _():
        for p in range(4):
            z_down.start(ztile, zbuf.at[z], {"seq": seq_of(x, p, c)})

    for p in z_group:
        z_own.start(ztile, zbuf.at[z], {"seq": seq_of(x, p, c)})

    @pl.when(relay)
    def _():
        tok_low.wait_recv()
        for p in range(3):
            tok_up.start(tokr.at[p], tokm, {"seq": seq_of(x, NZ - 1 - p, c)})
        z_low.wait_recv()
        for p in (7, 6, 5):
            for n in range(4):
                z_up.start(zbuf.at[n], zbuf.at[n], {"seq": seq_of(x, p, c)})
        tokm[...] = tokr[3]

    zbuf[pl.ds(z, 1)] = tile[None]

    def lanes_of(a, b):
        return jnp.concatenate([ytab[i, a:b] for i in range(NY)], axis=1)

    tab_copies.wait_recv()
    row16 = iota((V, 128), 0)
    l16 = iota((V, 128), 1)
    log_t = ytab[0, 48:64]
    for i in range(1, NY):
        log_t = jnp.where(l16 // 32 == i, ytab[i, 48:64], log_t)
    eye_t = jnp.where(row16 == l16 % 16, 1.0, 0.0)
    tables = jnp.concatenate([lanes_of(32, 48), lanes_of(16, 32), g_tab, jnp.exp(log_t), eye_t], axis=1)
    tables = jnp.concatenate([jnp.concatenate(split3(tables), axis=0), emb_p], axis=1)
    inner_rep = jnp.concatenate([lanes_of(0, 16)] * 8, axis=0)
    bd = iota((128, 512), 0) // 16 == iota((128, 512), 1) // 64
    x_bd = split2(jnp.where(bd, inner_rep, 0.0))
    outnorm_all = lanes_of(64, 65)
    other_core = {"seq": seq_of(x, z, 1 - c)}
    wo1_passed = Group(sc["wo1"].at[pl.ds(0, NY - 1), pl.ds(0, 64)])
    wo1_copies.wait_recv()
    for p in y_peers:
        half = sc["wo1"].at[p, core_rows]
        wo1_passed.start(half, half, other_core)
    wo2_copies = Group(sc["wo2"].at[pl.ds(0, NY - 1)])
    for p in y_peers:
        wo2_copies.start(vm["op2"], sc["wo2"].at[y], {"head": p})
    pl.when(low)(tokm_copy.wait_recv)
    pl.when(above)(tok_up.wait_recv)
    hot_m = as_int(sc["tokm"][...] == r16).astype(F32).astype(BF)
    hot_rev = mmt(rev, jnp.concatenate([hot_m] * 3, axis=0)).astype(BF)
    taken = mm(hot_rev, tables)
    silu_g, skip_x = taken[:, :512], taken[:, 512:1024]
    g_row, decay, hot = taken[:, 1024:1152], taken[:, 1152:1280], taken[:, 1280:1408]
    embedded = taken[:, 1408:]
    up_c, up_p = scan_rows(hot, decay, False)
    dn_c, dn_p = scan_rows(hot, decay, True)

    z_own.wait_recv()
    pl.when(low)(z_down.wait_recv)
    pl.when(above)(z_up.wait_recv)
    ld_all = mm(
        jnp.concatenate(split2(zbuf[:, 5, :]), axis=1), spread
    )
    ld_all = jnp.concatenate([ld_all[:, 128 * i : 128 * i + 128] for i in range(NX)], axis=0)
    share = jnp.exp(exact_left(between, ld_all))
    zrow = iota((8, 128), 0)
    coefs = jnp.concatenate(
        [
            jnp.where((zrow > zm) & (jnp.full((8, 128), xm, jnp.int32) == i), zbuf[:, 4, :], zbuf[:, i, :])
            for i in range(NX)
        ],
        axis=0,
    )
    terms = share * coefs
    qrow = iota((32, 128), 0)
    carry_f = jnp.sum(jnp.where(qrow < qm, terms, 0.0), axis=0, keepdims=True)
    carry_b = jnp.sum(jnp.where(qrow > qm, terms, 0.0), axis=0, keepdims=True)
    at_m = zbuf[pl.ds(zm, 1)].reshape(8, 128)
    sib, sib_d = at_m[6:7], jnp.exp(at_m[7:8])
    carry_f = pick(c, carry_f, sib_d * carry_f + sib)
    carry_b = pick(c, sib_d * carry_b + sib, carry_b)
    coef = jnp.concatenate([up_c + up_p * carry_b, dn_c + dn_p * carry_f], axis=0)
    coef = coef * jnp.concatenate([g_row] * 2, axis=0)
    ssm = dot3_short(coef, x_bd)

    def head_scale(w):
        parts = []
        for i in range(w.shape[1] // 128):
            parts.append(mm(jnp.concatenate(split2(w[:, 128 * i : 128 * i + 128] ** 2), axis=1), same_head))
        sq = parts[0] if len(parts) == 1 else jnp.concatenate(parts, axis=1)
        return lax.rsqrt(sq + EPS)

    wo1_passed.wait_recv()
    wo1_p = split2(sc["wo1"][...].reshape(512, 256))
    w_up = (ssm[:T] + skip_x) * silu_g
    w_dn = (ssm[T:] + skip_x) * silu_g
    mixed = (w_up * head_scale(w_up) + w_dn * head_scale(w_dn)) * outnorm_all
    mirrored = embedded + dot3(mixed, wo1_p)
    mir = sc["mir"]
    mir[...] = mirrored

    n2 = split2(mirrored)
    rms2 = lax.rsqrt(jnp.mean(mirrored * mirrored, axis=-1, keepdims=True) + EPS)
    step = softplus(dot3(n2, sp2_p, mmt) * rms2 + halves(vm["sb2"][...]))
    both = dot3(n2, w2_early) * rms2
    inner, write = both[:, :128], both[:, 128:]
    cum = exact_left(lower_tri, -halves(vm["ra2"][...]) * step)
    end = cum[T - 1 : T]
    stepped = inner * step
    write_t2 = split2(write.T)
    state = dot3(write_t2, stepped * jnp.exp(end - cum))
    own_d = jnp.exp(end)
    st, e1s, e1r = sc["st"], sc["e1s"], sc["e1r"]
    st[...] = state
    chunks = range(2)

    def fill(buf, rows, decay):
        buf[0:HALF] = rows
        buf[HALF:MSG] = jnp.broadcast_to(decay, (8, 128))

    def sent(ref, i):
        return ref.at[pl.ds(0, HALF + 1 if i == 0 else HALF)]

    def part(core, i):
        return st[pl.ds(pl.multiple_of(64 * core + HALF * i, HALF), HALF), :]

    e1o, n1r = sc["e1o"], sc["n1r"]
    next_same = {"seq": seq_of(x, xor(z, 1, 3), c)}
    next_other = {"seq": seq_of(x, xor(z, 1, 3), 1 - c)}
    e1 = [Group(sc["bs"].at[pl.ds(0, 3), pl.ds(0, HALF + 1 - i)]) for i in chunks]
    for i in chunks:
        fill(e1s.at[i], part(1 - c, i), own_d)
        fill(e1o.at[i], part(c, i), own_d)
        e1[i].start(sent(e1s.at[i], i), sent(n1r.at[c, i], i), next_other)
        e1[i].start(sent(e1o.at[i], i), sent(n1r.at[c, i], i), next_same)
        e1[i].start(sent(e1s.at[i], i), sent(e1r.at[i], i), other_core)

    s0, tot, dec, pre, pre_d = [None] * 2, [None] * 2, [None] * 2, [None] * 2, [None] * 2
    rounds = [[None] * 2 for _ in range(3)]

    def send_round(r, i):
        bs, br = sc["bs"].at[2 * r + i], sc["br"].at[2 * r + i]
        fill(bs, tot[i], dec[i])
        rounds[r][i] = remote(
            sent(bs, i), sent(br, i), {"seq": seq_of(x, xor(z, 1 << r, 3), c)}
        )
        rounds[r][i].start()

    both = dot3(n2, w2_late) * rms2
    gate, read = both[:, :128], both[:, 128:]
    read2 = split2(read)
    sc["rd"][...] = jnp.concatenate(read2, axis=1)
    pairs = dot3_short(read2, write_t2)
    cum_t = cum.T
    allowed = tri_r >= tri_c
    local = halves(vm["sk2"][...]) * inner
    first = iota((T, 128), 1) < 64
    xs, xr = sc["xs"], sc["xr"]
    x_peers = [xor(x, k, 2) for k in (2, 1, 3)]
    x_copies = [[], []]
    for r in range(3):
        later = z // (1 << r) % 2
        for i in chunks:
            if r == 0:
                e1[i].wait_recv()
                own, got = part(c, i), e1r[i, 0:HALF]
                s0[i], s1_ = pick(c, got, own), pick(c, own, got)
                if i == 0:
                    got_d = e1r[0, HALF : HALF + 1]
                    d0, d1 = pick(c, got_d, own_d), pick(c, own_d, got_d)
                    n0, n1 = n1r[0, 0, HALF : HALF + 1], n1r[1, 0, HALF : HALF + 1]
                    next_d = n0 * n1
                tot[i], dec[i] = d1 * s0[i] + s1_, d0 * d1
                pre[i], pre_d[i] = jnp.zeros((HALF, 128), F32), jnp.ones((1, 128), F32)
                got, got_d = n1 * n1r[0, i, 0:HALF] + n1r[1, i, 0:HALF], next_d
            else:
                rounds[r][i].wait_recv()
                got, got_d = sc["br"][2 * r + i, 0:HALF], sc["br"][2 * r, HALF : HALF + 1]
            tot[i] = pick(later, dec[i] * got + tot[i], got_d * tot[i] + got)
            dec[i] = dec[i] * got_d
            if r < 2:
                send_round(r + 1, i)
            else:
                fill(xs.at[i], tot[i], dec[i])
                x_copies[i] = [
                    remote(sent(xs.at[i], i), sent(xr.at[i, x], i), {"seq": seq_of(p, z, c)}) for p in x_peers
                ]
                for cp, p in zip(x_copies[i], x_peers):
                    pl.when(p > x)(cp.start)
            pre[i] = pick(later, pre_d[i] * got + pre[i], pre[i])
            pre_d[i] = pick(later, got_d * pre_d[i], pre_d[i])
        if r < 2:
            h = r
            diff = cum[:, 64 * h : 64 * h + 1] - cum_t[64 * h : 64 * h + 1, :]
            wts = jnp.where(allowed, jnp.exp(jnp.where(allowed, diff, 0.0)) * pairs, 0.0)
            local = local + dot3(wts, jnp.where(first if h == 0 else ~first, stepped, 0.0))
    sc["loc"][...] = local
    sc["gat"][...] = silu(gate)
    sc["cue"][...] = jnp.exp(cum)
    wo2_copies.wait_recv()
    ks, kr = sc["ks"], sc["kr"]
    k_copies, mine = Group(kr), []
    for i in chunks:
        for cp, p in zip(x_copies[i], x_peers):
            pl.when(p < x)(cp.wait_recv)
        row_in = jnp.zeros((HALF, 128), F32)
        for n in range(NX - 1):
            row_in = pick(as_int(x > n), xr[0, n, HALF : HALF + 1] * row_in + xr[i, n, 0:HALF], row_in)
        k0 = pre_d[i] * row_in + pre[i]
        k1 = d0 * k0 + s0[i]
        ks[i] = pick(c, k0, k1)
        k_copies.start(ks.at[i], kr.at[i], other_core)
        mine.append(pick(c, k1, k0))
    k_copies.wait_recv()
    got = jnp.concatenate([kr[0], kr[1]], axis=0)
    mine = jnp.concatenate(mine, axis=0)
    carried = jnp.concatenate([pick(c, got, mine), pick(c, mine, got)], axis=0)
    ch, cl = split2(carried)
    chh = jnp.concatenate([ch, ch], axis=0)
    gs, gr = sc["gs"], sc["gr"]

    def finish(rows):
        rd = sc["rd"][rows, :]
        y2 = sc["loc"][rows, :] + (mm(rd, chh) + mm(rd[:, :128], cl)) * sc["cue"][rows, :]
        w = y2 * sc["gat"][rows, :]
        return w * head_scale(w) * vm["on2"][...]

    def rows_of(p):
        return pl.ds(pl.multiple_of(64 * p, 64), 64)

    far = y_peers[0]
    gf = sc["gf"]
    gf[...] = finish(rows_of(far))
    g_copies = [remote(gf, gr.at[y], {"head": far})]
    g_copies[0].start()
    gs[...] = finish(pl.ds(0, T))
    for p in y_peers[1:]:
        g_copies.append(remote(gs.at[rows_of(p)], gr.at[y], {"head": p}))
        g_copies[-1].start()
    wo2 = sc["wo2"]
    out = mir[rows_of(y), :] + dot3_short(gs[rows_of(y), :], wo2[y])
    for cp, p in zip(g_copies[1:] + g_copies[:1], y_peers[1:] + y_peers[:1]):
        cp.wait_recv()
        out = out + dot3_short(gr[p], wo2[p])
    out_ref[...] = out

    for cp in (
        [log_copies, tab_copies, tok_first, tok_copies, wo1_copies, wo1_passed, wo2_copies, z_own]
        + e1 + rounds[1] + rounds[2] + [k_copies] + g_copies
    ):
        cp.wait_send()
    for cond, cp in (
        (low, tok_low), (low, z_low), (high, tokm_copy), (high, z_down), (relay, tok_up), (relay, z_up)
    ):
        pl.when(cond)(cp.wait_send)
    for i in chunks:
        for cp, p in zip(x_copies[i], x_peers):
            pl.when(p > x)(cp.wait_send)


def per_device(*args):
    a = dict(zip(NAMES, args))
    for n in ("sp1", "sp2"):
        a[n] = a[n].T
    flat = [a[n].reshape(s) for n, s in zip(NAMES, SHAPES)]
    return pl.pallas_call(
        kernel,
        out_shape=pltpu.VMEM((64, 256), F32),
        in_specs=[pl.BlockSpec(memory_space=pltpu.HBM)] * N_IN,
        out_specs=pl.BlockSpec(memory_space=pltpu.VMEM),
        scratch_shapes=[pltpu.VMEM(s, t) for s, t in zip(SHAPES, TYPES)]
        + [pltpu.VMEM(s, t) for _, s, t in SCRATCH]
        + [
            pltpu.SemaphoreType.DMA((N_IN + 1 + N_MORE,)),
            pltpu.SemaphoreType.DMA((N_RECV,)),
            pltpu.SemaphoreType.REGULAR,
        ],
        compiler_params=pltpu.CompilerParams(
            collective_id=0, has_side_effects=True, vmem_limit_bytes=60 * 2**20
        ),
    )(*flat)


def solution(mesh):
    tokens = P(("rep", "seq"))
    layer = (P(), P(None, None, "head"), P(), P(None, "head")) + (P("head"),) * 4 + (P("head", None),)
    in_specs = (tokens, P(), P()) + layer + layer
    return jax.shard_map(
        per_device,
        mesh=mesh,
        in_specs=in_specs,
        out_specs=P(("rep", "seq", "head"), None),
        check_vma=False,
    )
```
